32 devices in a mesh: group: 8 (over z, x), dom: 4 (over y, core).
Axes of the slice: x: 2, y: 2, z: 4, core: 2. Of those that a mesh axis runs over, the one named last changes fastest.
Arguments:
- features: bfloat16 [65536, 128], P(('group', 'dom')), may hold values from -6 to 6
- w_in: bfloat16 [128, 1024], replicated, may hold values from -0.5 to 0.5
- b_in: float32 [1024], replicated, may hold values from -4 to 4
- w_out: bfloat16 [1024, 128], replicated, may hold values from -0.1875 to 0.1875
- anchor_ids: int32 [131072], P(('group', 'dom')), may hold values from 0 to 8191
- local_tiles: int32 [1024, 4], P(('group', 'dom')), may hold values from 0 to 63
- requests: int32 [8, 4, 8, 8], P('group', 'dom'), may hold values from 0 to 63
- counts: int32 [8, 4, 8], P('group', 'dom'), may hold values from 0 to 8, as said below
- remote_refs: int32 [1024, 4], P(('group', 'dom')), may hold values from 0 to 63
- teacher: bfloat16 [131072, 1024], P(('group', 'dom')), may hold values from -12 to 12
Outputs:
- anchor_kl: float32 [131072], P(('group', 'dom'))
- node_grad: float32 [65536, 128], P(('group', 'dom'))
- grad_w_in: float32 [128, 1024], replicated
- grad_b_in: float32 [1024], replicated
- grad_w_out: float32 [1024, 128], replicated
The draws below stay inside these ranges and needn't reach their ends.
Inputs may be any that keep to these rules, and one draw needn't show every extreme that they name: `requests`: slots at or past the count hold tile numbers too. counts[g, d, g] is 0; in every draw some device has 8 live slots from every other group.
All inputs are finite; a program needn't handle non-finite values.
Results may differ from the reference program's by a relative error of at most 0.0067.
Values may be sent and summed in bfloat16 or wider, within the bound.
A program may use at most 192 MiB of HBM per device.

```python
import jax
import jax.numpy as jnp
from jax import lax

F = 128
HID = 1024
EMB = 128
TILE = 128
NODE_DEV = 2048
ANCH_DEV = 4096
ABLK = 128
LOC_T = 4
REM_T = 4
CAP = 8
GROUP_NODES = 8192
GROUP_TILES = 64
NODES = 65536
ANCHORS = 131072
BLOCKS = 1024
CTX = 1024
N_GROUP = 8
N_DOM = 4


def draw_counts(key, part):
    base_key = jax.random.fold_in(key, 11)
    key_list = jax.random.split(base_key, 4)
    base_counts = jax.random.randint(key_list[0], (N_GROUP, N_DOM, N_GROUP), 1, CAP // 2 + 1)
    hot_rows = jax.random.randint(key_list[1], (N_GROUP, N_DOM, 1), 0, 8) == 0
    forced_group = jax.random.randint(key_list[2], (), 0, N_GROUP)
    forced_dom = jax.random.randint(key_list[3], (), 0, N_DOM)
    group_iota = jnp.arange(N_GROUP)[:, None, None]
    dom_iota = jnp.arange(N_DOM)[None, :, None]
    source_iota = jnp.arange(N_GROUP)[None, None, :]
    forced = (group_iota == forced_group) & (dom_iota == forced_dom)
    full_rows = hot_rows | forced
    counts_all = jnp.where(full_rows, CAP, base_counts)
    return jnp.where(group_iota == source_iota, 0, counts_all).astype(jnp.int32)


def set_ends(entries, rng, low, largest):
    extent = entries.shape
    place = [jax.random.randint(jax.random.fold_in(rng, axis), (), 0, extent[axis]) for axis in range(len(extent))]
    entries = entries.at[tuple(place)].set(low)
    longest = extent.index(max(extent))
    place[longest] = (place[longest] + 1) % extent[longest]
    return entries.at[tuple(place)].set(largest)


def block_scale(key, extent, cuts, least, high):
    factor_of = 1.0
    for axis_at, blocks in cuts:
        steps = jax.random.uniform(jax.random.fold_in(jax.random.fold_in(key, 6), axis_at), (blocks,), jnp.float32, least / len(cuts), high / len(cuts))
        factor_of = factor_of * jnp.repeat(jnp.exp(steps), extent[axis_at] // blocks).reshape((-1,) + (1,) * (len(extent) - 1 - axis_at))
    return factor_of


def scatter_about(key, extent, scale, limit, cuts=(), kind=jnp.bfloat16):
    entries = jax.random.normal(key, extent, jnp.float32) * scale
    if len(cuts) > 0:
        entries = block_scale(key, extent, cuts, -0.22, 0.18) * entries
    return jnp.clip(entries, min=-limit, max=limit).astype(kind)


def setup_inputs(seed: int = 0) -> dict:
    streams_of = jax.random.split(jax.random.key(seed), 11)
    return {
        "features": scatter_about(streams_of[0], (NODES, F), 1.0, 6.0, ((0, 32),)),
        "w_in": scatter_about(streams_of[1], (F, HID), F ** -0.5, 0.5),
        "b_in": scatter_about(streams_of[2], (HID,), 1.0, 4.0, (), jnp.float32),
        "w_out": scatter_about(streams_of[3], (HID, EMB), HID ** -0.5, 0.1875),
        "anchor_ids": set_ends(jax.random.randint(streams_of[4], (ANCHORS,), 0, GROUP_NODES), jax.random.fold_in(streams_of[4], 1), 0, GROUP_NODES - 1).astype(jnp.int32),
        "local_tiles": set_ends(jax.random.randint(streams_of[5], (BLOCKS, LOC_T), 0, GROUP_TILES), jax.random.fold_in(streams_of[5], 1), 0, GROUP_TILES - 1).astype(jnp.int32),
        "requests": set_ends(jax.random.randint(streams_of[6], (N_GROUP, N_DOM, N_GROUP, CAP), 0, GROUP_TILES), jax.random.fold_in(streams_of[6], 1), 0, GROUP_TILES - 1).astype(jnp.int32),
        "counts": draw_counts(jax.random.fold_in(streams_of[10], 71), 0),
        "remote_refs": set_ends(jax.random.randint(streams_of[8], (BLOCKS, REM_T), 0, N_GROUP * CAP), jax.random.fold_in(streams_of[8], 1), 0, (N_GROUP * CAP) - 1).astype(jnp.int32),
        "teacher": scatter_about(streams_of[9], (ANCHORS, CTX), 3.0, 12.0, ((0, 32),)),
    }


SCORE_SCALE = 8.0
EPSILON = 1e-06

def node_forward(feature_rows, w_in, b_in, w_out):
    pre_act = jnp.dot(feature_rows, w_in, preferred_element_type=jnp.float32) + b_in
    hidden = jax.nn.silu(pre_act).astype(jnp.bfloat16)
    embedding = jnp.dot(hidden, w_out, preferred_element_type=jnp.float32)
    spread = jnp.sqrt(lax.optimization_barrier(jnp.mean(embedding * embedding, axis=1, keepdims=True)) + EPSILON)
    unit_rows = (embedding / spread).astype(jnp.bfloat16)
    return (pre_act, hidden, embedding, spread, unit_rows)

def reference(features, w_in, b_in, w_out, anchor_ids, local_tiles, requests, counts, remote_refs, teacher):
    devices = N_GROUP * N_DOM
    per_device = ANCH_DEV // ABLK
    feature_blocks = features.reshape(devices, NODE_DEV, F)
    unit_all = lax.map(lambda rows_in: node_forward(rows_in, w_in, b_in, w_out)[4], feature_blocks).reshape(NODES, EMB)
    tile_iota = jnp.arange(TILE, dtype=jnp.int32)
    score_scale = SCORE_SCALE / EMB

    def score_device(grad_rows, inputs):
        device_index, anchor_block, local_block, remote_block, teacher_block = inputs
        group_index = device_index // N_DOM
        dom_index = device_index % N_DOM
        group_base = group_index * GROUP_NODES
        own_requests = requests[group_index, dom_index]
        own_counts = counts[group_index, dom_index]
        source_group = remote_block // CAP
        slot_index = remote_block % CAP
        tile_numbers = own_requests[source_group, slot_index]
        remote_live = slot_index < own_counts[source_group]
        local_rows = group_base + local_block[:, :, None] * TILE + tile_iota
        remote_rows = source_group[:, :, None] * GROUP_NODES + tile_numbers[:, :, None] * TILE + tile_iota
        context_rows = jnp.concatenate([local_rows, remote_rows], axis=1).reshape(per_device, CTX)
        live_tiles = jnp.concatenate([jnp.ones((per_device, LOC_T), jnp.bool_), remote_live], axis=1)
        live_mask = jnp.repeat(live_tiles, TILE, axis=1).astype(jnp.float32)[:, None, :]
        anchor_rows = group_base + anchor_block
        anchor_vecs = unit_all[anchor_rows].astype(jnp.float32)
        context_vecs = unit_all[context_rows].astype(jnp.float32)
        scores = jnp.einsum('bae,bce->bac', anchor_vecs, context_vecs) * score_scale
        student_exp = jnp.exp(scores) * live_mask
        student_total = lax.optimization_barrier(jnp.sum(student_exp, axis=2, keepdims=True))
        teacher_f = teacher_block.astype(jnp.float32)
        target_exp = jnp.exp(teacher_f) * live_mask
        target_total = lax.optimization_barrier(jnp.sum(target_exp, axis=2, keepdims=True))
        target_prob = target_exp / target_total
        divergence = lax.optimization_barrier(jnp.sum(target_prob * (teacher_f - scores), axis=2)) - jnp.log(target_total[:, :, 0]) + jnp.log(student_total[:, :, 0])
        prob_delta = (student_exp / student_total - target_prob).astype(jnp.bfloat16).astype(jnp.float32)
        anchor_grad = jnp.einsum('bac,bce->bae', prob_delta, context_vecs) * score_scale
        context_grad = jnp.einsum('bac,bae->bce', prob_delta, anchor_vecs) * score_scale
        grad_rows = grad_rows.at[anchor_rows.reshape(-1)].add(anchor_grad.reshape(-1, EMB))
        grad_rows = grad_rows.at[context_rows.reshape(-1)].add(context_grad.reshape(-1, EMB))
        return (grad_rows, divergence)
    score_inputs = (jnp.arange(devices, dtype=jnp.int32), anchor_ids.reshape(devices, per_device, ABLK), local_tiles.reshape(devices, per_device, LOC_T), remote_refs.reshape(devices, per_device, REM_T), teacher.reshape(devices, per_device, ABLK, CTX))
    node_grad, divergence = lax.scan(score_device, jnp.zeros((NODES, EMB), jnp.float32), score_inputs)
    anchor_kl = divergence.reshape(ANCHORS)

    def backward_device(totals, inputs):
        feature_rows, unit_grad = inputs
        pre_act, hidden, embedding, spread, unit_rows = node_forward(feature_rows, w_in, b_in, w_out)
        normed = embedding / spread
        embed_grad = ((unit_grad - normed * lax.optimization_barrier(jnp.mean(unit_grad * normed, axis=1, keepdims=True))) / spread).astype(jnp.bfloat16)
        out_grad = jnp.dot(hidden.T, embed_grad, preferred_element_type=jnp.float32)
        hidden_grad = jnp.dot(embed_grad, w_out.T, preferred_element_type=jnp.float32)
        sigmoid_pre = jax.nn.sigmoid(pre_act)
        pre_grad = hidden_grad * sigmoid_pre * (1.0 + pre_act * (1.0 - sigmoid_pre))
        bias_grad = lax.optimization_barrier(jnp.sum(pre_grad, axis=0))
        in_grad = jnp.dot(feature_rows.T, pre_grad.astype(jnp.bfloat16), preferred_element_type=jnp.float32)
        return ((totals[0] + in_grad, totals[1] + bias_grad, totals[2] + out_grad), None)
    start_totals = (jnp.zeros((F, HID), jnp.float32), jnp.zeros((HID,), jnp.float32), jnp.zeros((HID, EMB), jnp.float32))
    totals, unused = lax.scan(backward_device, start_totals, (feature_blocks, node_grad.reshape(devices, NODE_DEV, EMB)))
    inverse = 1.0 / devices
    return (anchor_kl, node_grad, totals[0] * inverse, totals[1] * inverse, totals[2] * inverse)
```

```python
import functools
import math

import jax
import jax.numpy as jnp
from jax import lax
from jax.experimental import pallas as pl
from jax.experimental.pallas import tpu as pltpu
from jax.sharding import PartitionSpec as P

TILE = 128
ABLK = 128

SCORE_SCALE = 8.0
EPSILON = 1e-06
VMEM_LIMIT = 60 * 1024 * 1024
CHUNK = 256

ONE_COPY = pl.Buffered(1)


def whole(shape):
    return pl.BlockSpec(shape, lambda *_: (0,) * len(shape), pipeline_mode=ONE_COPY)


def node_rows(feature_rows, w_in, b_in, w_out):
    pre_act = jnp.dot(feature_rows, w_in, preferred_element_type=jnp.float32) + b_in
    hidden = (pre_act * jax.nn.sigmoid(pre_act)).astype(jnp.bfloat16)
    embedding = jnp.dot(hidden, w_out, preferred_element_type=jnp.float32)
    spread = jnp.sqrt(jnp.mean(embedding * embedding, axis=1, keepdims=True) + EPSILON)
    return embedding, (embedding / spread).astype(jnp.bfloat16)


def rows_of(index, count=TILE):
    return pl.ds(pl.multiple_of(index * count, count), count)


def cost(flops, moved, powers):
    return pl.CostEstimate(flops=flops, bytes_accessed=moved, transcendentals=powers)


def clear_rows(ref):
    zero_chunk = jnp.zeros((CHUNK, ref.shape[1]), ref.dtype)

    def clear(index, carry):
        ref[rows_of(index, CHUNK), :] = zero_chunk
        return carry

    lax.fori_loop(0, ref.shape[0] // CHUNK, clear, 0)


def as_row(column):
    return jnp.broadcast_to(column, (ABLK, TILE)).T[0:1, :]


def as_column(row):
    return jnp.broadcast_to(row, (TILE, ABLK)).T[:, 0:1]


def tile_scores(anchors, context):
    return lax.dot_general(
        anchors, context, (((1,), (1,)), ((), ())), preferred_element_type=jnp.float32
    )


def prepare_kernel(
    per_step, local_count, remote_count, slot_count, ids_ref, tiles_ref, refs_ref, counts_ref,
    table_ref, teacher_ref, anchors_ref, near_ref, far_ref, base_ref, partial_ref,
    table_f, anchor_rows,
):
    scale = SCORE_SCALE / table_ref.shape[1]

    @pl.when(pl.program_id(0) == 0)
    def _():
        def widen(index, carry):
            here = rows_of(index, CHUNK)
            table_f[here, :] = table_ref[here, :].astype(jnp.float32)
            return carry

        lax.fori_loop(0, table_f.shape[0] // CHUNK, widen, 0)

    for sub in range(per_step):
        block = pl.program_id(0) * per_step + sub
        rows = slice(sub * ABLK, (sub + 1) * ABLK)
        for row in range(ABLK):
            at = sub * ABLK + row
            index = ids_ref[block * ABLK + row]
            anchor_rows[at : at + 1, :] = table_f[pl.ds(index, 1), :]
        anchors = (anchor_rows[rows, :] * scale).astype(jnp.bfloat16)
        anchors_ref[rows, :] = anchors
        target_sum = gap_sum = student_sum = None
        exps = []
        for i in range(local_count + remote_count):
            teacher = teacher_ref[rows, i * TILE : (i + 1) * TILE].astype(jnp.float32)
            target_exp = jnp.exp(teacher)
            if i >= local_count:
                ref = refs_ref[block * remote_count + i - local_count]
                live = lax.rem(ref, slot_count) < counts_ref[lax.div(ref, slot_count)]
                target_exp = target_exp * jnp.where(live, 1.0, 0.0).astype(jnp.float32)
                gap = target_exp * teacher
            else:
                place = rows_of(tiles_ref[block * local_count + i])
                scores = tile_scores(anchors, table_ref[place, :])
                gap = target_exp * (teacher - scores)
                student_exp = jnp.exp(scores)
                student_sum = student_exp if i == 0 else student_sum + student_exp
            target_sum = target_exp if i == 0 else target_sum + target_exp
            gap_sum = gap if i == 0 else gap_sum + gap
            exps.append(target_exp)
        total = jnp.sum(target_sum, axis=1, keepdims=True)
        inverse = 1.0 / total
        base = jnp.sum(gap_sum, axis=1, keepdims=True) * inverse - jnp.log(total)
        base_ref[sub] = as_row(base)
        partial_ref[sub] = as_row(jnp.sum(student_sum, axis=1, keepdims=True))
        for i, target_exp in enumerate(exps):
            out_ref, at = (near_ref, i) if i < local_count else (far_ref, i - local_count)
            out_ref[rows, at * TILE : (at + 1) * TILE] = (target_exp * inverse).astype(
                jnp.bfloat16
            )


def prepare(per_step, anchor_ids, local_tiles, remote_refs, own_counts, table, teacher, slots):
    blocks, remote_count = remote_refs.shape
    local_count = local_tiles.shape[1]
    near, far = local_count * TILE, remote_count * TILE
    anchors, context_width = teacher.shape
    width = table.shape[1]
    rows = per_step * ABLK
    return pl.pallas_call(
        functools.partial(prepare_kernel, per_step, local_count, remote_count, slots),
        out_shape=(
            jax.ShapeDtypeStruct((anchors, width), jnp.bfloat16),
            jax.ShapeDtypeStruct((anchors, near), jnp.bfloat16),
            jax.ShapeDtypeStruct((anchors, far), jnp.bfloat16),
            jax.ShapeDtypeStruct((blocks, 1, ABLK), jnp.float32),
            jax.ShapeDtypeStruct((blocks, 1, ABLK), jnp.float32),
        ),
        grid_spec=pltpu.PrefetchScalarGridSpec(
            num_scalar_prefetch=4,
            grid=(blocks // per_step,),
            in_specs=[
                whole(table.shape),
                pl.BlockSpec((rows, context_width), lambda b, *_: (b, 0)),
            ],
            out_specs=(
                pl.BlockSpec((rows, width), lambda b, *_: (b, 0)),
                pl.BlockSpec((rows, near), lambda b, *_: (b, 0)),
                pl.BlockSpec((rows, far), lambda b, *_: (b, 0)),
                pl.BlockSpec((per_step, 1, ABLK), lambda b, *_: (b, 0, 0)),
                pl.BlockSpec((per_step, 1, ABLK), lambda b, *_: (b, 0, 0)),
            ),
            scratch_shapes=[
                pltpu.VMEM(table.shape, jnp.float32),
                pltpu.VMEM((rows, width), jnp.float32),
            ],
        ),
        compiler_params=pltpu.CompilerParams(vmem_limit_bytes=VMEM_LIMIT),
        cost_estimate=cost(
            10 * anchors * context_width, 4 * anchors * context_width, anchors * context_width
        ),
    )(
        anchor_ids, local_tiles.reshape(-1), remote_refs.reshape(-1), own_counts, table, teacher
    )


def take_context(block, sub, context, tiles_ref, refs_ref, table_ref, fetched_ref, counts):
    local_count, remote_count = counts
    places = []
    for i in range(local_count):
        place = rows_of(tiles_ref[block * local_count + i])
        context[sub, i * TILE : (i + 1) * TILE, :] = table_ref[place, :]
        places.append(place)
    for i in range(remote_count):
        place = rows_of(refs_ref[block * remote_count + i])
        at = local_count + i
        context[sub, at * TILE : (at + 1) * TILE, :] = fetched_ref[place, :]
        places.append(place)
    return places


def tile_grad(delta, anchors):
    return lax.dot_general(
        delta, anchors, (((0,), (0,)), ((), ())), preferred_element_type=jnp.float32
    )


def score_kernel(
    per_step, remote_count, slot_count, refs_ref, counts_ref,
    fetched_ref, anchors_ref, far_ref, base_ref, partial_ref,
    kl_ref, inverse_ref, delta_ref, remote_grad_ref, remote_acc,
):
    @pl.when(pl.program_id(0) == 0)
    def _():
        clear_rows(remote_acc)

    for sub in range(per_step):
        block = pl.program_id(0) * per_step + sub
        rows = slice(sub * ABLK, (sub + 1) * ABLK)
        anchors = anchors_ref[rows, :]
        places = []
        student = []
        student_sum = gap_sum = None
        for i in range(remote_count):
            span = slice(i * TILE, (i + 1) * TILE)
            ref = refs_ref[block * remote_count + i]
            places.append(rows_of(ref))
            live = lax.rem(ref, slot_count) < counts_ref[lax.div(ref, slot_count)]
            scores = tile_scores(anchors, fetched_ref[places[i], :])
            student_exp = jnp.exp(scores) * jnp.where(live, 1.0, 0.0).astype(jnp.float32)
            gap = far_ref[rows, span].astype(jnp.float32) * scores
            student_sum = student_exp if i == 0 else student_sum + student_exp
            gap_sum = gap if i == 0 else gap_sum + gap
            student.append(student_exp)
        total = as_column(partial_ref[sub]) + jnp.sum(student_sum, axis=1, keepdims=True)
        inverse = 1.0 / total
        rest = jnp.log(total) - jnp.sum(gap_sum, axis=1, keepdims=True)
        kl_ref[sub] = base_ref[sub] + as_row(rest)
        inverse_ref[sub] = as_row(inverse)
        for i in range(remote_count):
            span = slice(i * TILE, (i + 1) * TILE)
            delta = (student[i] * inverse - far_ref[rows, span].astype(jnp.float32)).astype(
                jnp.bfloat16
            )
            delta_ref[rows, span] = delta
            remote_acc[places[i], :] += tile_grad(delta, anchors)

    @pl.when(pl.program_id(0) == pl.num_programs(0) - 1)
    def _():
        def finish(index, carry):
            here = rows_of(index, CHUNK)
            remote_grad_ref[here, :] = remote_acc[here, :].astype(jnp.bfloat16)
            return carry

        lax.fori_loop(0, remote_acc.shape[0] // CHUNK, finish, 0)


def score(per_step, remote_refs, own_counts, fetched, prepared, slots):
    anchors, near, far, base, partial = prepared
    blocks, remote_count = remote_refs.shape
    width = anchors.shape[1]
    rows = per_step * ABLK
    pairs = far.shape[0] * far.shape[1]
    row_spec = pl.BlockSpec((per_step, 1, ABLK), lambda b, *_: (b, 0, 0))
    far_spec = pl.BlockSpec((rows, far.shape[1]), lambda b, *_: (b, 0))
    return pl.pallas_call(
        functools.partial(score_kernel, per_step, remote_count, slots),
        out_shape=(
            jax.ShapeDtypeStruct((blocks, 1, ABLK), jnp.float32),
            jax.ShapeDtypeStruct((blocks, 1, ABLK), jnp.float32),
            jax.ShapeDtypeStruct(far.shape, jnp.bfloat16),
            jax.ShapeDtypeStruct(fetched.shape, jnp.bfloat16),
        ),
        grid_spec=pltpu.PrefetchScalarGridSpec(
            num_scalar_prefetch=2,
            grid=(blocks // per_step,),
            in_specs=[
                whole(fetched.shape),
                pl.BlockSpec((rows, width), lambda b, *_: (b, 0)),
                far_spec,
                row_spec,
                row_spec,
            ],
            out_specs=(row_spec, row_spec, far_spec, whole(fetched.shape)),
            scratch_shapes=[pltpu.VMEM(fetched.shape, jnp.float32)],
        ),
        compiler_params=pltpu.CompilerParams(vmem_limit_bytes=VMEM_LIMIT),
        cost_estimate=cost(3 * pairs * width, 4 * pairs, pairs),
    )(remote_refs.reshape(-1), own_counts, fetched, anchors, far, base, partial)


def local_kernel(
    per_step, local_count, remote_count, lanes, ids_ref, tiles_ref, refs_ref,
    table_ref, fetched_ref, anchors_ref, near_ref, inverse_ref, delta_ref, local_grad_ref,
    context, near_delta, anchor_grad, *row_accs,
):
    scale = SCORE_SCALE / table_ref.shape[1]

    @pl.when(pl.program_id(0) == 0)
    def _():
        clear_rows(local_grad_ref)
        for acc in row_accs:
            clear_rows(acc)

    for sub in range(per_step):
        block = pl.program_id(0) * per_step + sub
        rows = slice(sub * ABLK, (sub + 1) * ABLK)
        places = take_context(
            block, sub, context, tiles_ref, refs_ref, table_ref, fetched_ref,
            (local_count, remote_count),
        )
        anchors = anchors_ref[rows, :]
        inverse = as_column(inverse_ref[sub])
        near = local_count * TILE
        for i in range(local_count):
            span = slice(i * TILE, (i + 1) * TILE)
            student = jnp.exp(tile_scores(anchors, context[sub, span, :])) * inverse
            delta = (student - near_ref[rows, span].astype(jnp.float32)).astype(jnp.bfloat16)
            near_delta[rows, span] = delta
            local_grad_ref[places[i], :] += tile_grad(delta, anchors)
        near_part = jnp.dot(
            near_delta[rows, :], context[sub, :near, :], preferred_element_type=jnp.float32
        )
        far_part = jnp.dot(
            delta_ref[rows, :], context[sub, near:, :], preferred_element_type=jnp.float32
        )
        anchor_grad[rows, :] = (near_part + far_part) * scale
        for row in range(ABLK):
            acc = row_accs[row % lanes]
            at = sub * ABLK + row
            acc[pl.ds(ids_ref[block * ABLK + row], 1), :] += anchor_grad[at : at + 1, :]

    @pl.when(pl.program_id(0) == pl.num_programs(0) - 1)
    def _():
        def finish(index, carry):
            here = rows_of(index, CHUNK)
            total = local_grad_ref[here, :]
            for acc in row_accs:
                total = total + acc[here, :]
            local_grad_ref[here, :] = total
            return carry

        lax.fori_loop(0, local_grad_ref.shape[0] // CHUNK, finish, 0)


def local_grads(
    per_step, anchor_ids, local_tiles, remote_refs, table, fetched, anchors, near, inverse, delta
):
    blocks, local_count = local_tiles.shape
    remote_count = remote_refs.shape[1]
    context_width = near.shape[1] + delta.shape[1]
    width = table.shape[1]
    rows = per_step * ABLK
    lanes = 4 if table.shape[0] <= 8192 else 1
    pairs = delta.shape[0] * context_width
    return pl.pallas_call(
        functools.partial(local_kernel, per_step, local_count, remote_count, lanes),
        out_shape=jax.ShapeDtypeStruct(table.shape, jnp.float32),
        grid_spec=pltpu.PrefetchScalarGridSpec(
            num_scalar_prefetch=3,
            grid=(blocks // per_step,),
            in_specs=[
                whole(table.shape),
                whole(fetched.shape),
                pl.BlockSpec((rows, width), lambda b, *_: (b, 0)),
                pl.BlockSpec((rows, near.shape[1]), lambda b, *_: (b, 0)),
                pl.BlockSpec((per_step, 1, ABLK), lambda b, *_: (b, 0, 0)),
                pl.BlockSpec((rows, delta.shape[1]), lambda b, *_: (b, 0)),
            ],
            out_specs=whole(table.shape),
            scratch_shapes=[
                pltpu.VMEM((per_step, context_width, width), jnp.bfloat16),
                pltpu.VMEM((rows, near.shape[1]), jnp.bfloat16),
                pltpu.VMEM((rows, width), jnp.float32),
            ]
            + [pltpu.VMEM(table.shape, jnp.float32)] * lanes,
        ),
        compiler_params=pltpu.CompilerParams(vmem_limit_bytes=VMEM_LIMIT),
        cost_estimate=cost(3 * pairs * width, 2 * pairs, 0),
    )(
        anchor_ids, local_tiles.reshape(-1), remote_refs.reshape(-1),
        table, fetched, anchors, near, inverse, delta,
    )


def merge_kernel(asked_ref, local_ref, returned_ref, out_ref, acc):
    def load(index, carry):
        here = rows_of(index, CHUNK)
        acc[here, :] = local_ref[here, :]
        return carry

    lax.fori_loop(0, acc.shape[0] // CHUNK, load, 0)

    def add(slot, carry):
        acc[rows_of(asked_ref[slot]), :] += returned_ref[rows_of(slot), :].astype(jnp.float32)
        return carry

    lax.fori_loop(0, returned_ref.shape[0] // TILE, add, 0)

    def store(index, carry):
        here = rows_of(index, CHUNK)
        out_ref[here, :] = acc[here, :].astype(jnp.bfloat16)
        return carry

    lax.fori_loop(0, acc.shape[0] // CHUNK, store, 0)


def merge(asked, local_grad, returned):
    return pl.pallas_call(
        merge_kernel,
        out_shape=jax.ShapeDtypeStruct(local_grad.shape, jnp.bfloat16),
        grid_spec=pltpu.PrefetchScalarGridSpec(
            num_scalar_prefetch=1,
            grid=(1,),
            in_specs=[whole(local_grad.shape), whole(returned.shape)],
            out_specs=whole(local_grad.shape),
            scratch_shapes=[pltpu.VMEM(local_grad.shape, jnp.float32)],
        ),
        compiler_params=pltpu.CompilerParams(vmem_limit_bytes=VMEM_LIMIT),
    )(asked, local_grad, returned)


MESH = pl.DeviceIdType.MESH
ANYWHERE = pl.BlockSpec(memory_space=pl.ANY)
IN_VMEM = pl.BlockSpec(memory_space=pltpu.VMEM)


def greet(partners):
    barrier = pltpu.get_barrier_semaphore()
    for partner in partners:
        pl.semaphore_signal(barrier, inc=1, device_id=partner, device_id_type=MESH)
    pl.semaphore_wait(barrier, len(partners))


def push(src, dst, sems, index, partner):
    copy = pltpu.make_async_remote_copy(
        src_ref=src,
        dst_ref=dst,
        send_sem=sems[0].at[index],
        recv_sem=sems[1].at[index],
        device_id=partner,
        device_id_type=MESH,
    )
    copy.start()
    return copy


def dom_partners(doms):
    group, dom = lax.axis_index("group"), lax.axis_index("dom")
    chips = doms // 2
    chip, core = dom // 2, dom % 2
    other = chip * 2 + (1 - core)
    ahead = [lax.rem(chip + k, chips) * 2 + core for k in range(1, chips)]
    behind = [lax.rem(chip + chips - k, chips) for k in range(1, chips)]
    return group, dom, core, other, ahead, behind


def fetch_kernel(
    groups, doms, chunks, features_ref, w_in_ref, b_in_ref, w_out_ref, requests_ref, own_asks,
    table_ref, fetched_ref, embedding_ref,
    table, relay, served, blank, ask_out, ask_in, asked,
    near_sems, far_sems, on_sems, swap_sems, relay_near, relay_far, relay_on,
    ask_sems, serve_sems, relay_serve, own_sems,
):
    group, dom, core, other, ahead, behind = dom_partners(doms)
    half = groups // 2
    slots = requests_ref.shape[1]
    count = features_ref.shape[0]
    part = count // chunks
    step = min(CHUNK, part)
    first = group // half * half
    place = lax.rem(group, half)
    mates = [first + lax.rem(place + k, half) for k in range(1, half)]
    partner = lax.rem(group + half, groups)
    greet(
        [(group, other)] + [(group, far) for far in ahead]
        + [(mate, dom) for mate in mates] + [(partner, dom)]
    )

    tiles = part // TILE

    def span(owner, chunk):
        return pl.ds(owner * (count // TILE) + chunk * tiles, tiles)

    def both(sems, *index):
        return sems[0].at[index], sems[1].at[index]

    def send(src, dst, sems, partner_at):
        copy = pltpu.make_async_remote_copy(
            src_ref=src, dst_ref=dst, send_sem=sems[0], recv_sem=sems[1],
            device_id=partner_at, device_id_type=MESH,
        )
        copy.start()
        return copy

    def spread_chunk(here, owner, chunk, near, far):
        rows = here.at[span(owner, chunk)]
        far_copies = [
            send(rows, rows, both(far, k, chunk), (group, there)) for k, there in enumerate(ahead)
        ]
        return far_copies, send(rows, rows, both(near, chunk), (group, other))

    def pass_on(here, far_copies, chunk, on):
        copies = []
        for k, copy in enumerate(far_copies):
            copy.wait_recv()
            rows = here.at[span(behind[k] * 2 + core, chunk)]
            copies.append(send(rows, rows, both(on, k, chunk), (group, other)))
        return copies

    ask_out[...] = jnp.zeros_like(ask_out)
    ask_out[:, 0:slots] = requests_ref[...]
    asks = [
        send(ask_out, ask_in.at[place], both(ask_sems, k), (mate, dom))
        for k, mate in enumerate(mates)
    ]
    blank[...] = jnp.zeros_like(blank)
    sent = []
    far_copies, near_copies, swaps = [], [], []
    for chunk in range(chunks):
        def forward(index, carry):
            at = pl.ds(pl.multiple_of(chunk * part + index * step, step), step)
            embedding, unit_rows = node_rows(
                features_ref[at, :], w_in_ref[...], b_in_ref[...], w_out_ref[...]
            )
            embedding_ref[at, :] = embedding
            to = pl.ds((dom * count + chunk * part) // TILE + index * (step // TILE), step // TILE)
            table[to] = unit_rows.reshape(step // TILE, TILE, unit_rows.shape[1])
            return carry

        lax.fori_loop(0, part // step, forward, 0)
        rows = span(dom, chunk)
        swaps.append(
            send(table.at[rows], relay.at[rows], both(swap_sems, chunk), (partner, dom))
        )
        far, near = spread_chunk(table, dom, chunk, near_sems, far_sems)
        far_copies.append(far)
        near_copies.append(near)
    clear = pltpu.make_async_copy(blank, fetched_ref.at[pl.ds(group * slots, slots)], own_sems.at[0])
    clear.start()
    on_copies, relay_fars, relay_nears, relay_ons = [], [], [], []

    def relay_chunk(chunk):
        swaps[chunk].wait_recv()
        far, near = spread_chunk(relay, dom, chunk, relay_near, relay_far)
        relay_fars.append(far)
        relay_nears.append(near)

    for chunk in range(chunks):
        on_copies += pass_on(table, far_copies[chunk], chunk, on_sems)
        if chunk % 2 == 1:
            relay_chunk(chunk // 2)
    for copy in asks:
        copy.wait_recv()
    read_asks = pltpu.make_async_copy(ask_in, asked, own_sems.at[1])
    read_asks.start()
    for copy in on_copies + near_copies:
        copy.wait_recv()
    keep = pltpu.make_async_copy(table, table_ref, own_sems.at[2])
    keep.start()
    read_asks.wait()

    def serve(here, base, asked_of):
        for k in range(half - 1):
            source = lax.rem(place + k + 1, half)

            def pick(slot, carry):
                wanted = asked[source, asked_of, slot]
                served[base + k, slot] = here[wanted]
                return carry

            lax.fori_loop(0, slots, pick, 0)

    def push_served(base, asked_of, sems):
        return [
            send(
                served.at[base + k], fetched_ref.at[pl.ds(asked_of * slots, slots)], both(sems, k),
                (mate, dom),
            )
            for k, mate in enumerate(mates)
        ]

    serve(table, 0, group)
    sent += push_served(0, group, serve_sems)
    done = len(relay_fars)
    for chunk in range(done, chunks):
        relay_chunk(chunk)
    for chunk in range(chunks):
        relay_ons += pass_on(relay, relay_fars[chunk], chunk, relay_on)
    for copy in relay_ons + relay_nears:
        copy.wait_recv()
    serve(relay, half - 1, partner)
    sent += push_served(half - 1, partner, relay_serve)

    def pick_own(slot, carry):
        wanted = own_asks[partner, slot]
        served[2 * half - 2, slot] = relay[wanted]
        return carry

    lax.fori_loop(0, slots, pick_own, 0)
    mine = pltpu.make_async_copy(
        served.at[2 * half - 2], fetched_ref.at[pl.ds(partner * slots, slots)], own_sems.at[3]
    )
    mine.start()
    for copy in sent:
        copy.wait_recv()
    clear.wait()
    keep.wait()
    mine.wait()
    for copy in asks + swaps + near_copies + on_copies + relay_nears + relay_ons + sent:
        copy.wait_send()
    for copies in far_copies + relay_fars:
        for copy in copies:
            copy.wait_send()


def fetch_tiles(features, w_in, b_in, w_out, own_requests, groups, doms):
    slots = own_requests.shape[1]
    count = features.shape[0]
    width = w_out.shape[1]
    chunks = 4
    half = groups // 2
    far, mates = max(doms // 2 - 1, 1), max(half - 1, 1)
    dma = pltpu.SemaphoreType.DMA
    nodes = doms * count
    table, fetched, embedding = pl.pallas_call(
        functools.partial(fetch_kernel, groups, doms, chunks),
        out_shape=(
            jax.ShapeDtypeStruct((nodes // TILE, TILE, width), jnp.bfloat16),
            jax.ShapeDtypeStruct((groups * slots, TILE, width), jnp.bfloat16),
            jax.ShapeDtypeStruct((count, width), jnp.float32),
        ),
        in_specs=[IN_VMEM] * 5 + [pl.BlockSpec(memory_space=pltpu.SMEM)],
        out_specs=(ANYWHERE, ANYWHERE, IN_VMEM),
        scratch_shapes=[
            pltpu.VMEM((nodes // TILE, TILE, width), jnp.bfloat16),
            pltpu.VMEM((nodes // TILE, TILE, width), jnp.bfloat16),
            pltpu.VMEM((2 * half - 1, slots, TILE, width), jnp.bfloat16),
            pltpu.VMEM((slots, TILE, width), jnp.bfloat16),
            pltpu.VMEM((groups, 128), jnp.int32),
            pltpu.VMEM((half, groups, 128), jnp.int32),
            pltpu.SMEM((half, groups, 128), jnp.int32),
            [dma((chunks,)), dma((chunks,))],
            [dma((far, chunks)), dma((far, chunks))],
            [dma((far, chunks)), dma((far, chunks))],
            [dma((chunks,)), dma((chunks,))],
            [dma((chunks,)), dma((chunks,))],
            [dma((far, chunks)), dma((far, chunks))],
            [dma((far, chunks)), dma((far, chunks))],
            [dma((mates,)), dma((mates,))],
            [dma((mates,)), dma((mates,))],
            [dma((mates,)), dma((mates,))],
            dma((4,)),
        ],
        compiler_params=pltpu.CompilerParams(
            collective_id=0, has_side_effects=True, vmem_limit_bytes=VMEM_LIMIT
        ),
    )(features, w_in, b_in.reshape(1, -1), w_out, own_requests, own_requests)
    return table.reshape(-1, width), fetched.reshape(-1, width), embedding


def scatter_kernel(
    doms, merged_ref, out_ref, mine, kept, near_got, far_out, far_got,
    own_sem, near_send, near_recv, far_send, far_recv,
):
    group, dom, core, other, ahead, behind = dom_partners(doms)
    count = out_ref.shape[0]
    chips = doms // 2
    greet([(group, other)] + [(group, far) for far in ahead])
    order = [dom // 2] + [lax.rem(dom // 2 + k, chips) for k in range(1, chips)]
    order = order[1:] + order[:1]
    near_copies = []
    own_copies = []
    for k, chip in enumerate(order):
        theirs = merged_ref.at[rows_of(chip * 2 + (1 - core), count), :]
        near_copies.append(push(theirs, near_got.at[k], (near_send, near_recv), k, (group, other)))
        ours = merged_ref.at[rows_of(chip * 2 + core, count), :]
        copy = pltpu.make_async_copy(ours, mine.at[k], own_sem.at[k])
        copy.start()
        own_copies.append(copy)
    far_copies = []
    for k in range(chips - 1):
        near_copies[k].wait_recv()
        own_copies[k].wait()
        total = mine[k].astype(jnp.float32) + near_got[k].astype(jnp.float32)
        far_out[k] = total.astype(jnp.bfloat16)
        far_copies.append(
            push(far_out.at[k], far_got.at[k], (far_send, far_recv), k, (group, ahead[k]))
        )
    near_copies[chips - 1].wait_recv()
    own_copies[chips - 1].wait()
    kept[...] = mine[chips - 1].astype(jnp.float32) + near_got[chips - 1].astype(jnp.float32)
    for k, copy in enumerate(far_copies):
        copy.wait_recv()
        kept[...] += far_got[k].astype(jnp.float32)
    out_ref[...] = kept[...]
    for copy in near_copies + far_copies:
        copy.wait_send()


def scatter_sums(merged, doms):
    count, width = merged.shape[0] // doms, merged.shape[1]
    chips = doms // 2
    far = max(chips - 1, 1)
    dma = pltpu.SemaphoreType.DMA
    return pl.pallas_call(
        functools.partial(scatter_kernel, doms),
        out_shape=jax.ShapeDtypeStruct((count, width), jnp.float32),
        in_specs=[ANYWHERE],
        out_specs=IN_VMEM,
        scratch_shapes=[
            pltpu.VMEM((chips, count, width), jnp.bfloat16),
            pltpu.VMEM((count, width), jnp.float32),
            pltpu.VMEM((chips, count, width), jnp.bfloat16),
            pltpu.VMEM((far, count, width), jnp.bfloat16),
            pltpu.VMEM((far, count, width), jnp.bfloat16),
            dma((chips,)), dma((chips,)), dma((chips,)), dma((far,)), dma((far,)),
        ],
        compiler_params=pltpu.CompilerParams(
            collective_id=1, has_side_effects=True, vmem_limit_bytes=VMEM_LIMIT
        ),
    )(merged)


def totals_kernel(
    groups, doms, x_ref, out_ref, out1, got1, part, out2, got2, gather1, gather2,
    send1, recv1, send2, recv2, send3, recv3, send4, recv4,
):
    group, dom = lax.axis_index("group"), lax.axis_index("dom")
    wide = x_ref.shape[0] // doms
    thin = wide // groups
    dom_peers = [lax.rem(dom + k, doms) for k in range(1, doms)]
    group_peers = [lax.rem(group + k, groups) for k in range(1, groups)]
    greet([(group, peer) for peer in dom_peers] + [(peer, dom) for peer in group_peers])
    copies = []
    first = []
    for k, peer in enumerate(dom_peers):
        out1[k] = x_ref[rows_of(peer, wide), :].astype(jnp.bfloat16)
        first.append(push(out1.at[k], got1.at[k], (send1, recv1), k, (group, peer)))
    part[...] = x_ref[rows_of(dom, wide), :]
    for k, copy in enumerate(first):
        copy.wait_recv()
        part[...] += got1[k].astype(jnp.float32)
    copies += first
    second = []
    for k, peer in enumerate(group_peers):
        out2[k] = part[rows_of(peer, thin), :].astype(jnp.bfloat16)
        second.append(push(out2.at[k], got2.at[k], (send2, recv2), k, (peer, dom)))
    total = part[rows_of(group, thin), :]
    for k, copy in enumerate(second):
        copy.wait_recv()
        total = total + got2[k].astype(jnp.float32)
    copies += second
    gather1[group] = (total * (1.0 / (groups * doms))).astype(jnp.bfloat16)
    mine = gather1.at[group]
    third = [
        push(mine, mine, (send3, recv3), k, (peer, dom)) for k, peer in enumerate(group_peers)
    ]
    for copy in third:
        copy.wait_recv()
    copies += third
    fourth = [
        push(gather1, gather2.at[dom], (send4, recv4), k, (group, peer))
        for k, peer in enumerate(dom_peers)
    ]
    out_ref[dom] = gather1[...].astype(jnp.float32)
    for k, copy in enumerate(fourth):
        copy.wait_recv()
        source = lax.rem(dom + doms - (k + 1), doms)
        out_ref[source] = gather2[source].astype(jnp.float32)
    copies += fourth
    for copy in copies:
        copy.wait_send()


def mean_over_devices(x, groups, doms):
    rows, width = x.shape
    wide = rows // doms
    thin = wide // groups
    a, b = max(doms - 1, 1), max(groups - 1, 1)
    half = jnp.bfloat16
    dma = pltpu.SemaphoreType.DMA
    out = pl.pallas_call(
        functools.partial(totals_kernel, groups, doms),
        out_shape=jax.ShapeDtypeStruct((doms, groups, thin, width), jnp.float32),
        in_specs=[IN_VMEM],
        out_specs=IN_VMEM,
        scratch_shapes=[
            pltpu.VMEM((a, wide, width), half),
            pltpu.VMEM((a, wide, width), half),
            pltpu.VMEM((wide, width), jnp.float32),
            pltpu.VMEM((b, thin, width), half),
            pltpu.VMEM((b, thin, width), half),
            pltpu.VMEM((groups, thin, width), half),
            pltpu.VMEM((doms, groups, thin, width), half),
            dma((a,)), dma((a,)), dma((b,)), dma((b,)), dma((b,)), dma((b,)), dma((a,)), dma((a,)),
        ],
        compiler_params=pltpu.CompilerParams(
            collective_id=2, has_side_effects=True, vmem_limit_bytes=VMEM_LIMIT
        ),
    )(x)
    return out.reshape(rows, width)


def shards(
    features, w_in, b_in, w_out, anchor_ids, local_tiles, requests, counts, remote_refs, teacher
):
    groups = lax.axis_size("group")
    doms = lax.axis_size("dom")
    devices = groups * doms
    own_requests = requests[0, 0]
    own_counts = counts[0, 0]
    slot_count = own_requests.shape[1]
    table, fetched, embedding = fetch_tiles(
        features, w_in, b_in, w_out, own_requests, groups, doms
    )
    per_step = math.gcd(local_tiles.shape[0], 2)
    prepared = prepare(
        per_step, anchor_ids, local_tiles, remote_refs, own_counts, table, teacher, slot_count
    )
    anchor_kl, inverse, delta, remote_grad = score(
        per_step, remote_refs, own_counts, fetched, prepared, slot_count
    )
    anchor_kl = anchor_kl.reshape(-1)
    returned = lax.all_to_all(remote_grad, "group", split_axis=0, concat_axis=0, tiled=True)
    local_grad = local_grads(
        per_step, anchor_ids, local_tiles, remote_refs, table, fetched, prepared[0], prepared[1],
        inverse, delta,
    )
    asked = lax.all_to_all(own_requests, "group", split_axis=0, concat_axis=0, tiled=True)
    merged = merge(asked.reshape(-1), local_grad, returned)
    node_grad = scatter_sums(merged, doms)
    pre_act = jnp.dot(features, w_in, preferred_element_type=jnp.float32) + b_in
    hidden = jax.nn.silu(pre_act).astype(jnp.bfloat16)
    spread = jnp.sqrt(jnp.mean(embedding * embedding, axis=1, keepdims=True) + EPSILON)
    normed = embedding / spread
    embed_grad = (
        (node_grad - normed * jnp.mean(node_grad * normed, axis=1, keepdims=True)) / spread
    ).astype(jnp.bfloat16)
    out_grad = jnp.dot(hidden.T, embed_grad, preferred_element_type=jnp.float32)
    hidden_grad = jnp.dot(embed_grad, w_out.T, preferred_element_type=jnp.float32)
    sigmoid_pre = jax.nn.sigmoid(pre_act)
    pre_grad = hidden_grad * sigmoid_pre * (1.0 + pre_act * (1.0 - sigmoid_pre))
    bias_grad = jnp.sum(pre_grad, axis=0)
    in_grad_t = jnp.dot(
        pre_grad.astype(jnp.bfloat16).T, features, preferred_element_type=jnp.float32
    )
    hid = in_grad_t.shape[0]
    width = out_grad.shape[1]
    bias_rows = bias_grad.reshape(-1, width)
    used = 2 * hid + bias_rows.shape[0]
    unit = devices * 16
    padding = -used % unit
    stacked = jnp.concatenate(
        [in_grad_t, out_grad, bias_rows, jnp.zeros((padding, width), jnp.float32)], axis=0
    )
    totals = mean_over_devices(stacked, groups, doms)
    return (
        anchor_kl,
        node_grad,
        totals[:hid].T,
        totals[2 * hid : used].reshape(-1),
        totals[hid : 2 * hid],
    )


def solution(mesh):
    return jax.shard_map(
        shards,
        mesh=mesh,
        in_specs=(
            P(("group", "dom"), None),
            P(),
            P(),
            P(),
            P(("group", "dom")),
            P(("group", "dom"), None),
            P("group", "dom", None, None),
            P("group", "dom", None),
            P(("group", "dom"), None),
            P(("group", "dom"), None),
        ),
        out_specs=(P(("group", "dom")), P(("group", "dom"), None), P(), P(), P()),
        check_vma=False,
    )
```

```python
import functools
import math

import jax
import jax.numpy as jnp
from jax import lax
from jax.experimental import pallas as pl
from jax.experimental.pallas import tpu as pltpu
from jax.sharding import PartitionSpec as P

TILE = 128
ABLK = 128

SCORE_SCALE = 8.0
EPSILON = 1e-06
VMEM_LIMIT = 60 * 1024 * 1024
CHUNK = 256

ONE_COPY = pl.Buffered(1)


def whole(shape):
    return pl.BlockSpec(shape, lambda *_: (0,) * len(shape), pipeline_mode=ONE_COPY)


def node_rows(feature_rows, w_in, b_in, w_out):
    pre_act = jnp.dot(feature_rows, w_in, preferred_element_type=jnp.float32) + b_in
    hidden = (pre_act * jax.nn.sigmoid(pre_act)).astype(jnp.bfloat16)
    embedding = jnp.dot(hidden, w_out, preferred_element_type=jnp.float32)
    spread = jnp.sqrt(jnp.mean(embedding * embedding, axis=1, keepdims=True) + EPSILON)
    return embedding, (embedding / spread).astype(jnp.bfloat16)


def rows_of(index, count=TILE):
    return pl.ds(pl.multiple_of(index * count, count), count)


def cost(flops, moved, powers):
    return pl.CostEstimate(flops=flops, bytes_accessed=moved, transcendentals=powers)


def clear_rows(ref):
    zero_chunk = jnp.zeros((CHUNK, ref.shape[1]), ref.dtype)

    def clear(index, carry):
        ref[rows_of(index, CHUNK), :] = zero_chunk
        return carry

    lax.fori_loop(0, ref.shape[0] // CHUNK, clear, 0)


def as_row(column):
    return jnp.broadcast_to(column, (ABLK, TILE)).T[0:1, :]


def as_column(row):
    return jnp.broadcast_to(row, (TILE, ABLK)).T[:, 0:1]


def tile_scores(anchors, context):
    return lax.dot_general(
        anchors, context, (((1,), (1,)), ((), ())), preferred_element_type=jnp.float32
    )


def prepare_block(
    scale, shapes, block, rows, teacher_rows, ids_ref, tiles_ref, refs_ref, counts_ref,
    table, table_f, anchor_rows, near_rows, far_rows,
):
    local_count, remote_count, slot_count = shapes

    def gather(index, carry):
        for lane in range(16):
            row = index * 16 + lane
            anchor_rows[row, :] = table_f[ids_ref[block * ABLK + row], :]
        return carry

    lax.fori_loop(0, ABLK // 16, gather, 0)
    anchors = (anchor_rows[...] * scale).astype(jnp.bfloat16)
    target_sum = gap_sum = student_sum = None
    exps = []
    for i in range(local_count + remote_count):
        teacher = teacher_rows[rows, i * TILE : (i + 1) * TILE].astype(jnp.float32)
        target_exp = jnp.exp(teacher)
        if i >= local_count:
            ref = refs_ref[block * remote_count + i - local_count]
            live = lax.rem(ref, slot_count) < counts_ref[lax.div(ref, slot_count)]
            target_exp = target_exp * jnp.where(live, 1.0, 0.0).astype(jnp.float32)
            gap = target_exp * teacher
        else:
            scores = tile_scores(anchors, table[tiles_ref[block * local_count + i]])
            gap = target_exp * (teacher - scores)
            student_exp = jnp.exp(scores)
            student_sum = student_exp if i == 0 else student_sum + student_exp
        target_sum = target_exp if i == 0 else target_sum + target_exp
        gap_sum = gap if i == 0 else gap_sum + gap
        exps.append(target_exp)
    total = jnp.sum(target_sum, axis=1, keepdims=True)
    inverse = 1.0 / total
    base = jnp.sum(gap_sum, axis=1, keepdims=True) * inverse - jnp.log(total)
    for i, target_exp in enumerate(exps):
        out, at = (near_rows, i) if i < local_count else (far_rows, i - local_count)
        out[rows, at * TILE : (at + 1) * TILE] = (target_exp * inverse).astype(jnp.bfloat16)
    return anchors, as_row(base), as_row(jnp.sum(student_sum, axis=1, keepdims=True))


def take_context(block, sub, context, tiles_ref, refs_ref, table_ref, fetched_ref, counts):
    local_count, remote_count = counts
    places = []
    for i in range(local_count):
        place = rows_of(tiles_ref[block * local_count + i])
        context[sub, i * TILE : (i + 1) * TILE, :] = table_ref[place, :]
        places.append(place)
    for i in range(remote_count):
        place = rows_of(refs_ref[block * remote_count + i])
        at = local_count + i
        context[sub, at * TILE : (at + 1) * TILE, :] = fetched_ref[place, :]
        places.append(place)
    return places


def tile_grad(delta, anchors):
    return lax.dot_general(
        delta, anchors, (((0,), (0,)), ((), ())), preferred_element_type=jnp.float32
    )


def score_kernel(
    per_step, remote_count, slot_count, refs_ref, counts_ref,
    fetched_ref, anchors_ref, far_ref, base_ref, partial_ref,
    kl_ref, inverse_ref, delta_ref, remote_grad_ref, remote_acc,
):
    @pl.when(pl.program_id(0) == 0)
    def _():
        clear_rows(remote_acc)

    for sub in range(per_step):
        block = pl.program_id(0) * per_step + sub
        rows = slice(sub * ABLK, (sub + 1) * ABLK)
        anchors = anchors_ref[rows, :]
        places = []
        student = []
        student_sum = gap_sum = None
        for i in range(remote_count):
            span = slice(i * TILE, (i + 1) * TILE)
            ref = refs_ref[block * remote_count + i]
            places.append(rows_of(ref))
            live = lax.rem(ref, slot_count) < counts_ref[lax.div(ref, slot_count)]
            scores = tile_scores(anchors, fetched_ref[places[i], :])
            student_exp = jnp.exp(scores) * jnp.where(live, 1.0, 0.0).astype(jnp.float32)
            gap = far_ref[rows, span].astype(jnp.float32) * scores
            student_sum = student_exp if i == 0 else student_sum + student_exp
            gap_sum = gap if i == 0 else gap_sum + gap
            student.append(student_exp)
        total = as_column(partial_ref[sub]) + jnp.sum(student_sum, axis=1, keepdims=True)
        inverse = 1.0 / total
        rest = jnp.log(total) - jnp.sum(gap_sum, axis=1, keepdims=True)
        kl_ref[sub] = base_ref[sub] + as_row(rest)
        inverse_ref[sub] = as_row(inverse)
        for i in range(remote_count):
            span = slice(i * TILE, (i + 1) * TILE)
            delta = (student[i] * inverse - far_ref[rows, span].astype(jnp.float32)).astype(
                jnp.bfloat16
            )
            delta_ref[rows, span] = delta
            remote_acc[places[i], :] += tile_grad(delta, anchors)

    @pl.when(pl.program_id(0) == pl.num_programs(0) - 1)
    def _():
        def finish(index, carry):
            here = rows_of(index, CHUNK)
            remote_grad_ref[here, :] = remote_acc[here, :].astype(jnp.bfloat16)
            return carry

        lax.fori_loop(0, remote_acc.shape[0] // CHUNK, finish, 0)


def score(per_step, remote_refs, own_counts, fetched, prepared, slots):
    anchors, near, far, base, partial = prepared
    blocks, remote_count = remote_refs.shape
    width = anchors.shape[1]
    rows = per_step * ABLK
    pairs = far.shape[0] * far.shape[1]
    row_spec = pl.BlockSpec((per_step, 1, ABLK), lambda b, *_: (b, 0, 0))
    far_spec = pl.BlockSpec((rows, far.shape[1]), lambda b, *_: (b, 0))
    return pl.pallas_call(
        functools.partial(score_kernel, per_step, remote_count, slots),
        out_shape=(
            jax.ShapeDtypeStruct((blocks, 1, ABLK), jnp.float32),
            jax.ShapeDtypeStruct((blocks, 1, ABLK), jnp.float32),
            jax.ShapeDtypeStruct(far.shape, jnp.bfloat16),
            jax.ShapeDtypeStruct(fetched.shape, jnp.bfloat16),
        ),
        grid_spec=pltpu.PrefetchScalarGridSpec(
            num_scalar_prefetch=2,
            grid=(blocks // per_step,),
            in_specs=[
                whole(fetched.shape),
                pl.BlockSpec((rows, width), lambda b, *_: (b, 0)),
                far_spec,
                row_spec,
                row_spec,
            ],
            out_specs=(row_spec, row_spec, far_spec, whole(fetched.shape)),
            scratch_shapes=[pltpu.VMEM(fetched.shape, jnp.float32)],
        ),
        compiler_params=pltpu.CompilerParams(vmem_limit_bytes=VMEM_LIMIT),
        cost_estimate=cost(3 * pairs * width, 4 * pairs, pairs),
    )(remote_refs.reshape(-1), own_counts, fetched, anchors, far, base, partial)


def local_kernel(
    per_step, local_count, remote_count, lanes, ids_ref, tiles_ref, refs_ref,
    table_ref, fetched_ref, anchors_ref, near_ref, inverse_ref, delta_ref, local_grad_ref,
    context, near_delta, anchor_grad, *row_accs,
):
    scale = SCORE_SCALE / table_ref.shape[1]

    @pl.when(pl.program_id(0) == 0)
    def _():
        clear_rows(local_grad_ref)
        for acc in row_accs:
            clear_rows(acc)

    for sub in range(per_step):
        block = pl.program_id(0) * per_step + sub
        rows = slice(sub * ABLK, (sub + 1) * ABLK)
        places = take_context(
            block, sub, context, tiles_ref, refs_ref, table_ref, fetched_ref,
            (local_count, remote_count),
        )
        anchors = anchors_ref[rows, :]
        inverse = as_column(inverse_ref[sub])
        near = local_count * TILE
        for i in range(local_count):
            span = slice(i * TILE, (i + 1) * TILE)
            student = jnp.exp(tile_scores(anchors, context[sub, span, :])) * inverse
            delta = (student - near_ref[rows, span].astype(jnp.float32)).astype(jnp.bfloat16)
            near_delta[rows, span] = delta
            local_grad_ref[places[i], :] += tile_grad(delta, anchors)
        near_part = jnp.dot(
            near_delta[rows, :], context[sub, :near, :], preferred_element_type=jnp.float32
        )
        far_part = jnp.dot(
            delta_ref[rows, :], context[sub, near:, :], preferred_element_type=jnp.float32
        )
        anchor_grad[rows, :] = (near_part + far_part) * scale
        for row in range(ABLK):
            acc = row_accs[row % lanes]
            at = sub * ABLK + row
            acc[pl.ds(ids_ref[block * ABLK + row], 1), :] += anchor_grad[at : at + 1, :]

    @pl.when(pl.program_id(0) == pl.num_programs(0) - 1)
    def _():
        def finish(index, carry):
            here = rows_of(index, CHUNK)
            total = local_grad_ref[here, :]
            for acc in row_accs:
                total = total + acc[here, :]
            local_grad_ref[here, :] = total
            return carry

        lax.fori_loop(0, local_grad_ref.shape[0] // CHUNK, finish, 0)


def local_grads(
    per_step, anchor_ids, local_tiles, remote_refs, table, fetched, anchors, near, inverse, delta
):
    blocks, local_count = local_tiles.shape
    remote_count = remote_refs.shape[1]
    context_width = near.shape[1] + delta.shape[1]
    width = table.shape[1]
    rows = per_step * ABLK
    lanes = 4 if table.shape[0] <= 8192 else 1
    pairs = delta.shape[0] * context_width
    return pl.pallas_call(
        functools.partial(local_kernel, per_step, local_count, remote_count, lanes),
        out_shape=jax.ShapeDtypeStruct(table.shape, jnp.float32),
        grid_spec=pltpu.PrefetchScalarGridSpec(
            num_scalar_prefetch=3,
            grid=(blocks // per_step,),
            in_specs=[
                whole(table.shape),
                whole(fetched.shape),
                pl.BlockSpec((rows, width), lambda b, *_: (b, 0)),
                pl.BlockSpec((rows, near.shape[1]), lambda b, *_: (b, 0)),
                pl.BlockSpec((per_step, 1, ABLK), lambda b, *_: (b, 0, 0)),
                pl.BlockSpec((rows, delta.shape[1]), lambda b, *_: (b, 0)),
            ],
            out_specs=whole(table.shape),
            scratch_shapes=[
                pltpu.VMEM((per_step, context_width, width), jnp.bfloat16),
                pltpu.VMEM((rows, near.shape[1]), jnp.bfloat16),
                pltpu.VMEM((rows, width), jnp.float32),
            ]
            + [pltpu.VMEM(table.shape, jnp.float32)] * lanes,
        ),
        compiler_params=pltpu.CompilerParams(vmem_limit_bytes=VMEM_LIMIT),
        cost_estimate=cost(3 * pairs * width, 2 * pairs, 0),
    )(
        anchor_ids, local_tiles.reshape(-1), remote_refs.reshape(-1),
        table, fetched, anchors, near, inverse, delta,
    )


def merge_kernel(asked_ref, local_ref, returned_ref, out_ref, acc):
    def load(index, carry):
        here = rows_of(index, CHUNK)
        acc[here, :] = local_ref[here, :]
        return carry

    lax.fori_loop(0, acc.shape[0] // CHUNK, load, 0)

    def add(slot, carry):
        acc[rows_of(asked_ref[slot]), :] += returned_ref[rows_of(slot), :].astype(jnp.float32)
        return carry

    lax.fori_loop(0, returned_ref.shape[0] // TILE, add, 0)

    def store(index, carry):
        here = rows_of(index, CHUNK)
        out_ref[here, :] = acc[here, :].astype(jnp.bfloat16)
        return carry

    lax.fori_loop(0, acc.shape[0] // CHUNK, store, 0)


def merge(asked, local_grad, returned):
    return pl.pallas_call(
        merge_kernel,
        out_shape=jax.ShapeDtypeStruct(local_grad.shape, jnp.bfloat16),
        grid_spec=pltpu.PrefetchScalarGridSpec(
            num_scalar_prefetch=1,
            grid=(1,),
            in_specs=[whole(local_grad.shape), whole(returned.shape)],
            out_specs=whole(local_grad.shape),
            scratch_shapes=[pltpu.VMEM(local_grad.shape, jnp.float32)],
        ),
        compiler_params=pltpu.CompilerParams(vmem_limit_bytes=VMEM_LIMIT),
    )(asked, local_grad, returned)


MESH = pl.DeviceIdType.MESH
ANYWHERE = pl.BlockSpec(memory_space=pl.ANY)
IN_VMEM = pl.BlockSpec(memory_space=pltpu.VMEM)


def greet(partners):
    barrier = pltpu.get_barrier_semaphore()
    for partner in partners:
        pl.semaphore_signal(barrier, inc=1, device_id=partner, device_id_type=MESH)
    pl.semaphore_wait(barrier, len(partners))


def push(src, dst, sems, index, partner):
    copy = pltpu.make_async_remote_copy(
        src_ref=src,
        dst_ref=dst,
        send_sem=sems[0].at[index],
        recv_sem=sems[1].at[index],
        device_id=partner,
        device_id_type=MESH,
    )
    copy.start()
    return copy


def dom_partners(doms):
    group, dom = lax.axis_index("group"), lax.axis_index("dom")
    chips = doms // 2
    chip, core = dom // 2, dom % 2
    other = chip * 2 + (1 - core)
    ahead = [lax.rem(chip + k, chips) * 2 + core for k in range(1, chips)]
    behind = [lax.rem(chip + chips - k, chips) for k in range(1, chips)]
    return group, dom, core, other, ahead, behind


def fetch_kernel(
    groups, doms, chunks, per_step, shapes,
    features_ref, w_in_ref, b_in_ref, w_out_ref, requests_ref, own_asks,
    ids_ref, tiles_ref, refs_ref, counts_ref, teacher_ref,
    table_ref, fetched_ref, embedding_ref, asked_ref,
    anchors_ref, near_ref, far_ref, base_ref, partial_ref,
    table, relay, served, blank, ask_out, ask_in, asked,
    table_f, anchor_rows, teacher_buf, near_buf, far_buf, in_sems, near_out_sems, far_out_sems,
    near_sems, far_sems, on_sems, swap_sems, relay_near, relay_far, relay_on,
    ask_sems, serve_sems, relay_serve, own_sems,
):
    group, dom, core, other, ahead, behind = dom_partners(doms)
    half = groups // 2
    slots = requests_ref.shape[1]
    count = features_ref.shape[0]
    part = count // chunks
    step = min(CHUNK, part)
    first = group // half * half
    place = lax.rem(group, half)
    mates = [first + lax.rem(place + k, half) for k in range(1, half)]
    partner = lax.rem(group + half, groups)
    peers = [lax.rem(group + k, groups) for k in range(1, groups)]
    steps = teacher_ref.shape[0] // (per_step * ABLK)
    step_rows = per_step * ABLK

    def teacher_in(index):
        return pltpu.make_async_copy(
            teacher_ref.at[rows_of(index, step_rows), :],
            teacher_buf.at[lax.rem(index, 2)],
            in_sems.at[lax.rem(index, 2)],
        )

    def targets_out(index):
        at = lax.rem(index, 2)
        rows = rows_of(index, step_rows)
        return (
            pltpu.make_async_copy(near_buf.at[at], near_ref.at[rows, :], near_out_sems.at[at]),
            pltpu.make_async_copy(far_buf.at[at], far_ref.at[rows, :], far_out_sems.at[at]),
        )

    def prepare_step(index, carry):
        at = lax.rem(index, 2)
        teacher_in(index).wait()

        @pl.when(index + 1 < steps)
        def _():
            teacher_in(index + 1).start()

        @pl.when(index >= 2)
        def _():
            for copy in targets_out(index - 2):
                copy.wait()

        for sub in range(per_step):
            block = index * per_step + sub
            anchors, base, partial = prepare_block(
                SCORE_SCALE / table.shape[2], shapes, block, pl.ds(sub * ABLK, ABLK),
                teacher_buf.at[at], ids_ref, tiles_ref, refs_ref, counts_ref,
                table, table_f, anchor_rows, near_buf.at[at], far_buf.at[at],
            )
            anchors_ref[rows_of(block), :] = anchors
            base_ref[block] = base
            partial_ref[block] = partial
        for copy in targets_out(index):
            copy.start()
        return carry

    teacher_in(0).start()
    greet(
        [(group, other)] + [(group, far) for far in ahead]
        + [(peer, dom) for peer in peers]
    )

    tiles = part // TILE

    def span(owner, chunk):
        return pl.ds(owner * (count // TILE) + chunk * tiles, tiles)

    def both(sems, *index):
        return sems[0].at[index], sems[1].at[index]

    def send(src, dst, sems, partner_at):
        copy = pltpu.make_async_remote_copy(
            src_ref=src, dst_ref=dst, send_sem=sems[0], recv_sem=sems[1],
            device_id=partner_at, device_id_type=MESH,
        )
        copy.start()
        return copy

    def spread_chunk(here, owner, chunk, near, far):
        rows = here.at[span(owner, chunk)]
        far_copies = [
            send(rows, rows, both(far, k, chunk), (group, there)) for k, there in enumerate(ahead)
        ]
        return far_copies, send(rows, rows, both(near, chunk), (group, other))

    def pass_on(here, far_copies, chunk, on):
        copies = []
        for k, copy in enumerate(far_copies):
            copy.wait_recv()
            rows = here.at[span(behind[k] * 2 + core, chunk)]
            copies.append(send(rows, rows, both(on, k, chunk), (group, other)))
        return copies

    ask_out[...] = jnp.zeros_like(ask_out)
    ask_out[:, 0:slots] = requests_ref[...]
    asks = [
        send(ask_out, ask_in.at[group], both(ask_sems, k), (peer, dom))
        for k, peer in enumerate(peers)
    ]
    ask_in[group] = ask_out[...]
    blank[...] = jnp.zeros_like(blank)
    sent = []
    far_copies, near_copies, swaps = [], [], []
    for chunk in range(chunks):
        def forward(index, carry):
            at = pl.ds(pl.multiple_of(chunk * part + index * step, step), step)
            embedding, unit_rows = node_rows(
                features_ref[at, :], w_in_ref[...], b_in_ref[...], w_out_ref[...]
            )
            embedding_ref[at, :] = embedding
            to = pl.ds((dom * count + chunk * part) // TILE + index * (step // TILE), step // TILE)
            table[to] = unit_rows.reshape(step // TILE, TILE, unit_rows.shape[1])
            return carry

        lax.fori_loop(0, part // step, forward, 0)
        rows = span(dom, chunk)
        swaps.append(
            send(table.at[rows], relay.at[rows], both(swap_sems, chunk), (partner, dom))
        )
        far, near = spread_chunk(table, dom, chunk, near_sems, far_sems)
        far_copies.append(far)
        near_copies.append(near)
    clear = pltpu.make_async_copy(blank, fetched_ref.at[pl.ds(group * slots, slots)], own_sems.at[0])
    clear.start()
    on_copies, relay_fars, relay_nears, relay_ons = [], [], [], []

    def relay_chunk(chunk):
        swaps[chunk].wait_recv()
        far, near = spread_chunk(relay, dom, chunk, relay_near, relay_far)
        relay_fars.append(far)
        relay_nears.append(near)

    for chunk in range(chunks):
        on_copies += pass_on(table, far_copies[chunk], chunk, on_sems)
        if chunk % 2 == 1:
            relay_chunk(chunk // 2)
    for copy in asks:
        copy.wait_recv()
    read_asks = pltpu.make_async_copy(ask_in, asked, own_sems.at[1])
    read_asks.start()
    asked_ref[...] = ask_in[...]
    for copy in on_copies + near_copies:
        copy.wait_recv()
    keep = pltpu.make_async_copy(table, table_ref, own_sems.at[2])
    keep.start()
    read_asks.wait()

    def serve(here, base, asked_of):
        for k in range(half - 1):
            source = mates[k]

            def pick(slot, carry):
                wanted = asked[source, asked_of, slot]
                served[base + k, slot] = here[wanted]
                return carry

            lax.fori_loop(0, slots, pick, 0)

    def push_served(base, asked_of, sems):
        return [
            send(
                served.at[base + k], fetched_ref.at[pl.ds(asked_of * slots, slots)], both(sems, k),
                (mate, dom),
            )
            for k, mate in enumerate(mates)
        ]

    serve(table, 0, group)
    sent += push_served(0, group, serve_sems)

    def widen(index, carry):
        table_f[rows_of(index), :] = table[index].astype(jnp.float32)
        return carry

    lax.fori_loop(0, table.shape[0], widen, 0)
    bounds = [steps * part // 16 for part in (0, 3, 6, 9, 12, 14, 16)]

    def prepare(segment):
        lax.fori_loop(bounds[segment], bounds[segment + 1], prepare_step, 0)

    def relay_pass(chunk):
        return pass_on(relay, relay_fars[chunk], chunk, relay_on)

    prepare(0)
    relay_chunk(2)
    relay_ons += relay_pass(0)
    prepare(1)
    relay_ons += relay_pass(1)
    prepare(2)
    relay_chunk(3)
    prepare(3)
    relay_ons += relay_pass(2)
    prepare(4)
    relay_ons += relay_pass(3)
    for copy in relay_ons + relay_nears:
        copy.wait_recv()
    serve(relay, half - 1, partner)
    sent += push_served(half - 1, partner, relay_serve)

    def pick_own(slot, carry):
        wanted = own_asks[partner, slot]
        served[2 * half - 2, slot] = relay[wanted]
        return carry

    lax.fori_loop(0, slots, pick_own, 0)
    mine = pltpu.make_async_copy(
        served.at[2 * half - 2], fetched_ref.at[pl.ds(partner * slots, slots)], own_sems.at[3]
    )
    mine.start()
    prepare(5)
    for index in range(max(steps - 2, 0), steps):
        for copy in targets_out(index):
            copy.wait()
    for copy in sent:
        copy.wait_recv()
    clear.wait()
    keep.wait()
    mine.wait()
    for copy in asks + swaps + near_copies + on_copies + relay_nears + relay_ons + sent:
        copy.wait_send()
    for copies in far_copies + relay_fars:
        for copy in copies:
            copy.wait_send()


def fetch_tiles(
    per_step, features, w_in, b_in, w_out, own_requests, anchor_ids, local_tiles, remote_refs,
    own_counts, teacher, groups, doms,
):
    slots = own_requests.shape[1]
    count = features.shape[0]
    width = w_out.shape[1]
    chunks = 4
    half = groups // 2
    far, mates = max(doms // 2 - 1, 1), max(half - 1, 1)
    dma = pltpu.SemaphoreType.DMA
    nodes = doms * count
    blocks, remote_count = remote_refs.shape
    local_count = local_tiles.shape[1]
    near, far_width = local_count * TILE, remote_count * TILE
    anchors, context_width = teacher.shape
    rows = per_step * ABLK
    peers = max(groups - 1, 1)
    in_smem = pl.BlockSpec(memory_space=pltpu.SMEM)
    table, fetched, embedding, asked, *prepared = pl.pallas_call(
        functools.partial(
            fetch_kernel, groups, doms, chunks, per_step, (local_count, remote_count, slots)
        ),
        out_shape=(
            jax.ShapeDtypeStruct((nodes // TILE, TILE, width), jnp.bfloat16),
            jax.ShapeDtypeStruct((groups * slots, TILE, width), jnp.bfloat16),
            jax.ShapeDtypeStruct((count, width), jnp.float32),
            jax.ShapeDtypeStruct((groups, groups, 128), jnp.int32),
            jax.ShapeDtypeStruct((anchors, width), jnp.bfloat16),
            jax.ShapeDtypeStruct((anchors, near), jnp.bfloat16),
            jax.ShapeDtypeStruct((anchors, far_width), jnp.bfloat16),
            jax.ShapeDtypeStruct((blocks, 1, ABLK), jnp.float32),
            jax.ShapeDtypeStruct((blocks, 1, ABLK), jnp.float32),
        ),
        in_specs=[IN_VMEM] * 5 + [in_smem] * 5 + [ANYWHERE],
        out_specs=(
            ANYWHERE, ANYWHERE, IN_VMEM, IN_VMEM, IN_VMEM, ANYWHERE, ANYWHERE, IN_VMEM, IN_VMEM
        ),
        scratch_shapes=[
            pltpu.VMEM((nodes // TILE, TILE, width), jnp.bfloat16),
            pltpu.VMEM((nodes // TILE, TILE, width), jnp.bfloat16),
            pltpu.VMEM((2 * half - 1, slots, TILE, width), jnp.bfloat16),
            pltpu.VMEM((slots, TILE, width), jnp.bfloat16),
            pltpu.VMEM((groups, 128), jnp.int32),
            pltpu.VMEM((groups, groups, 128), jnp.int32),
            pltpu.SMEM((groups, groups, 128), jnp.int32),
            pltpu.VMEM((nodes, width), jnp.float32),
            pltpu.VMEM((ABLK, width), jnp.float32),
            pltpu.VMEM((2, rows, context_width), jnp.bfloat16),
            pltpu.VMEM((2, rows, near), jnp.bfloat16),
            pltpu.VMEM((2, rows, far_width), jnp.bfloat16),
            dma((2,)),
            dma((2,)),
            dma((2,)),
            [dma((chunks,)), dma((chunks,))],
            [dma((far, chunks)), dma((far, chunks))],
            [dma((far, chunks)), dma((far, chunks))],
            [dma((chunks,)), dma((chunks,))],
            [dma((chunks,)), dma((chunks,))],
            [dma((far, chunks)), dma((far, chunks))],
            [dma((far, chunks)), dma((far, chunks))],
            [dma((peers,)), dma((peers,))],
            [dma((mates,)), dma((mates,))],
            [dma((mates,)), dma((mates,))],
            dma((4,)),
        ],
        compiler_params=pltpu.CompilerParams(
            collective_id=0, has_side_effects=True, vmem_limit_bytes=VMEM_LIMIT
        ),
    )(
        features, w_in, b_in.reshape(1, -1), w_out, own_requests, own_requests,
        anchor_ids, local_tiles.reshape(-1), remote_refs.reshape(-1), own_counts, teacher,
    )
    asked = lax.dynamic_index_in_dim(asked, lax.axis_index("group"), 1, keepdims=False)
    return (
        table.reshape(-1, width), fetched.reshape(-1, width), embedding,
        asked[:, :slots].reshape(-1), prepared,
    )


def scatter_kernel(
    doms, merged_ref, out_ref, mine, kept, near_got, far_out, far_got,
    own_sem, near_send, near_recv, far_send, far_recv,
):
    group, dom, core, other, ahead, behind = dom_partners(doms)
    count = out_ref.shape[0]
    chips = doms // 2
    greet([(group, other)] + [(group, far) for far in ahead])
    order = [dom // 2] + [lax.rem(dom // 2 + k, chips) for k in range(1, chips)]
    order = order[1:] + order[:1]
    near_copies = []
    own_copies = []
    for k, chip in enumerate(order):
        theirs = merged_ref.at[rows_of(chip * 2 + (1 - core), count), :]
        near_copies.append(push(theirs, near_got.at[k], (near_send, near_recv), k, (group, other)))
        ours = merged_ref.at[rows_of(chip * 2 + core, count), :]
        copy = pltpu.make_async_copy(ours, mine.at[k], own_sem.at[k])
        copy.start()
        own_copies.append(copy)
    far_copies = []
    for k in range(chips - 1):
        near_copies[k].wait_recv()
        own_copies[k].wait()
        total = mine[k].astype(jnp.float32) + near_got[k].astype(jnp.float32)
        far_out[k] = total.astype(jnp.bfloat16)
        far_copies.append(
            push(far_out.at[k], far_got.at[k], (far_send, far_recv), k, (group, ahead[k]))
        )
    near_copies[chips - 1].wait_recv()
    own_copies[chips - 1].wait()
    kept[...] = mine[chips - 1].astype(jnp.float32) + near_got[chips - 1].astype(jnp.float32)
    for k, copy in enumerate(far_copies):
        copy.wait_recv()
        kept[...] += far_got[k].astype(jnp.float32)
    out_ref[...] = kept[...]
    for copy in near_copies + far_copies:
        copy.wait_send()


def scatter_sums(merged, doms):
    count, width = merged.shape[0] // doms, merged.shape[1]
    chips = doms // 2
    far = max(chips - 1, 1)
    dma = pltpu.SemaphoreType.DMA
    return pl.pallas_call(
        functools.partial(scatter_kernel, doms),
        out_shape=jax.ShapeDtypeStruct((count, width), jnp.float32),
        in_specs=[ANYWHERE],
        out_specs=IN_VMEM,
        scratch_shapes=[
            pltpu.VMEM((chips, count, width), jnp.bfloat16),
            pltpu.VMEM((count, width), jnp.float32),
            pltpu.VMEM((chips, count, width), jnp.bfloat16),
            pltpu.VMEM((far, count, width), jnp.bfloat16),
            pltpu.VMEM((far, count, width), jnp.bfloat16),
            dma((chips,)), dma((chips,)), dma((chips,)), dma((far,)), dma((far,)),
        ],
        compiler_params=pltpu.CompilerParams(
            collective_id=1, has_side_effects=True, vmem_limit_bytes=VMEM_LIMIT
        ),
    )(merged)


def totals_kernel(
    groups, doms, x_ref, out_ref, out1, got1, part, out2, got2, gather1, gather2,
    send1, recv1, send2, recv2, send3, recv3, send4, recv4,
):
    group, dom = lax.axis_index("group"), lax.axis_index("dom")
    wide = x_ref.shape[0] // doms
    thin = wide // groups
    dom_peers = [lax.rem(dom + k, doms) for k in range(1, doms)]
    group_peers = [lax.rem(group + k, groups) for k in range(1, groups)]
    greet([(group, peer) for peer in dom_peers] + [(peer, dom) for peer in group_peers])
    copies = []
    first = []
    for k, peer in enumerate(dom_peers):
        out1[k] = x_ref[rows_of(peer, wide), :].astype(jnp.bfloat16)
        first.append(push(out1.at[k], got1.at[k], (send1, recv1), k, (group, peer)))
    part[...] = x_ref[rows_of(dom, wide), :]
    for k, copy in enumerate(first):
        copy.wait_recv()
        part[...] += got1[k].astype(jnp.float32)
    copies += first
    second = []
    for k, peer in enumerate(group_peers):
        out2[k] = part[rows_of(peer, thin), :].astype(jnp.bfloat16)
        second.append(push(out2.at[k], got2.at[k], (send2, recv2), k, (peer, dom)))
    total = part[rows_of(group, thin), :]
    for k, copy in enumerate(second):
        copy.wait_recv()
        total = total + got2[k].astype(jnp.float32)
    copies += second
    gather1[group] = (total * (1.0 / (groups * doms))).astype(jnp.bfloat16)
    mine = gather1.at[group]
    third = [
        push(mine, mine, (send3, recv3), k, (peer, dom)) for k, peer in enumerate(group_peers)
    ]
    for copy in third:
        copy.wait_recv()
    copies += third
    fourth = [
        push(gather1, gather2.at[dom], (send4, recv4), k, (group, peer))
        for k, peer in enumerate(dom_peers)
    ]
    out_ref[dom] = gather1[...].astype(jnp.float32)
    for k, copy in enumerate(fourth):
        copy.wait_recv()
        source = lax.rem(dom + doms - (k + 1), doms)
        out_ref[source] = gather2[source].astype(jnp.float32)
    copies += fourth
    for copy in copies:
        copy.wait_send()


def mean_over_devices(x, groups, doms):
    rows, width = x.shape
    wide = rows // doms
    thin = wide // groups
    a, b = max(doms - 1, 1), max(groups - 1, 1)
    half = jnp.bfloat16
    dma = pltpu.SemaphoreType.DMA
    out = pl.pallas_call(
        functools.partial(totals_kernel, groups, doms),
        out_shape=jax.ShapeDtypeStruct((doms, groups, thin, width), jnp.float32),
        in_specs=[IN_VMEM],
        out_specs=IN_VMEM,
        scratch_shapes=[
            pltpu.VMEM((a, wide, width), half),
            pltpu.VMEM((a, wide, width), half),
            pltpu.VMEM((wide, width), jnp.float32),
            pltpu.VMEM((b, thin, width), half),
            pltpu.VMEM((b, thin, width), half),
            pltpu.VMEM((groups, thin, width), half),
            pltpu.VMEM((doms, groups, thin, width), half),
            dma((a,)), dma((a,)), dma((b,)), dma((b,)), dma((b,)), dma((b,)), dma((a,)), dma((a,)),
        ],
        compiler_params=pltpu.CompilerParams(
            collective_id=2, has_side_effects=True, vmem_limit_bytes=VMEM_LIMIT
        ),
    )(x)
    return out.reshape(rows, width)


def shards(
    features, w_in, b_in, w_out, anchor_ids, local_tiles, requests, counts, remote_refs, teacher
):
    groups = lax.axis_size("group")
    doms = lax.axis_size("dom")
    devices = groups * doms
    own_requests = requests[0, 0]
    own_counts = counts[0, 0]
    slot_count = own_requests.shape[1]
    per_step = math.gcd(local_tiles.shape[0], 2)
    table, fetched, embedding, asked, prepared = fetch_tiles(
        per_step, features, w_in, b_in, w_out, own_requests, anchor_ids, local_tiles,
        remote_refs, own_counts, teacher, groups, doms,
    )
    anchor_kl, inverse, delta, remote_grad = score(
        per_step, remote_refs, own_counts, fetched, prepared, slot_count
    )
    anchor_kl = anchor_kl.reshape(-1)
    returned = lax.all_to_all(remote_grad, "group", split_axis=0, concat_axis=0, tiled=True)
    local_grad = local_grads(
        per_step, anchor_ids, local_tiles, remote_refs, table, fetched, prepared[0], prepared[1],
        inverse, delta,
    )
    merged = merge(asked, local_grad, returned)
    node_grad = scatter_sums(merged, doms)
    pre_act = jnp.dot(features, w_in, preferred_element_type=jnp.float32) + b_in
    hidden = jax.nn.silu(pre_act).astype(jnp.bfloat16)
    spread = jnp.sqrt(jnp.mean(embedding * embedding, axis=1, keepdims=True) + EPSILON)
    normed = embedding / spread
    embed_grad = (
        (node_grad - normed * jnp.mean(node_grad * normed, axis=1, keepdims=True)) / spread
    ).astype(jnp.bfloat16)
    out_grad = jnp.dot(hidden.T, embed_grad, preferred_element_type=jnp.float32)
    hidden_grad = jnp.dot(embed_grad, w_out.T, preferred_element_type=jnp.float32)
    sigmoid_pre = jax.nn.sigmoid(pre_act)
    pre_grad = hidden_grad * sigmoid_pre * (1.0 + pre_act * (1.0 - sigmoid_pre))
    bias_grad = jnp.sum(pre_grad, axis=0)
    in_grad_t = jnp.dot(
        pre_grad.astype(jnp.bfloat16).T, features, preferred_element_type=jnp.float32
    )
    hid = in_grad_t.shape[0]
    width = out_grad.shape[1]
    bias_rows = bias_grad.reshape(-1, width)
    used = 2 * hid + bias_rows.shape[0]
    unit = devices * 16
    padding = -used % unit
    stacked = jnp.concatenate(
        [in_grad_t, out_grad, bias_rows, jnp.zeros((padding, width), jnp.float32)], axis=0
    )
    totals = mean_over_devices(stacked, groups, doms)
    return (
        anchor_kl,
        node_grad,
        totals[:hid].T,
        totals[2 * hid : used].reshape(-1),
        totals[hid : 2 * hid],
    )


def solution(mesh):
    return jax.shard_map(
        shards,
        mesh=mesh,
        in_specs=(
            P(("group", "dom"), None),
            P(),
            P(),
            P(),
            P(("group", "dom")),
            P(("group", "dom"), None),
            P("group", "dom", None, None),
            P("group", "dom", None),
            P(("group", "dom"), None),
            P(("group", "dom"), None),
        ),
        out_specs=(P(("group", "dom")), P(("group", "dom"), None), P(), P(), P()),
        check_vma=False,
    )
```

```python
import functools
import math

import jax
import jax.numpy as jnp
from jax import lax
from jax.experimental import pallas as pl
from jax.experimental.pallas import tpu as pltpu
from jax.sharding import PartitionSpec as P

TILE = 128
ABLK = 128

SCORE_SCALE = 8.0
EPSILON = 1e-06
VMEM_LIMIT = 60 * 1024 * 1024
CHUNK = 256

ONE_COPY = pl.Buffered(1)


def whole(shape):
    return pl.BlockSpec(shape, lambda *_: (0,) * len(shape), pipeline_mode=ONE_COPY)


def node_rows(feature_rows, w_in, b_in, w_out):
    pre_act = jnp.dot(feature_rows, w_in, preferred_element_type=jnp.float32) + b_in
    hidden = (pre_act * jax.nn.sigmoid(pre_act)).astype(jnp.bfloat16)
    embedding = jnp.dot(hidden, w_out, preferred_element_type=jnp.float32)
    spread = jnp.sqrt(jnp.mean(embedding * embedding, axis=1, keepdims=True) + EPSILON)
    return embedding, (embedding / spread).astype(jnp.bfloat16)


def rows_of(index, count=TILE):
    return pl.ds(pl.multiple_of(index * count, count), count)


def cost(flops, moved, powers):
    return pl.CostEstimate(flops=flops, bytes_accessed=moved, transcendentals=powers)


def clear_rows(ref):
    zero_chunk = jnp.zeros((CHUNK, ref.shape[1]), ref.dtype)

    def clear(index, carry):
        ref[rows_of(index, CHUNK), :] = zero_chunk
        return carry

    lax.fori_loop(0, ref.shape[0] // CHUNK, clear, 0)


def as_row(column):
    return jnp.broadcast_to(column, (ABLK, TILE)).T[0:1, :]


def as_column(row):
    return jnp.broadcast_to(row, (TILE, ABLK)).T[:, 0:1]


def tile_scores(anchors, context):
    return lax.dot_general(
        anchors, context, (((1,), (1,)), ((), ())), preferred_element_type=jnp.float32
    )


def prepare_block(
    scale, shapes, block, rows, teacher_rows, ids_ref, tiles_ref, refs_ref, counts_ref,
    table, table_f, anchor_rows, near_rows, far_rows,
):
    local_count, remote_count, slot_count = shapes

    def gather(index, carry):
        for lane in range(16):
            row = index * 16 + lane
            anchor_rows[row, :] = table_f[ids_ref[block * ABLK + row], :]
        return carry

    lax.fori_loop(0, ABLK // 16, gather, 0)
    anchors = (anchor_rows[...] * scale).astype(jnp.bfloat16)
    target_sum = gap_sum = student_sum = None
    exps = []
    for i in range(local_count + remote_count):
        teacher = teacher_rows[rows, i * TILE : (i + 1) * TILE].astype(jnp.float32)
        target_exp = jnp.exp(teacher)
        if i >= local_count:
            ref = refs_ref[block * remote_count + i - local_count]
            live = lax.rem(ref, slot_count) < counts_ref[lax.div(ref, slot_count)]
            target_exp = target_exp * jnp.where(live, 1.0, 0.0).astype(jnp.float32)
            gap = target_exp * teacher
        else:
            scores = tile_scores(anchors, table[tiles_ref[block * local_count + i]])
            gap = target_exp * (teacher - scores)
            student_exp = jnp.exp(scores)
            student_sum = student_exp if i == 0 else student_sum + student_exp
        target_sum = target_exp if i == 0 else target_sum + target_exp
        gap_sum = gap if i == 0 else gap_sum + gap
        exps.append(target_exp)
    total = jnp.sum(target_sum, axis=1, keepdims=True)
    inverse = 1.0 / total
    base = jnp.sum(gap_sum, axis=1, keepdims=True) * inverse - jnp.log(total)
    for i, target_exp in enumerate(exps):
        out, at = (near_rows, i) if i < local_count else (far_rows, i - local_count)
        out[rows, at * TILE : (at + 1) * TILE] = (target_exp * inverse).astype(jnp.bfloat16)
    return anchors, as_row(base), as_row(jnp.sum(student_sum, axis=1, keepdims=True))


def take_context(block, sub, context, tiles_ref, refs_ref, table_ref, fetched_ref, counts):
    local_count, remote_count = counts
    places = []
    for i in range(local_count):
        place = rows_of(tiles_ref[block * local_count + i])
        context[sub, i * TILE : (i + 1) * TILE, :] = table_ref[place, :]
        places.append(place)
    for i in range(remote_count):
        place = rows_of(refs_ref[block * remote_count + i])
        at = local_count + i
        context[sub, at * TILE : (at + 1) * TILE, :] = fetched_ref[place, :]
        places.append(place)
    return places


def tile_grad(delta, anchors):
    return lax.dot_general(
        delta, anchors, (((0,), (0,)), ((), ())), preferred_element_type=jnp.float32
    )


def score_kernel(
    per_step, remote_count, slot_count, refs_ref, counts_ref,
    fetched_ref, anchors_ref, far_ref, base_ref, partial_ref,
    kl_ref, inverse_ref, delta_ref, remote_grad_ref, remote_acc,
):
    @pl.when(pl.program_id(0) == 0)
    def _():
        clear_rows(remote_acc)

    for sub in range(per_step):
        block = pl.program_id(0) * per_step + sub
        rows = slice(sub * ABLK, (sub + 1) * ABLK)
        anchors = anchors_ref[rows, :]
        places = []
        student = []
        student_sum = gap_sum = None
        for i in range(remote_count):
            span = slice(i * TILE, (i + 1) * TILE)
            ref = refs_ref[block * remote_count + i]
            places.append(rows_of(ref))
            live = lax.rem(ref, slot_count) < counts_ref[lax.div(ref, slot_count)]
            scores = tile_scores(anchors, fetched_ref[places[i], :])
            student_exp = jnp.exp(scores) * jnp.where(live, 1.0, 0.0).astype(jnp.float32)
            gap = far_ref[rows, span].astype(jnp.float32) * scores
            student_sum = student_exp if i == 0 else student_sum + student_exp
            gap_sum = gap if i == 0 else gap_sum + gap
            student.append(student_exp)
        total = as_column(partial_ref[sub]) + jnp.sum(student_sum, axis=1, keepdims=True)
        inverse = 1.0 / total
        rest = jnp.log(total) - jnp.sum(gap_sum, axis=1, keepdims=True)
        kl_ref[sub] = base_ref[sub] + as_row(rest)
        inverse_ref[sub] = as_row(inverse)
        for i in range(remote_count):
            span = slice(i * TILE, (i + 1) * TILE)
            delta = (student[i] * inverse - far_ref[rows, span].astype(jnp.float32)).astype(
                jnp.bfloat16
            )
            delta_ref[rows, span] = delta
            remote_acc[places[i], :] += tile_grad(delta, anchors)

    @pl.when(pl.program_id(0) == pl.num_programs(0) - 1)
    def _():
        def finish(index, carry):
            here = rows_of(index, CHUNK)
            remote_grad_ref[here, :] = remote_acc[here, :].astype(jnp.bfloat16)
            return carry

        lax.fori_loop(0, remote_acc.shape[0] // CHUNK, finish, 0)


def score(per_step, remote_refs, own_counts, fetched, prepared, slots):
    anchors, near, far, base, partial = prepared
    blocks, remote_count = remote_refs.shape
    width = anchors.shape[1]
    rows = per_step * ABLK
    pairs = far.shape[0] * far.shape[1]
    row_spec = pl.BlockSpec((per_step, 1, ABLK), lambda b, *_: (b, 0, 0))
    far_spec = pl.BlockSpec((rows, far.shape[1]), lambda b, *_: (b, 0))
    return pl.pallas_call(
        functools.partial(score_kernel, per_step, remote_count, slots),
        out_shape=(
            jax.ShapeDtypeStruct((blocks, 1, ABLK), jnp.float32),
            jax.ShapeDtypeStruct((blocks, 1, ABLK), jnp.float32),
            jax.ShapeDtypeStruct(far.shape, jnp.bfloat16),
            jax.ShapeDtypeStruct(fetched.shape, jnp.bfloat16),
        ),
        grid_spec=pltpu.PrefetchScalarGridSpec(
            num_scalar_prefetch=2,
            grid=(blocks // per_step,),
            in_specs=[
                whole(fetched.shape),
                pl.BlockSpec((rows, width), lambda b, *_: (b, 0)),
                far_spec,
                row_spec,
                row_spec,
            ],
            out_specs=(row_spec, row_spec, far_spec, whole(fetched.shape)),
            scratch_shapes=[pltpu.VMEM(fetched.shape, jnp.float32)],
        ),
        compiler_params=pltpu.CompilerParams(vmem_limit_bytes=VMEM_LIMIT),
        cost_estimate=cost(3 * pairs * width, 4 * pairs, pairs),
    )(remote_refs.reshape(-1), own_counts, fetched, anchors, far, base, partial)


def local_kernel(
    per_step, local_count, remote_count, lanes, ids_ref, tiles_ref, refs_ref,
    table_ref, fetched_ref, anchors_ref, near_ref, inverse_ref, delta_ref, local_grad_ref,
    context, near_delta, anchor_grad, *row_accs,
):
    scale = SCORE_SCALE / table_ref.shape[1]

    @pl.when(pl.program_id(0) == 0)
    def _():
        clear_rows(local_grad_ref)
        for acc in row_accs:
            clear_rows(acc)

    for sub in range(per_step):
        block = pl.program_id(0) * per_step + sub
        rows = slice(sub * ABLK, (sub + 1) * ABLK)
        places = take_context(
            block, sub, context, tiles_ref, refs_ref, table_ref, fetched_ref,
            (local_count, remote_count),
        )
        anchors = anchors_ref[rows, :]
        inverse = as_column(inverse_ref[sub])
        near = local_count * TILE
        for i in range(local_count):
            span = slice(i * TILE, (i + 1) * TILE)
            student = jnp.exp(tile_scores(anchors, context[sub, span, :])) * inverse
            delta = (student - near_ref[rows, span].astype(jnp.float32)).astype(jnp.bfloat16)
            near_delta[rows, span] = delta
            local_grad_ref[places[i], :] += tile_grad(delta, anchors)
        near_part = jnp.dot(
            near_delta[rows, :], context[sub, :near, :], preferred_element_type=jnp.float32
        )
        far_part = jnp.dot(
            delta_ref[rows, :], context[sub, near:, :], preferred_element_type=jnp.float32
        )
        anchor_grad[rows, :] = (near_part + far_part) * scale
        for row in range(ABLK):
            acc = row_accs[row % lanes]
            at = sub * ABLK + row
            acc[pl.ds(ids_ref[block * ABLK + row], 1), :] += anchor_grad[at : at + 1, :]

    @pl.when(pl.program_id(0) == pl.num_programs(0) - 1)
    def _():
        def finish(index, carry):
            here = rows_of(index, CHUNK)
            total = local_grad_ref[here, :]
            for acc in row_accs:
                total = total + acc[here, :]
            local_grad_ref[here, :] = total
            return carry

        lax.fori_loop(0, local_grad_ref.shape[0] // CHUNK, finish, 0)


def local_grads(
    per_step, anchor_ids, local_tiles, remote_refs, table, fetched, anchors, near, inverse, delta
):
    blocks, local_count = local_tiles.shape
    remote_count = remote_refs.shape[1]
    context_width = near.shape[1] + delta.shape[1]
    width = table.shape[1]
    rows = per_step * ABLK
    lanes = 4 if table.shape[0] <= 8192 else 1
    pairs = delta.shape[0] * context_width
    return pl.pallas_call(
        functools.partial(local_kernel, per_step, local_count, remote_count, lanes),
        out_shape=jax.ShapeDtypeStruct(table.shape, jnp.float32),
        grid_spec=pltpu.PrefetchScalarGridSpec(
            num_scalar_prefetch=3,
            grid=(blocks // per_step,),
            in_specs=[
                whole(table.shape),
                whole(fetched.shape),
                pl.BlockSpec((rows, width), lambda b, *_: (b, 0)),
                pl.BlockSpec((rows, near.shape[1]), lambda b, *_: (b, 0)),
                pl.BlockSpec((per_step, 1, ABLK), lambda b, *_: (b, 0, 0)),
                pl.BlockSpec((rows, delta.shape[1]), lambda b, *_: (b, 0)),
            ],
            out_specs=whole(table.shape),
            scratch_shapes=[
                pltpu.VMEM((per_step, context_width, width), jnp.bfloat16),
                pltpu.VMEM((rows, near.shape[1]), jnp.bfloat16),
                pltpu.VMEM((rows, width), jnp.float32),
            ]
            + [pltpu.VMEM(table.shape, jnp.float32)] * lanes,
        ),
        compiler_params=pltpu.CompilerParams(vmem_limit_bytes=VMEM_LIMIT),
        cost_estimate=cost(3 * pairs * width, 2 * pairs, 0),
    )(
        anchor_ids, local_tiles.reshape(-1), remote_refs.reshape(-1),
        table, fetched, anchors, near, inverse, delta,
    )


def merge_kernel(asked_ref, local_ref, returned_ref, out_ref, acc):
    def load(index, carry):
        here = rows_of(index, CHUNK)
        acc[here, :] = local_ref[here, :]
        return carry

    lax.fori_loop(0, acc.shape[0] // CHUNK, load, 0)

    def add(slot, carry):
        acc[rows_of(asked_ref[slot]), :] += returned_ref[rows_of(slot), :].astype(jnp.float32)
        return carry

    lax.fori_loop(0, returned_ref.shape[0] // TILE, add, 0)

    def store(index, carry):
        here = rows_of(index, CHUNK)
        out_ref[here, :] = acc[here, :].astype(jnp.bfloat16)
        return carry

    lax.fori_loop(0, acc.shape[0] // CHUNK, store, 0)


def merge(asked, local_grad, returned):
    return pl.pallas_call(
        merge_kernel,
        out_shape=jax.ShapeDtypeStruct(local_grad.shape, jnp.bfloat16),
        grid_spec=pltpu.PrefetchScalarGridSpec(
            num_scalar_prefetch=1,
            grid=(1,),
            in_specs=[whole(local_grad.shape), whole(returned.shape)],
            out_specs=whole(local_grad.shape),
            scratch_shapes=[pltpu.VMEM(local_grad.shape, jnp.float32)],
        ),
        compiler_params=pltpu.CompilerParams(vmem_limit_bytes=VMEM_LIMIT),
    )(asked, local_grad, returned)


MESH = pl.DeviceIdType.MESH
ANYWHERE = pl.BlockSpec(memory_space=pl.ANY)
IN_VMEM = pl.BlockSpec(memory_space=pltpu.VMEM)


def greet(partners):
    barrier = pltpu.get_barrier_semaphore()
    for partner in partners:
        pl.semaphore_signal(barrier, inc=1, device_id=partner, device_id_type=MESH)
    pl.semaphore_wait(barrier, len(partners))


def dom_partners(doms):
    group, dom = lax.axis_index("group"), lax.axis_index("dom")
    chips = doms // 2
    chip, core = dom // 2, dom % 2
    other = chip * 2 + (1 - core)
    ahead = [lax.rem(chip + k, chips) * 2 + core for k in range(1, chips)]
    behind = [lax.rem(chip + chips - k, chips) for k in range(1, chips)]
    return group, dom, core, other, ahead, behind


def fetch_kernel(
    groups, doms, chunks, per_step, shapes,
    features_ref, w_in_ref, b_in_ref, w_out_ref, requests_ref, own_asks,
    ids_ref, tiles_ref, refs_ref, counts_ref, teacher_ref,
    table_ref, fetched_ref, embedding_ref, asked_ref,
    anchors_ref, near_ref, far_ref, base_ref, partial_ref,
    table, relay, served, blank, ask_out, ask_in, asked,
    table_f, anchor_rows, teacher_buf, near_buf, far_buf, in_sems, near_out_sems, far_out_sems,
    near_sems, far_sems, on_sems, swap_sems, relay_near, relay_far, relay_on,
    ask_sems, serve_sems, relay_serve, own_sems,
):
    group, dom, core, other, ahead, behind = dom_partners(doms)
    half = groups // 2
    slots = requests_ref.shape[1]
    count = features_ref.shape[0]
    part = count // chunks
    step = min(CHUNK, part)
    first = group // half * half
    place = lax.rem(group, half)
    mates = [first + lax.rem(place + k, half) for k in range(1, half)]
    partner = lax.rem(group + half, groups)
    peers = [lax.rem(group + k, groups) for k in range(1, groups)]
    steps = teacher_ref.shape[0] // (per_step * ABLK)
    step_rows = per_step * ABLK

    def teacher_in(index):
        return pltpu.make_async_copy(
            teacher_ref.at[rows_of(index, step_rows), :],
            teacher_buf.at[lax.rem(index, 2)],
            in_sems.at[lax.rem(index, 2)],
        )

    def targets_out(index):
        at = lax.rem(index, 2)
        rows = rows_of(index, step_rows)
        return (
            pltpu.make_async_copy(near_buf.at[at], near_ref.at[rows, :], near_out_sems.at[at]),
            pltpu.make_async_copy(far_buf.at[at], far_ref.at[rows, :], far_out_sems.at[at]),
        )

    def prepare_step(index, carry):
        at = lax.rem(index, 2)
        teacher_in(index).wait()

        @pl.when(index + 1 < steps)
        def _():
            teacher_in(index + 1).start()

        @pl.when(index >= 2)
        def _():
            for copy in targets_out(index - 2):
                copy.wait()

        for sub in range(per_step):
            block = index * per_step + sub
            anchors, base, partial = prepare_block(
                SCORE_SCALE / table.shape[2], shapes, block, pl.ds(sub * ABLK, ABLK),
                teacher_buf.at[at], ids_ref, tiles_ref, refs_ref, counts_ref,
                table, table_f, anchor_rows, near_buf.at[at], far_buf.at[at],
            )
            anchors_ref[rows_of(block), :] = anchors
            base_ref[block] = base
            partial_ref[block] = partial
        for copy in targets_out(index):
            copy.start()
        return carry

    teacher_in(0).start()
    greet(
        [(group, other)] + [(group, far) for far in ahead]
        + [(peer, dom) for peer in peers]
    )

    tiles = part // TILE

    def span(owner, chunk):
        return pl.ds(owner * (count // TILE) + chunk * tiles, tiles)

    def both(sems, *index):
        return sems[0].at[index], sems[1].at[index]

    def send(src, dst, sems, partner_at):
        copy = pltpu.make_async_remote_copy(
            src_ref=src, dst_ref=dst, send_sem=sems[0], recv_sem=sems[1],
            device_id=partner_at, device_id_type=MESH,
        )
        copy.start()
        return copy

    def spread_chunk(here, owner, chunk, near, far):
        rows = here.at[span(owner, chunk)]
        far_copies = [
            send(rows, rows, both(far, k, chunk), (group, there)) for k, there in enumerate(ahead)
        ]
        return far_copies, send(rows, rows, both(near, chunk), (group, other))

    def pass_on(here, far_copies, chunk, on):
        copies = []
        for k, copy in enumerate(far_copies):
            copy.wait_recv()
            rows = here.at[span(behind[k] * 2 + core, chunk)]
            copies.append(send(rows, rows, both(on, k, chunk), (group, other)))
        return copies

    ask_out[...] = jnp.zeros_like(ask_out)
    ask_out[:, 0:slots] = requests_ref[...]
    asks = [
        send(ask_out, ask_in.at[group], both(ask_sems, k), (peer, dom))
        for k, peer in enumerate(peers)
    ]
    ask_in[group] = ask_out[...]
    blank[...] = jnp.zeros_like(blank)
    sent = []
    far_copies, near_copies, swaps = [], [], []
    for chunk in range(chunks):
        def forward(index, carry):
            at = pl.ds(pl.multiple_of(chunk * part + index * step, step), step)
            embedding, unit_rows = node_rows(
                features_ref[at, :], w_in_ref[...], b_in_ref[...], w_out_ref[...]
            )
            embedding_ref[at, :] = embedding
            to = pl.ds((dom * count + chunk * part) // TILE + index * (step // TILE), step // TILE)
            table[to] = unit_rows.reshape(step // TILE, TILE, unit_rows.shape[1])
            return carry

        lax.fori_loop(0, part // step, forward, 0)
        rows = span(dom, chunk)
        swaps.append(
            send(table.at[rows], relay.at[rows], both(swap_sems, chunk), (partner, dom))
        )
        far, near = spread_chunk(table, dom, chunk, near_sems, far_sems)
        far_copies.append(far)
        near_copies.append(near)
    clear = pltpu.make_async_copy(blank, fetched_ref.at[pl.ds(group * slots, slots)], own_sems.at[0])
    clear.start()
    on_copies, relay_fars, relay_nears, relay_ons = [], [], [], []

    def relay_chunk(chunk):
        swaps[chunk].wait_recv()
        far, near = spread_chunk(relay, dom, chunk, relay_near, relay_far)
        relay_fars.append(far)
        relay_nears.append(near)

    for chunk in range(chunks):
        on_copies += pass_on(table, far_copies[chunk], chunk, on_sems)
        if chunk % 2 == 1:
            relay_chunk(chunk // 2)
    for copy in asks:
        copy.wait_recv()
    read_asks = pltpu.make_async_copy(ask_in, asked, own_sems.at[1])
    read_asks.start()
    asked_ref[...] = ask_in[...]
    for copy in on_copies + near_copies:
        copy.wait_recv()
    keep = pltpu.make_async_copy(table, table_ref, own_sems.at[2])
    keep.start()
    read_asks.wait()

    def serve(here, base, asked_of):
        for k in range(half - 1):
            source = mates[k]

            def pick(slot, carry):
                wanted = asked[source, asked_of, slot]
                served[base + k, slot] = here[wanted]
                return carry

            lax.fori_loop(0, slots, pick, 0)

    def push_served(base, asked_of, sems):
        return [
            send(
                served.at[base + k], fetched_ref.at[pl.ds(asked_of * slots, slots)], both(sems, k),
                (mate, dom),
            )
            for k, mate in enumerate(mates)
        ]

    serve(table, 0, group)
    sent += push_served(0, group, serve_sems)

    def widen(index, carry):
        table_f[rows_of(index), :] = table[index].astype(jnp.float32)
        return carry

    lax.fori_loop(0, table.shape[0], widen, 0)
    bounds = [steps * part // 16 for part in (0, 3, 6, 9, 12, 14, 16)]

    def prepare(segment):
        lax.fori_loop(bounds[segment], bounds[segment + 1], prepare_step, 0)

    def relay_pass(chunk):
        return pass_on(relay, relay_fars[chunk], chunk, relay_on)

    prepare(0)
    relay_chunk(2)
    relay_ons += relay_pass(0)
    prepare(1)
    relay_ons += relay_pass(1)
    prepare(2)
    relay_chunk(3)
    prepare(3)
    relay_ons += relay_pass(2)
    prepare(4)
    relay_ons += relay_pass(3)
    for copy in relay_ons + relay_nears:
        copy.wait_recv()
    serve(relay, half - 1, partner)
    sent += push_served(half - 1, partner, relay_serve)

    def pick_own(slot, carry):
        wanted = own_asks[partner, slot]
        served[2 * half - 2, slot] = relay[wanted]
        return carry

    lax.fori_loop(0, slots, pick_own, 0)
    mine = pltpu.make_async_copy(
        served.at[2 * half - 2], fetched_ref.at[pl.ds(partner * slots, slots)], own_sems.at[3]
    )
    mine.start()
    prepare(5)
    for index in range(max(steps - 2, 0), steps):
        for copy in targets_out(index):
            copy.wait()
    for copy in sent:
        copy.wait_recv()
    clear.wait()
    keep.wait()
    mine.wait()
    for copy in asks + swaps + near_copies + on_copies + relay_nears + relay_ons + sent:
        copy.wait_send()
    for copies in far_copies + relay_fars:
        for copy in copies:
            copy.wait_send()


def fetch_tiles(
    per_step, features, w_in, b_in, w_out, own_requests, anchor_ids, local_tiles, remote_refs,
    own_counts, teacher, groups, doms,
):
    slots = own_requests.shape[1]
    count = features.shape[0]
    width = w_out.shape[1]
    chunks = 4
    half = groups // 2
    far, mates = max(doms // 2 - 1, 1), max(half - 1, 1)
    dma = pltpu.SemaphoreType.DMA
    nodes = doms * count
    blocks, remote_count = remote_refs.shape
    local_count = local_tiles.shape[1]
    near, far_width = local_count * TILE, remote_count * TILE
    anchors, context_width = teacher.shape
    rows = per_step * ABLK
    peers = max(groups - 1, 1)
    in_smem = pl.BlockSpec(memory_space=pltpu.SMEM)
    table, fetched, embedding, asked, *prepared = pl.pallas_call(
        functools.partial(
            fetch_kernel, groups, doms, chunks, per_step, (local_count, remote_count, slots)
        ),
        out_shape=(
            jax.ShapeDtypeStruct((nodes // TILE, TILE, width), jnp.bfloat16),
            jax.ShapeDtypeStruct((groups * slots, TILE, width), jnp.bfloat16),
            jax.ShapeDtypeStruct((count, width), jnp.float32),
            jax.ShapeDtypeStruct((groups, groups, 128), jnp.int32),
            jax.ShapeDtypeStruct((anchors, width), jnp.bfloat16),
            jax.ShapeDtypeStruct((anchors, near), jnp.bfloat16),
            jax.ShapeDtypeStruct((anchors, far_width), jnp.bfloat16),
            jax.ShapeDtypeStruct((blocks, 1, ABLK), jnp.float32),
            jax.ShapeDtypeStruct((blocks, 1, ABLK), jnp.float32),
        ),
        in_specs=[IN_VMEM] * 5 + [in_smem] * 5 + [ANYWHERE],
        out_specs=(
            ANYWHERE, ANYWHERE, IN_VMEM, IN_VMEM, IN_VMEM, ANYWHERE, ANYWHERE, IN_VMEM, IN_VMEM
        ),
        scratch_shapes=[
            pltpu.VMEM((nodes // TILE, TILE, width), jnp.bfloat16),
            pltpu.VMEM((nodes // TILE, TILE, width), jnp.bfloat16),
            pltpu.VMEM((2 * half - 1, slots, TILE, width), jnp.bfloat16),
            pltpu.VMEM((slots, TILE, width), jnp.bfloat16),
            pltpu.VMEM((groups, 128), jnp.int32),
            pltpu.VMEM((groups, groups, 128), jnp.int32),
            pltpu.SMEM((groups, groups, 128), jnp.int32),
            pltpu.VMEM((nodes, width), jnp.float32),
            pltpu.VMEM((ABLK, width), jnp.float32),
            pltpu.VMEM((2, rows, context_width), jnp.bfloat16),
            pltpu.VMEM((2, rows, near), jnp.bfloat16),
            pltpu.VMEM((2, rows, far_width), jnp.bfloat16),
            dma((2,)),
            dma((2,)),
            dma((2,)),
            [dma((chunks,)), dma((chunks,))],
            [dma((far, chunks)), dma((far, chunks))],
            [dma((far, chunks)), dma((far, chunks))],
            [dma((chunks,)), dma((chunks,))],
            [dma((chunks,)), dma((chunks,))],
            [dma((far, chunks)), dma((far, chunks))],
            [dma((far, chunks)), dma((far, chunks))],
            [dma((peers,)), dma((peers,))],
            [dma((mates,)), dma((mates,))],
            [dma((mates,)), dma((mates,))],
            dma((4,)),
        ],
        compiler_params=pltpu.CompilerParams(
            collective_id=0, has_side_effects=True, vmem_limit_bytes=VMEM_LIMIT
        ),
    )(
        features, w_in, b_in.reshape(1, -1), w_out, own_requests, own_requests,
        anchor_ids, local_tiles.reshape(-1), remote_refs.reshape(-1), own_counts, teacher,
    )
    asked = lax.dynamic_index_in_dim(asked, lax.axis_index("group"), 1, keepdims=False)
    return (
        table.reshape(-1, width), fetched.reshape(-1, width), embedding,
        asked[:, :slots].reshape(-1), prepared,
    )


def finish_kernel(
    groups, doms, chunks, merged_ref, embedding_ref, features_ref, w_in_ref, b_in_ref, w_out_ref,
    node_ref, in_ref, bias_ref, out_ref,
    near_got, far_out, far_got, grad_rows, acc, bias_acc, bias_other, bias_all,
    half_out, half_got, shard_out, shard_got, gathered,
    near_sems, far_sems, half_sems, bias_sems, shard_sems, bias_all_sems, gather_sems, pass_sems,
):
    group, dom, core, other, ahead, behind = dom_partners(doms)
    count, width = node_ref.shape
    chips = doms // 2
    chip = dom // 2
    units = groups * chips
    unit = group * chips + chip
    blocks = acc.shape[0] // 2
    shard = shard_got.shape[1]
    part = count // chunks
    step = min(CHUNK, part)
    per_block = acc.shape[1] // shard
    barrier = pltpu.get_barrier_semaphore()

    def at_unit(index):
        return (index // chips, lax.rem(index, chips) * 2 + core)

    def unit_after(k):
        return lax.rem(unit + k + 1, units)

    def unit_before(k):
        return lax.rem(unit + units - k - 1, units)

    def each(start, stop, work):
        def body(k, carry):
            work(k)
            return carry

        lax.fori_loop(start, stop, body, 0)

    def greet_unit(k):
        pl.semaphore_signal(
            barrier, inc=1, device_id=at_unit(unit_after(k)), device_id_type=MESH
        )

    pl.semaphore_signal(barrier, inc=1, device_id=(group, other), device_id_type=MESH)
    each(0, units - 1, greet_unit)
    acc[...] = jnp.zeros_like(acc)
    bias_acc[...] = jnp.zeros_like(bias_acc)
    pl.semaphore_wait(barrier, units)

    def remote(src, dst, sems, index, device):
        return pltpu.make_async_remote_copy(
            src_ref=src, dst_ref=dst, send_sem=sems[0].at[index], recv_sem=sems[1].at[index],
            device_id=device, device_id_type=MESH,
        )

    order = [lax.rem(chip + k, chips) for k in range(1, chips)] + [chip]

    def rows_in(owner, chunk):
        return pl.ds(pl.multiple_of(owner * count + chunk * part, part), part)

    near_copies = {}
    for chunk in range(chunks):
        rows = pl.ds(chunk * part, part)
        for k, to in enumerate(order):
            theirs = merged_ref.at[rows_in(to * 2 + (1 - core), chunk), :]
            copy = remote(
                theirs, near_got.at[k, rows, :], near_sems, (k, chunk), (group, other)
            )
            copy.start()
            near_copies[k, chunk] = copy
    far_copies = {}
    for chunk in range(chunks):
        rows = pl.ds(chunk * part, part)
        for k in range(chips - 1):
            near_copies[k, chunk].wait_recv()
            total = merged_ref[rows_in(order[k] * 2 + core, chunk), :].astype(jnp.float32)
            total = total + near_got[k, rows, :].astype(jnp.float32)
            far_out[k, rows, :] = total.astype(jnp.bfloat16)
            copy = remote(
                far_out.at[k, rows, :], far_got.at[k, rows, :], far_sems, (k, chunk),
                (group, ahead[k]),
            )
            copy.start()
            far_copies[k, chunk] = copy

    def backward(base, hidden_half):
        here = pl.ds(base, step)
        span = blocks * 128
        lanes = pl.ds(pl.multiple_of(hidden_half * span, span), span)
        features = features_ref[here, :]
        grads = grad_rows[here, :]
        pre_act = (
            jnp.dot(features, w_in_ref[:, lanes], preferred_element_type=jnp.float32)
            + b_in_ref[:, lanes]
        )
        sigmoid_pre = jax.nn.sigmoid(pre_act)
        hidden = (pre_act * sigmoid_pre).astype(jnp.bfloat16)
        out_grad = tile_grad(grads, hidden)
        hidden_grad = tile_scores(grads, w_out_ref[lanes, :])
        pre_grad = hidden_grad * sigmoid_pre * (1.0 + pre_act * (1.0 - sigmoid_pre))
        bias = jnp.sum(pre_grad, axis=0, keepdims=True)
        in_grad = tile_grad(features, pre_grad.astype(jnp.bfloat16))
        for b in range(blocks):
            cols = slice(b * 128, (b + 1) * 128)
            at = hidden_half * blocks + b
            acc[at, 0:width, :] += in_grad[:, cols]
            acc[at, width : 2 * width, :] += out_grad[:, cols]
            bias_acc[pl.ds(at, 1), :] += bias[:, cols]

    half_copy = remote(half_out, half_got, half_sems, 0, (group, other))
    bias_copy = remote(bias_acc, bias_other, bias_sems, 0, (group, other))
    for chunk in range(chunks):
        rows = pl.ds(chunk * part, part)
        near_copies[chips - 1, chunk].wait_recv()
        total = merged_ref[rows_in(dom, chunk), :].astype(jnp.float32)
        total = total + near_got[chips - 1, rows, :].astype(jnp.float32)
        for k in range(chips - 1):
            far_copies[k, chunk].wait_recv()
            total = total + far_got[k, rows, :].astype(jnp.float32)
        node_ref[rows, :] = total
        embedding = embedding_ref[rows, :]
        spread = jnp.sqrt(jnp.mean(embedding * embedding, axis=1, keepdims=True) + EPSILON)
        normed = embedding / spread
        grads = (total - normed * jnp.mean(total * normed, axis=1, keepdims=True)) / spread
        grad_rows[rows, :] = grads.astype(jnp.bfloat16)
        for side in (1 - core, core):
            each(0, part // step, lambda k: backward(chunk * part + k * step, side))
            if chunk == chunks - 1 and side is not core:
                for b in range(blocks):
                    half_out[b] = acc[side * blocks + b].astype(jnp.bfloat16)
                half_copy.start()
    bias_copy.start()
    half_copy.wait_recv()

    def shard_at(index):
        block = index // per_block
        row = pl.ds(pl.multiple_of(lax.rem(index, per_block) * shard, shard), shard)
        mine = acc[core * blocks + block, row, :]
        return mine + half_got[block, row, :].astype(jnp.float32)

    def shard_copy(k):
        return remote(
            shard_out.at[k], shard_got.at[k], shard_sems, k, at_unit(unit_after(k))
        )

    def bias_all_copy(k):
        rows = bias_all.at[unit]
        return remote(rows, rows, bias_all_sems, k, at_unit(unit_after(k)))

    def gather_copy(k):
        rows = gathered.at[core, unit]
        return remote(rows, rows, gather_sems, k, at_unit(unit_after(k)))

    def pass_copy(k):
        rows = gathered.at[core, unit_before(k)]
        return remote(rows, rows, pass_sems, k, (group, other))

    def send_shard(k):
        shard_out[k] = shard_at(unit_after(k)).astype(jnp.bfloat16)
        shard_copy(k).start()

    each(0, units - 1, send_shard)
    bias_copy.wait_recv()
    bias_all[unit] = bias_acc[...] + bias_other[...]
    each(0, units - 1, lambda k: bias_all_copy(k).start())

    def add_shard(k, total):
        shard_copy(k).wait_recv()
        return total + shard_got[k].astype(jnp.float32)

    total = lax.fori_loop(0, units - 1, add_shard, shard_at(unit))
    scale = 1.0 / (groups * doms)
    gathered[core, unit] = (total * scale).astype(jnp.bfloat16)
    each(0, units - 1, lambda k: gather_copy(k).start())
    pass_copy(units - 1).start()

    def pass_on(k):
        gather_copy(k).wait_recv()
        pass_copy(k).start()

    each(0, units - 1, lambda k: bias_all_copy(k).wait_recv())
    bias_ref[...] = lax.fori_loop(
        1, units, lambda k, total: total + bias_all[k], bias_all[0]
    ) * scale
    each(0, units - 1, pass_on)

    def write(side):
        for b in range(blocks):
            rows = gathered[side, pl.ds(b * per_block, per_block)].astype(jnp.float32)
            rows = rows.reshape(per_block * shard, 128)
            span = pl.ds(pl.multiple_of((side * blocks + b) * 128, 128), 128)
            in_ref[:, span] = rows[0:width]
            out_ref[span, :] = rows[width : 2 * width].T

    write(core)
    each(0, units, lambda k: pass_copy(k).wait_recv())
    write(1 - core)
    for copy in list(near_copies.values()) + list(far_copies.values()) + [half_copy, bias_copy]:
        copy.wait_send()

    def drain(k):
        shard_copy(k).wait_send()
        bias_all_copy(k).wait_send()
        gather_copy(k).wait_send()
        pass_copy(k).wait_send()

    each(0, units - 1, drain)
    pass_copy(units - 1).wait_send()


def finish(merged, embedding, features, w_in, b_in, w_out, groups, doms):
    count, width = embedding.shape
    hid = w_out.shape[0]
    chips = doms // 2
    units = groups * chips
    chunks = 4
    blocks = hid // 128
    shard = hid * 2 * width // (2 * 128) // units
    far = max(chips - 1, 1)
    half = jnp.bfloat16
    dma = pltpu.SemaphoreType.DMA

    def pair(*shape):
        return [dma(shape), dma(shape)]

    node_grad, in_grad, bias, out_grad = pl.pallas_call(
        functools.partial(finish_kernel, groups, doms, chunks),
        out_shape=(
            jax.ShapeDtypeStruct((count, width), jnp.float32),
            jax.ShapeDtypeStruct((width, hid), jnp.float32),
            jax.ShapeDtypeStruct((blocks, 128), jnp.float32),
            jax.ShapeDtypeStruct((hid, width), jnp.float32),
        ),
        in_specs=[IN_VMEM] * 6,
        out_specs=(IN_VMEM,) * 4,
        scratch_shapes=[
            pltpu.VMEM((chips, count, width), half),
            pltpu.VMEM((far, count, width), half),
            pltpu.VMEM((far, count, width), half),
            pltpu.VMEM((count, width), half),
            pltpu.VMEM((blocks, 2 * width, 128), jnp.float32),
            pltpu.VMEM((blocks, 128), jnp.float32),
            pltpu.VMEM((blocks, 128), jnp.float32),
            pltpu.VMEM((units, blocks, 128), jnp.float32),
            pltpu.VMEM((blocks // 2, 2 * width, 128), half),
            pltpu.VMEM((blocks // 2, 2 * width, 128), half),
            pltpu.VMEM((units - 1, shard, 128), half),
            pltpu.VMEM((units - 1, shard, 128), half),
            pltpu.VMEM((2, units, shard, 128), half),
            pair(chips, chunks),
            pair(far, chunks),
            pair(1),
            pair(1),
            pair(units - 1),
            pair(units - 1),
            pair(units - 1),
            pair(units),
        ],
        compiler_params=pltpu.CompilerParams(
            collective_id=1, has_side_effects=True, vmem_limit_bytes=VMEM_LIMIT
        ),
    )(merged, embedding, features, w_in, b_in.reshape(1, -1), w_out)
    return node_grad, in_grad, bias.reshape(-1), out_grad


def shards(
    features, w_in, b_in, w_out, anchor_ids, local_tiles, requests, counts, remote_refs, teacher
):
    groups = lax.axis_size("group")
    doms = lax.axis_size("dom")
    devices = groups * doms
    own_requests = requests[0, 0]
    own_counts = counts[0, 0]
    slot_count = own_requests.shape[1]
    per_step = math.gcd(local_tiles.shape[0], 2)
    table, fetched, embedding, asked, prepared = fetch_tiles(
        per_step, features, w_in, b_in, w_out, own_requests, anchor_ids, local_tiles,
        remote_refs, own_counts, teacher, groups, doms,
    )
    anchor_kl, inverse, delta, remote_grad = score(
        per_step, remote_refs, own_counts, fetched, prepared, slot_count
    )
    anchor_kl = anchor_kl.reshape(-1)
    returned = lax.all_to_all(remote_grad, "group", split_axis=0, concat_axis=0, tiled=True)
    local_grad = local_grads(
        per_step, anchor_ids, local_tiles, remote_refs, table, fetched, prepared[0], prepared[1],
        inverse, delta,
    )
    merged = merge(asked, local_grad, returned)
    node_grad, in_grad, bias_grad, out_grad = finish(
        merged, embedding, features, w_in, b_in, w_out, groups, doms
    )
    return anchor_kl, node_grad, in_grad, bias_grad, out_grad


def solution(mesh):
    return jax.shard_map(
        shards,
        mesh=mesh,
        in_specs=(
            P(("group", "dom"), None),
            P(),
            P(),
            P(),
            P(("group", "dom")),
            P(("group", "dom"), None),
            P("group", "dom", None, None),
            P("group", "dom", None),
            P(("group", "dom"), None),
            P(("group", "dom"), None),
        ),
        out_specs=(P(("group", "dom")), P(("group", "dom"), None), P(), P(), P()),
        check_vma=False,
    )
```

```python
import functools
import math

import jax
import jax.numpy as jnp
from jax import lax
from jax.experimental import pallas as pl
from jax.experimental.pallas import tpu as pltpu
from jax.sharding import PartitionSpec as P

TILE = 128
ABLK = 128

SCORE_SCALE = 8.0
EPSILON = 1e-06
VMEM_LIMIT = 60 * 1024 * 1024
CHUNK = 256
LAY_STEPS = 2

ONE_COPY = pl.Buffered(1)


def whole(shape):
    return pl.BlockSpec(shape, lambda *_: (0,) * len(shape), pipeline_mode=ONE_COPY)


def node_rows(feature_rows, w_in, b_in, w_out):
    pre_act = jnp.dot(feature_rows, w_in, preferred_element_type=jnp.float32) + b_in
    hidden = (pre_act * jax.nn.sigmoid(pre_act)).astype(jnp.bfloat16)
    embedding = jnp.dot(hidden, w_out, preferred_element_type=jnp.float32)
    spread = jnp.sqrt(jnp.mean(embedding * embedding, axis=1, keepdims=True) + EPSILON)
    return embedding, (embedding / spread).astype(jnp.bfloat16)


def rows_of(index, count=TILE):
    return pl.ds(pl.multiple_of(index * count, count), count)


def cost(flops, moved, powers):
    return pl.CostEstimate(flops=flops, bytes_accessed=moved, transcendentals=powers)


def clear_rows(ref):
    zero_chunk = jnp.zeros((CHUNK, ref.shape[1]), ref.dtype)

    def clear(index, carry):
        ref[rows_of(index, CHUNK), :] = zero_chunk
        return carry

    lax.fori_loop(0, ref.shape[0] // CHUNK, clear, 0)


def tile_scores(anchors, context):
    return lax.dot_general(
        anchors, context, (((1,), (1,)), ((), ())), preferred_element_type=jnp.float32
    )


def prepare_block(
    scale, shapes, block, rows, teacher_rows, ids_ref, tiles_ref, refs_ref, counts_ref,
    table, table_f, anchor_rows, context, near_rows, far_rows,
):
    local_count, remote_count, slot_count = shapes

    def gather(index, carry):
        for lane in range(16):
            row = index * 16 + lane
            anchor_rows[row, :] = table_f[ids_ref[block * ABLK + row], :]
        return carry

    lax.fori_loop(0, ABLK // 16, gather, 0)
    anchors = (anchor_rows[...] * scale).astype(jnp.bfloat16)
    for i in range(local_count):
        context[i * TILE : (i + 1) * TILE, :] = table[tiles_ref[block * local_count + i]]
    all_scores = tile_scores(anchors, context[...])
    target_sum = gap_sum = student_sum = None
    exps = []
    for i in range(local_count + remote_count):
        teacher = teacher_rows[rows, i * TILE : (i + 1) * TILE].astype(jnp.float32)
        target_exp = jnp.exp(teacher)
        if i >= local_count:
            ref = refs_ref[block * remote_count + i - local_count]
            live = lax.rem(ref, slot_count) < counts_ref[lax.div(ref, slot_count)]
            target_exp = target_exp * jnp.where(live, 1.0, 0.0).astype(jnp.float32)
            gap = target_exp * teacher
        else:
            scores = all_scores[:, i * TILE : (i + 1) * TILE]
            gap = target_exp * (teacher - scores)
            student_exp = jnp.exp(scores)
            student_sum = student_exp if i == 0 else student_sum + student_exp
        target_sum = target_exp if i == 0 else target_sum + target_exp
        gap_sum = gap if i == 0 else gap_sum + gap
        exps.append(target_exp)
    total = jnp.sum(target_sum.T, axis=0, keepdims=True)
    inverse = 1.0 / total
    base = jnp.sum(gap_sum.T, axis=0, keepdims=True) * inverse - jnp.log(total)
    spread_inverse = jnp.broadcast_to(inverse, (TILE, ABLK)).T
    for i, target_exp in enumerate(exps):
        out, at = (near_rows, i) if i < local_count else (far_rows, i - local_count)
        out[rows, at * TILE : (at + 1) * TILE] = (target_exp * spread_inverse).astype(
            jnp.bfloat16
        )
    return anchors, base, jnp.sum(student_sum.T, axis=0, keepdims=True)


def take_context(block, sub, context, tiles_ref, refs_ref, table_ref, fetched_ref, counts):
    local_count, remote_count = counts
    places = []
    for i in range(local_count):
        place = rows_of(tiles_ref[block * local_count + i])
        context[sub, i * TILE : (i + 1) * TILE, :] = table_ref[place, :]
        places.append(place)
    for i in range(remote_count):
        place = rows_of(refs_ref[block * remote_count + i])
        at = local_count + i
        context[sub, at * TILE : (at + 1) * TILE, :] = fetched_ref[place, :]
        places.append(place)
    return places


def tile_grad(delta, anchors):
    return lax.dot_general(
        delta, anchors, (((0,), (0,)), ((), ())), preferred_element_type=jnp.float32
    )


def score_kernel(
    per_step, remote_count, slot_count, refs_ref, counts_ref,
    fetched_ref, anchors_ref, far_ref, base_ref, partial_ref,
    kl_ref, inverse_ref, delta_ref, remote_grad_ref, remote_acc, context,
):
    @pl.when(pl.program_id(0) == 0)
    def _():
        clear_rows(remote_acc)

    for sub in range(per_step):
        block = pl.program_id(0) * per_step + sub
        rows = slice(sub * ABLK, (sub + 1) * ABLK)
        anchors = anchors_ref[rows, :]
        places = []
        lives = []
        for i in range(remote_count):
            ref = refs_ref[block * remote_count + i]
            places.append(rows_of(ref))
            live = lax.rem(ref, slot_count) < counts_ref[lax.div(ref, slot_count)]
            lives.append(jnp.where(live, 1.0, 0.0).astype(jnp.float32))
            context[sub, i * TILE : (i + 1) * TILE, :] = fetched_ref[places[i], :]
        all_scores = tile_scores(anchors, context[sub])
        student = []
        student_sum = gap_sum = None
        for i in range(remote_count):
            span = slice(i * TILE, (i + 1) * TILE)
            scores = all_scores[:, span]
            student_exp = jnp.exp(scores) * lives[i]
            gap = far_ref[rows, span].astype(jnp.float32) * scores
            student_sum = student_exp if i == 0 else student_sum + student_exp
            gap_sum = gap if i == 0 else gap_sum + gap
            student.append(student_exp)
        total = partial_ref[sub] + jnp.sum(student_sum.T, axis=0, keepdims=True)
        inverse = 1.0 / total
        kl_ref[sub] = base_ref[sub] + jnp.log(total) - jnp.sum(gap_sum.T, axis=0, keepdims=True)
        inverse_ref[sub] = inverse
        spread_inverse = jnp.broadcast_to(inverse, (TILE, ABLK)).T
        for i in range(remote_count):
            span = slice(i * TILE, (i + 1) * TILE)
            delta = (student[i] * spread_inverse - far_ref[rows, span].astype(jnp.float32)).astype(
                jnp.bfloat16
            )
            delta_ref[rows, span] = delta
        grads = tile_grad(delta_ref[rows, :], anchors)
        for i in range(remote_count):
            remote_acc[places[i], :] += grads[i * TILE : (i + 1) * TILE]

    @pl.when(pl.program_id(0) == pl.num_programs(0) - 1)
    def _():
        def finish(index, carry):
            here = rows_of(index, CHUNK)
            remote_grad_ref[here, :] = remote_acc[here, :].astype(jnp.bfloat16)
            return carry

        lax.fori_loop(0, remote_acc.shape[0] // CHUNK, finish, 0)


def score(per_step, remote_refs, own_counts, fetched, prepared, slots):
    anchors, near, far, base, partial = prepared
    blocks, remote_count = remote_refs.shape
    width = anchors.shape[1]
    rows = per_step * ABLK
    pairs = far.shape[0] * far.shape[1]
    row_spec = pl.BlockSpec((per_step, 1, ABLK), lambda b, *_: (b, 0, 0))
    far_spec = pl.BlockSpec((rows, far.shape[1]), lambda b, *_: (b, 0))
    return pl.pallas_call(
        functools.partial(score_kernel, per_step, remote_count, slots),
        out_shape=(
            jax.ShapeDtypeStruct((blocks, 1, ABLK), jnp.float32),
            jax.ShapeDtypeStruct((blocks, 1, ABLK), jnp.float32),
            jax.ShapeDtypeStruct(far.shape, jnp.bfloat16),
            jax.ShapeDtypeStruct(fetched.shape, jnp.bfloat16),
        ),
        grid_spec=pltpu.PrefetchScalarGridSpec(
            num_scalar_prefetch=2,
            grid=(blocks // per_step,),
            in_specs=[
                whole(fetched.shape),
                pl.BlockSpec((rows, width), lambda b, *_: (b, 0)),
                far_spec,
                row_spec,
                row_spec,
            ],
            out_specs=(row_spec, row_spec, far_spec, whole(fetched.shape)),
            scratch_shapes=[
                pltpu.VMEM(fetched.shape, jnp.float32),
                pltpu.VMEM((per_step, far.shape[1], width), jnp.bfloat16),
            ],
        ),
        compiler_params=pltpu.CompilerParams(vmem_limit_bytes=VMEM_LIMIT),
        cost_estimate=cost(3 * pairs * width, 4 * pairs, pairs),
    )(remote_refs.reshape(-1), own_counts, fetched, anchors, far, base, partial)


def local_kernel(
    per_step, local_count, remote_count, lanes, ids_ref, tiles_ref, refs_ref,
    table_ref, fetched_ref, anchors_ref, near_ref, inverse_ref, delta_ref, local_grad_ref,
    context, near_delta, anchor_grad, *row_accs,
):
    scale = SCORE_SCALE / table_ref.shape[1]

    @pl.when(pl.program_id(0) == 0)
    def _():
        clear_rows(local_grad_ref)
        for acc in row_accs:
            clear_rows(acc)

    for sub in range(per_step):
        block = pl.program_id(0) * per_step + sub
        rows = slice(sub * ABLK, (sub + 1) * ABLK)
        places = take_context(
            block, sub, context, tiles_ref, refs_ref, table_ref, fetched_ref,
            (local_count, remote_count),
        )
        anchors = anchors_ref[rows, :]
        spread_inverse = jnp.broadcast_to(inverse_ref[sub], (TILE, ABLK)).T
        near = local_count * TILE
        scores = tile_scores(anchors, context[sub, :near, :])
        for i in range(local_count):
            span = slice(i * TILE, (i + 1) * TILE)
            student = jnp.exp(scores[:, span]) * spread_inverse
            delta = (student - near_ref[rows, span].astype(jnp.float32)).astype(jnp.bfloat16)
            near_delta[rows, span] = delta
        grads = tile_grad(near_delta[rows, :], anchors)
        for i in range(local_count):
            local_grad_ref[places[i], :] += grads[i * TILE : (i + 1) * TILE]
        near_part = jnp.dot(
            near_delta[rows, :], context[sub, :near, :], preferred_element_type=jnp.float32
        )
        far_part = jnp.dot(
            delta_ref[rows, :], context[sub, near:, :], preferred_element_type=jnp.float32
        )
        anchor_grad[rows, :] = (near_part + far_part) * scale
        for row in range(ABLK):
            acc = row_accs[row % lanes]
            at = sub * ABLK + row
            acc[pl.ds(ids_ref[block * ABLK + row], 1), :] += anchor_grad[at : at + 1, :]

    @pl.when(pl.program_id(0) == pl.num_programs(0) - 1)
    def _():
        def finish(index, carry):
            here = rows_of(index, CHUNK)
            total = local_grad_ref[here, :]
            for acc in row_accs:
                total = total + acc[here, :]
            local_grad_ref[here, :] = total
            return carry

        lax.fori_loop(0, local_grad_ref.shape[0] // CHUNK, finish, 0)


def local_grads(
    per_step, anchor_ids, local_tiles, remote_refs, table, fetched, anchors, near, inverse, delta
):
    blocks, local_count = local_tiles.shape
    remote_count = remote_refs.shape[1]
    context_width = near.shape[1] + delta.shape[1]
    width = table.shape[1]
    rows = per_step * ABLK
    lanes = 4 if table.shape[0] <= 8192 else 1
    pairs = delta.shape[0] * context_width
    return pl.pallas_call(
        functools.partial(local_kernel, per_step, local_count, remote_count, lanes),
        out_shape=jax.ShapeDtypeStruct(table.shape, jnp.float32),
        grid_spec=pltpu.PrefetchScalarGridSpec(
            num_scalar_prefetch=3,
            grid=(blocks // per_step,),
            in_specs=[
                whole(table.shape),
                whole(fetched.shape),
                pl.BlockSpec((rows, width), lambda b, *_: (b, 0)),
                pl.BlockSpec((rows, near.shape[1]), lambda b, *_: (b, 0)),
                pl.BlockSpec((per_step, 1, ABLK), lambda b, *_: (b, 0, 0)),
                pl.BlockSpec((rows, delta.shape[1]), lambda b, *_: (b, 0)),
            ],
            out_specs=whole(table.shape),
            scratch_shapes=[
                pltpu.VMEM((per_step, context_width, width), jnp.bfloat16),
                pltpu.VMEM((rows, near.shape[1]), jnp.bfloat16),
                pltpu.VMEM((rows, width), jnp.float32),
            ]
            + [pltpu.VMEM(table.shape, jnp.float32)] * lanes,
        ),
        compiler_params=pltpu.CompilerParams(vmem_limit_bytes=VMEM_LIMIT),
        cost_estimate=cost(3 * pairs * width, 2 * pairs, 0),
    )(
        anchor_ids, local_tiles.reshape(-1), remote_refs.reshape(-1),
        table, fetched, anchors, near, inverse, delta,
    )


def merge_kernel(asked_ref, local_ref, returned_ref, out_ref, acc):
    def load(index, carry):
        here = rows_of(index, CHUNK)
        acc[here, :] = local_ref[here, :]
        return carry

    lax.fori_loop(0, acc.shape[0] // CHUNK, load, 0)

    def add(slot, carry):
        acc[rows_of(asked_ref[slot]), :] += returned_ref[rows_of(slot), :].astype(jnp.float32)
        return carry

    lax.fori_loop(0, returned_ref.shape[0] // TILE, add, 0)

    def store(index, carry):
        here = rows_of(index, CHUNK)
        out_ref[here, :] = acc[here, :].astype(jnp.bfloat16)
        return carry

    lax.fori_loop(0, acc.shape[0] // CHUNK, store, 0)


def merge(asked, local_grad, returned):
    return pl.pallas_call(
        merge_kernel,
        out_shape=jax.ShapeDtypeStruct(local_grad.shape, jnp.bfloat16),
        grid_spec=pltpu.PrefetchScalarGridSpec(
            num_scalar_prefetch=1,
            grid=(1,),
            in_specs=[whole(local_grad.shape), whole(returned.shape)],
            out_specs=whole(local_grad.shape),
            scratch_shapes=[pltpu.VMEM(local_grad.shape, jnp.float32)],
        ),
        compiler_params=pltpu.CompilerParams(vmem_limit_bytes=VMEM_LIMIT),
    )(asked, local_grad, returned)


MESH = pl.DeviceIdType.MESH
ANYWHERE = pl.BlockSpec(memory_space=pl.ANY)
IN_VMEM = pl.BlockSpec(memory_space=pltpu.VMEM)


def greet(partners):
    barrier = pltpu.get_barrier_semaphore()
    for partner in partners:
        pl.semaphore_signal(barrier, inc=1, device_id=partner, device_id_type=MESH)
    pl.semaphore_wait(barrier, len(partners))


def dom_partners(doms):
    group, dom = lax.axis_index("group"), lax.axis_index("dom")
    chips = doms // 2
    chip, core = dom // 2, dom % 2
    other = chip * 2 + (1 - core)
    ahead = [lax.rem(chip + k, chips) * 2 + core for k in range(1, chips)]
    behind = [lax.rem(chip + chips - k, chips) for k in range(1, chips)]
    return group, dom, core, other, ahead, behind


def fetch_kernel(
    groups, doms, chunks, per_step, shapes,
    features_ref, w_in_ref, b_in_ref, w_out_ref, requests_ref, own_asks,
    ids_ref, tiles_ref, refs_ref, counts_ref, teacher_ref,
    table_ref, fetched_ref, embedding_out, asked_ref,
    anchors_ref, near_ref, far_ref, base_ref, partial_ref,
    table, relay, served, blank, ask_out, ask_in, asked,
    table_f, anchor_rows, context, embedding_ref, teacher_buf, near_buf, far_buf, anchor_buf,
    in_sems, near_out_sems, far_out_sems, anchor_out_sems,
    near_sems, far_sems, on_sems, swap_sems, relay_near, relay_far, relay_on,
    ask_sems, serve_sems, relay_serve, own_sems,
):
    group, dom, core, other, ahead, behind = dom_partners(doms)
    half = groups // 2
    slots = requests_ref.shape[1]
    count = features_ref.shape[0]
    part = count // chunks
    step = min(CHUNK, part)
    first = group // half * half
    place = lax.rem(group, half)
    mates = [first + lax.rem(place + k, half) for k in range(1, half)]
    partner = lax.rem(group + half, groups)
    peers = [lax.rem(group + k, groups) for k in range(1, groups)]
    steps = teacher_ref.shape[0] // (per_step * ABLK)
    step_rows = per_step * ABLK

    def teacher_in(index):
        return pltpu.make_async_copy(
            teacher_ref.at[rows_of(index, step_rows), :],
            teacher_buf.at[lax.rem(index, 2)],
            in_sems.at[lax.rem(index, 2)],
        )

    def targets_out(index):
        at = lax.rem(index, 2)
        rows = rows_of(index, step_rows)
        return (
            pltpu.make_async_copy(near_buf.at[at], near_ref.at[rows, :], near_out_sems.at[at]),
            pltpu.make_async_copy(far_buf.at[at], far_ref.at[rows, :], far_out_sems.at[at]),
            pltpu.make_async_copy(
                anchor_buf.at[at], anchors_ref.at[rows, :], anchor_out_sems.at[at]
            ),
        )

    def prepare_step(index, carry):
        at = lax.rem(index, 2)
        teacher_in(index).wait()

        @pl.when(index + 1 < steps)
        def _():
            teacher_in(index + 1).start()

        @pl.when(index >= 2)
        def _():
            for copy in targets_out(index - 2):
                copy.wait()

        for sub in range(per_step):
            block = index * per_step + sub
            anchors, base, partial = prepare_block(
                SCORE_SCALE / table.shape[2], shapes, block, pl.ds(sub * ABLK, ABLK),
                teacher_buf.at[at], ids_ref, tiles_ref, refs_ref, counts_ref,
                table, table_f, anchor_rows.at[sub], context.at[sub], near_buf.at[at],
                far_buf.at[at],
            )
            anchor_buf[at, sub * ABLK : (sub + 1) * ABLK, :] = anchors
            base_ref[block] = base
            partial_ref[block] = partial
        for copy in targets_out(index):
            copy.start()
        return carry

    teacher_in(0).start()
    greet(
        [(group, other)] + [(group, far) for far in ahead]
        + [(peer, dom) for peer in peers]
    )

    tiles = part // TILE

    def span(owner, chunk):
        return pl.ds(owner * (count // TILE) + chunk * tiles, tiles)

    def both(sems, *index):
        return sems[0].at[index], sems[1].at[index]

    def send(src, dst, sems, partner_at):
        copy = pltpu.make_async_remote_copy(
            src_ref=src, dst_ref=dst, send_sem=sems[0], recv_sem=sems[1],
            device_id=partner_at, device_id_type=MESH,
        )
        copy.start()
        return copy

    def spread_chunk(here, owner, chunk, near, far):
        rows = here.at[span(owner, chunk)]
        far_copies = [
            send(rows, rows, both(far, k, chunk), (group, there)) for k, there in enumerate(ahead)
        ]
        return far_copies, send(rows, rows, both(near, chunk), (group, other))

    def pass_on(here, far_copies, chunk, on):
        copies = []
        for k, copy in enumerate(far_copies):
            copy.wait_recv()
            rows = here.at[span(behind[k] * 2 + core, chunk)]
            copies.append(send(rows, rows, both(on, k, chunk), (group, other)))
        return copies

    ask_out[...] = jnp.zeros_like(ask_out)
    ask_out[:, 0:slots] = requests_ref[...]
    asks = [
        send(ask_out, ask_in.at[group], both(ask_sems, k), (peer, dom))
        for k, peer in enumerate(peers)
    ]
    ask_in[group] = ask_out[...]
    blank[...] = jnp.zeros_like(blank)
    sent = []
    far_copies, near_copies, swaps = [], [], []
    for chunk in range(chunks):
        def forward(index, carry):
            at = pl.ds(pl.multiple_of(chunk * part + index * step, step), step)
            embedding, unit_rows = node_rows(
                features_ref[at, :], w_in_ref[...], b_in_ref[...], w_out_ref[...]
            )
            embedding_ref[at, :] = embedding
            to = pl.ds((dom * count + chunk * part) // TILE + index * (step // TILE), step // TILE)
            table[to] = unit_rows.reshape(step // TILE, TILE, unit_rows.shape[1])
            return carry

        lax.fori_loop(0, part // step, forward, 0)
        rows = span(dom, chunk)
        swaps.append(
            send(table.at[rows], relay.at[rows], both(swap_sems, chunk), (partner, dom))
        )
        far, near = spread_chunk(table, dom, chunk, near_sems, far_sems)
        far_copies.append(far)
        near_copies.append(near)
    clear = pltpu.make_async_copy(blank, fetched_ref.at[pl.ds(group * slots, slots)], own_sems.at[0])
    clear.start()
    on_copies, relay_fars, relay_nears, relay_ons = [], [], [], []

    def relay_chunk(chunk):
        swaps[chunk].wait_recv()
        far, near = spread_chunk(relay, dom, chunk, relay_near, relay_far)
        relay_fars.append(far)
        relay_nears.append(near)

    for chunk in range(chunks):
        on_copies += pass_on(table, far_copies[chunk], chunk, on_sems)
    keep_embedding = pltpu.make_async_copy(embedding_ref, embedding_out, own_sems.at[4])
    keep_embedding.start()
    relay_chunk(0)
    relay_chunk(1)
    for copy in asks:
        copy.wait_recv()
    read_asks = pltpu.make_async_copy(ask_in, asked, own_sems.at[1])
    read_asks.start()
    asked_ref[...] = ask_in[...]
    for copy in on_copies + near_copies:
        copy.wait_recv()
    keep = pltpu.make_async_copy(table, table_ref, own_sems.at[2])
    keep.start()
    read_asks.wait()

    def serve(here, base, asked_of):
        for k in range(half - 1):
            source = mates[k]

            def pick(slot, carry):
                wanted = asked[source, asked_of, slot]
                served[base + k, slot] = here[wanted]
                return carry

            lax.fori_loop(0, slots, pick, 0)

    def push_served(base, asked_of, sems):
        return [
            send(
                served.at[base + k], fetched_ref.at[pl.ds(asked_of * slots, slots)], both(sems, k),
                (mate, dom),
            )
            for k, mate in enumerate(mates)
        ]

    serve(table, 0, group)
    sent += push_served(0, group, serve_sems)

    def widen(index, carry):
        table_f[rows_of(index), :] = table[index].astype(jnp.float32)
        return carry

    lax.fori_loop(0, table.shape[0], widen, 0)
    bounds = [steps * part // 8 for part in (0, 1, 3, 4, 8)]

    def prepare(segment):
        lax.fori_loop(bounds[segment], bounds[segment + 1], prepare_step, 0)

    def relay_pass(chunk):
        return pass_on(relay, relay_fars[chunk], chunk, relay_on)

    prepare(0)
    relay_chunk(2)
    relay_ons += relay_pass(0) + relay_pass(1)
    prepare(1)
    relay_chunk(3)
    relay_ons += relay_pass(2)
    prepare(2)
    relay_ons += relay_pass(3)
    for copy in relay_ons + relay_nears:
        copy.wait_recv()
    serve(relay, half - 1, partner)
    sent += push_served(half - 1, partner, relay_serve)

    def pick_own(slot, carry):
        wanted = own_asks[partner, slot]
        served[2 * half - 2, slot] = relay[wanted]
        return carry

    lax.fori_loop(0, slots, pick_own, 0)
    mine = pltpu.make_async_copy(
        served.at[2 * half - 2], fetched_ref.at[pl.ds(partner * slots, slots)], own_sems.at[3]
    )
    mine.start()
    prepare(3)
    for index in range(max(steps - 2, 0), steps):
        for copy in targets_out(index):
            copy.wait()
    for copy in sent:
        copy.wait_recv()
    clear.wait()
    keep.wait()
    keep_embedding.wait()
    mine.wait()
    for copy in asks + swaps + near_copies + on_copies + relay_nears + relay_ons + sent:
        copy.wait_send()
    for copies in far_copies + relay_fars:
        for copy in copies:
            copy.wait_send()


def fetch_tiles(
    per_step, features, w_in, b_in, w_out, own_requests, anchor_ids, local_tiles, remote_refs,
    own_counts, teacher, groups, doms,
):
    slots = own_requests.shape[1]
    count = features.shape[0]
    width = w_out.shape[1]
    chunks = 4
    half = groups // 2
    far, mates = max(doms // 2 - 1, 1), max(half - 1, 1)
    dma = pltpu.SemaphoreType.DMA
    nodes = doms * count
    blocks, remote_count = remote_refs.shape
    local_count = local_tiles.shape[1]
    near, far_width = local_count * TILE, remote_count * TILE
    anchors, context_width = teacher.shape
    rows = per_step * ABLK
    peers = max(groups - 1, 1)
    in_smem = pl.BlockSpec(memory_space=pltpu.SMEM)
    table, fetched, embedding, asked, *prepared = pl.pallas_call(
        functools.partial(
            fetch_kernel, groups, doms, chunks, per_step, (local_count, remote_count, slots)
        ),
        out_shape=(
            jax.ShapeDtypeStruct((nodes // TILE, TILE, width), jnp.bfloat16),
            jax.ShapeDtypeStruct((groups * slots, TILE, width), jnp.bfloat16),
            jax.ShapeDtypeStruct((count, width), jnp.float32),
            jax.ShapeDtypeStruct((groups, groups, 128), jnp.int32),
            jax.ShapeDtypeStruct((anchors, width), jnp.bfloat16),
            jax.ShapeDtypeStruct((anchors, near), jnp.bfloat16),
            jax.ShapeDtypeStruct((anchors, far_width), jnp.bfloat16),
            jax.ShapeDtypeStruct((blocks, 1, ABLK), jnp.float32),
            jax.ShapeDtypeStruct((blocks, 1, ABLK), jnp.float32),
        ),
        in_specs=[IN_VMEM] * 5 + [in_smem] * 5 + [ANYWHERE],
        out_specs=(
            ANYWHERE, ANYWHERE, ANYWHERE, IN_VMEM, ANYWHERE, ANYWHERE, ANYWHERE, IN_VMEM, IN_VMEM
        ),
        scratch_shapes=[
            pltpu.VMEM((nodes // TILE, TILE, width), jnp.bfloat16),
            pltpu.VMEM((nodes // TILE, TILE, width), jnp.bfloat16),
            pltpu.VMEM((2 * half - 1, slots, TILE, width), jnp.bfloat16),
            pltpu.VMEM((slots, TILE, width), jnp.bfloat16),
            pltpu.VMEM((groups, 128), jnp.int32),
            pltpu.VMEM((groups, groups, 128), jnp.int32),
            pltpu.SMEM((groups, groups, 128), jnp.int32),
            pltpu.VMEM((nodes, width), jnp.float32),
            pltpu.VMEM((per_step, ABLK, width), jnp.float32),
            pltpu.VMEM((per_step, near, width), jnp.bfloat16),
            pltpu.VMEM((count, width), jnp.float32),
            pltpu.VMEM((2, rows, context_width), jnp.bfloat16),
            pltpu.VMEM((2, rows, near), jnp.bfloat16),
            pltpu.VMEM((2, rows, far_width), jnp.bfloat16),
            pltpu.VMEM((2, rows, width), jnp.bfloat16),
            dma((2,)),
            dma((2,)),
            dma((2,)),
            dma((2,)),
            [dma((chunks,)), dma((chunks,))],
            [dma((far, chunks)), dma((far, chunks))],
            [dma((far, chunks)), dma((far, chunks))],
            [dma((chunks,)), dma((chunks,))],
            [dma((chunks,)), dma((chunks,))],
            [dma((far, chunks)), dma((far, chunks))],
            [dma((far, chunks)), dma((far, chunks))],
            [dma((peers,)), dma((peers,))],
            [dma((mates,)), dma((mates,))],
            [dma((mates,)), dma((mates,))],
            dma((5,)),
        ],
        compiler_params=pltpu.CompilerParams(
            collective_id=0, has_side_effects=True, vmem_limit_bytes=VMEM_LIMIT
        ),
    )(
        features, w_in, b_in.reshape(1, -1), w_out, own_requests, own_requests,
        anchor_ids, local_tiles.reshape(-1), remote_refs.reshape(-1), own_counts, teacher,
    )
    asked = lax.dynamic_index_in_dim(asked, lax.axis_index("group"), 1, keepdims=False)
    return (
        table.reshape(-1, width), fetched.reshape(-1, width), embedding,
        asked[:, :slots].reshape(-1), prepared,
    )


def finish_kernel(
    groups, doms, chunks, merged_ref, embedding_ref, features_ref, w_in_ref, b_in_ref, w_out_ref,
    node_ref, bias_ref, gathered,
    near_got, far_out, far_got, grad_rows, acc, bias_acc, bias_other, bias_all,
    half_out, half_got, shard_out, shard_got,
    near_sems, far_sems, half_sems, bias_sems, shard_sems, bias_all_sems, gather_sems, pass_sems,
):
    group, dom, core, other, ahead, behind = dom_partners(doms)
    count, width = node_ref.shape
    chips = doms // 2
    chip = dom // 2
    units = groups * chips
    unit = group * chips + chip
    blocks = acc.shape[0] // 2
    shard = shard_got.shape[1]
    part = count // chunks
    step = min(CHUNK, part)
    per_block = acc.shape[1] // shard
    barrier = pltpu.get_barrier_semaphore()

    def at_unit(index):
        return (index // chips, lax.rem(index, chips) * 2 + core)

    def unit_after(k):
        return lax.rem(unit + k + 1, units)

    def unit_before(k):
        return lax.rem(unit + units - k - 1, units)

    def each(start, stop, work):
        def body(k, carry):
            work(k)
            return carry

        lax.fori_loop(start, stop, body, 0)

    def greet_unit(k):
        pl.semaphore_signal(
            barrier, inc=1, device_id=at_unit(unit_after(k)), device_id_type=MESH
        )

    pl.semaphore_signal(barrier, inc=1, device_id=(group, other), device_id_type=MESH)
    each(0, units - 1, greet_unit)
    acc[...] = jnp.zeros_like(acc)
    bias_acc[...] = jnp.zeros_like(bias_acc)
    pl.semaphore_wait(barrier, units)

    def remote(src, dst, sems, index, device):
        return pltpu.make_async_remote_copy(
            src_ref=src, dst_ref=dst, send_sem=sems[0].at[index], recv_sem=sems[1].at[index],
            device_id=device, device_id_type=MESH,
        )

    order = [lax.rem(chip + k, chips) for k in range(1, chips)] + [chip]

    def rows_in(owner, chunk):
        return pl.ds(pl.multiple_of(owner * count + chunk * part, part), part)

    near_copies = {}
    for chunk in range(chunks):
        rows = pl.ds(chunk * part, part)
        for k, to in enumerate(order):
            theirs = merged_ref.at[rows_in(to * 2 + (1 - core), chunk), :]
            copy = remote(
                theirs, near_got.at[k, rows, :], near_sems, (k, chunk), (group, other)
            )
            copy.start()
            near_copies[k, chunk] = copy
    far_copies = {}
    for chunk in range(chunks):
        rows = pl.ds(chunk * part, part)
        for k in range(chips - 1):
            near_copies[k, chunk].wait_recv()
            total = merged_ref[rows_in(order[k] * 2 + core, chunk), :].astype(jnp.float32)
            total = total + near_got[k, rows, :].astype(jnp.float32)
            far_out[k, rows, :] = total.astype(jnp.bfloat16)
            copy = remote(
                far_out.at[k, rows, :], far_got.at[k, rows, :], far_sems, (k, chunk),
                (group, ahead[k]),
            )
            copy.start()
            far_copies[k, chunk] = copy

    def backward(base, hidden_half):
        here = pl.ds(base, step)
        span = blocks * 128
        lanes = pl.ds(pl.multiple_of(hidden_half * span, span), span)
        features = features_ref[here, :]
        grads = grad_rows[here, :]
        pre_act = (
            jnp.dot(features, w_in_ref[:, lanes], preferred_element_type=jnp.float32)
            + b_in_ref[:, lanes]
        )
        sigmoid_pre = jax.nn.sigmoid(pre_act)
        hidden = (pre_act * sigmoid_pre).astype(jnp.bfloat16)
        out_grad = tile_grad(grads, hidden)
        hidden_grad = tile_scores(grads, w_out_ref[lanes, :])
        pre_grad = hidden_grad * sigmoid_pre * (1.0 + pre_act * (1.0 - sigmoid_pre))
        bias = jnp.sum(pre_grad, axis=0, keepdims=True)
        in_grad = tile_grad(features, pre_grad.astype(jnp.bfloat16))
        for b in range(blocks):
            cols = slice(b * 128, (b + 1) * 128)
            at = hidden_half * blocks + b
            acc[at, 0:width, :] += in_grad[:, cols]
            acc[at, width : 2 * width, :] += out_grad[:, cols]
            bias_acc[pl.ds(at, 1), :] += bias[:, cols]

    half_copy = remote(half_out, half_got, half_sems, 0, (group, other))
    bias_copy = remote(bias_acc, bias_other, bias_sems, 0, (group, other))
    for chunk in range(chunks):
        rows = pl.ds(chunk * part, part)
        near_copies[chips - 1, chunk].wait_recv()
        total = merged_ref[rows_in(dom, chunk), :].astype(jnp.float32)
        total = total + near_got[chips - 1, rows, :].astype(jnp.float32)
        for k in range(chips - 1):
            far_copies[k, chunk].wait_recv()
            total = total + far_got[k, rows, :].astype(jnp.float32)
        node_ref[rows, :] = total
        embedding = embedding_ref[rows, :]
        spread = jnp.sqrt(jnp.mean(embedding * embedding, axis=1, keepdims=True) + EPSILON)
        normed = embedding / spread
        grads = (total - normed * jnp.mean(total * normed, axis=1, keepdims=True)) / spread
        grad_rows[rows, :] = grads.astype(jnp.bfloat16)
        for side in (1 - core, core):
            each(0, part // step, lambda k: backward(chunk * part + k * step, side))
            if chunk == chunks - 1 and side is not core:
                for b in range(blocks):
                    half_out[b] = acc[side * blocks + b].astype(jnp.bfloat16)
                half_copy.start()
    bias_copy.start()
    half_copy.wait_recv()

    def shard_at(index):
        block = index // per_block
        row = pl.ds(pl.multiple_of(lax.rem(index, per_block) * shard, shard), shard)
        mine = acc[core * blocks + block, row, :]
        return mine + half_got[block, row, :].astype(jnp.float32)

    def shard_copy(k):
        return remote(
            shard_out.at[k], shard_got.at[k], shard_sems, k, at_unit(unit_after(k))
        )

    def bias_all_copy(k):
        rows = bias_all.at[unit]
        return remote(rows, rows, bias_all_sems, k, at_unit(unit_after(k)))

    def gather_copy(k):
        rows = gathered.at[core, unit]
        return remote(rows, rows, gather_sems, k, at_unit(unit_after(k)))

    def pass_copy(k):
        rows = gathered.at[core, unit_before(k)]
        return remote(rows, rows, pass_sems, k, (group, other))

    def send_shard(k):
        shard_out[k] = shard_at(unit_after(k)).astype(jnp.bfloat16)
        shard_copy(k).start()

    each(0, units - 1, send_shard)
    bias_copy.wait_recv()
    bias_all[unit] = bias_acc[...] + bias_other[...]
    each(0, units - 1, lambda k: bias_all_copy(k).start())

    def add_shard(k, total):
        shard_copy(k).wait_recv()
        return total + shard_got[k].astype(jnp.float32)

    total = lax.fori_loop(0, units - 1, add_shard, shard_at(unit))
    scale = 1.0 / (groups * doms)
    gathered[core, unit] = (total * scale).astype(jnp.bfloat16)
    each(0, units - 1, lambda k: gather_copy(k).start())
    pass_copy(units - 1).start()

    def pass_on(k):
        gather_copy(k).wait_recv()
        pass_copy(k).start()

    each(0, units - 1, lambda k: bias_all_copy(k).wait_recv())
    bias_ref[...] = lax.fori_loop(
        1, units, lambda k, total: total + bias_all[k], bias_all[0]
    ) * scale
    each(0, units - 1, pass_on)

    each(0, units, lambda k: pass_copy(k).wait_recv())
    for copy in list(near_copies.values()) + list(far_copies.values()) + [half_copy, bias_copy]:
        copy.wait_send()

    def drain(k):
        shard_copy(k).wait_send()
        bias_all_copy(k).wait_send()
        gather_copy(k).wait_send()
        pass_copy(k).wait_send()

    each(0, units - 1, drain)
    pass_copy(units - 1).wait_send()


def lay_out_kernel(node_ref, bias_ref, gathered_ref, node_out, in_out, bias_out, out_out):
    width = out_out.shape[1]
    node_out[...] = node_ref[...]
    for b in range(gathered_ref.shape[0]):
        rows = gathered_ref[b].astype(jnp.float32)
        in_out[:, b * 128 : (b + 1) * 128] = rows[0:width]
        out_out[b * 128 : (b + 1) * 128, :] = rows[width : 2 * width].T

    @pl.when(pl.program_id(0) == 0)
    def _():
        for b in range(bias_ref.shape[0]):
            bias_out[b * 128 : (b + 1) * 128] = bias_ref[b, :]


def lay_out(node_grad, bias, gathered):
    count, width = node_grad.shape
    blocks = bias.shape[0]
    return pl.pallas_call(
        lay_out_kernel,
        out_shape=(
            jax.ShapeDtypeStruct((count, width), jnp.float32),
            jax.ShapeDtypeStruct((width, blocks * 128), jnp.float32),
            jax.ShapeDtypeStruct((blocks * 128,), jnp.float32),
            jax.ShapeDtypeStruct((blocks * 128, width), jnp.float32),
        ),
        grid=(LAY_STEPS,),
        in_specs=[
            pl.BlockSpec((count // LAY_STEPS, width), lambda b: (b, 0)),
            whole(bias.shape),
            pl.BlockSpec((blocks // LAY_STEPS, 2 * width, 128), lambda b: (b, 0, 0)),
        ],
        out_specs=(
            pl.BlockSpec((count // LAY_STEPS, width), lambda b: (b, 0)),
            pl.BlockSpec((width, 128 * blocks // LAY_STEPS), lambda b: (0, b)),
            whole((blocks * 128,)),
            pl.BlockSpec((128 * blocks // LAY_STEPS, width), lambda b: (b, 0)),
        ),
    )(node_grad, bias, gathered)


def finish(merged, embedding, features, w_in, b_in, w_out, groups, doms):
    count, width = embedding.shape
    hid = w_out.shape[0]
    chips = doms // 2
    units = groups * chips
    chunks = 4
    blocks = hid // 128
    shard = hid * 2 * width // (2 * 128) // units
    far = max(chips - 1, 1)
    half = jnp.bfloat16
    dma = pltpu.SemaphoreType.DMA

    def pair(*shape):
        return [dma(shape), dma(shape)]

    node_grad, bias, gathered = pl.pallas_call(
        functools.partial(finish_kernel, groups, doms, chunks),
        out_shape=(
            jax.ShapeDtypeStruct((count, width), jnp.float32),
            jax.ShapeDtypeStruct((blocks, 128), jnp.float32),
            jax.ShapeDtypeStruct((2, units, shard, 128), half),
        ),
        in_specs=[IN_VMEM] * 6,
        out_specs=(IN_VMEM,) * 3,
        scratch_shapes=[
            pltpu.VMEM((chips, count, width), half),
            pltpu.VMEM((far, count, width), half),
            pltpu.VMEM((far, count, width), half),
            pltpu.VMEM((count, width), half),
            pltpu.VMEM((blocks, 2 * width, 128), jnp.float32),
            pltpu.VMEM((blocks, 128), jnp.float32),
            pltpu.VMEM((blocks, 128), jnp.float32),
            pltpu.VMEM((units, blocks, 128), jnp.float32),
            pltpu.VMEM((blocks // 2, 2 * width, 128), half),
            pltpu.VMEM((blocks // 2, 2 * width, 128), half),
            pltpu.VMEM((units - 1, shard, 128), half),
            pltpu.VMEM((units - 1, shard, 128), half),
            pair(chips, chunks),
            pair(far, chunks),
            pair(1),
            pair(1),
            pair(units - 1),
            pair(units - 1),
            pair(units - 1),
            pair(units),
        ],
        compiler_params=pltpu.CompilerParams(
            collective_id=1, has_side_effects=True, vmem_limit_bytes=VMEM_LIMIT
        ),
    )(merged, embedding, features, w_in, b_in.reshape(1, -1), w_out)
    return lay_out(node_grad, bias, gathered.reshape(blocks, 2 * width, 128))


def shards(
    features, w_in, b_in, w_out, anchor_ids, local_tiles, requests, counts, remote_refs, teacher
):
    groups = lax.axis_size("group")
    doms = lax.axis_size("dom")
    devices = groups * doms
    own_requests = requests[0, 0]
    own_counts = counts[0, 0]
    slot_count = own_requests.shape[1]
    per_step = math.gcd(local_tiles.shape[0], 4)
    table, fetched, embedding, asked, prepared = fetch_tiles(
        per_step, features, w_in, b_in, w_out, own_requests, anchor_ids, local_tiles,
        remote_refs, own_counts, teacher, groups, doms,
    )
    anchor_kl, inverse, delta, remote_grad = score(
        math.gcd(local_tiles.shape[0], 8), remote_refs, own_counts, fetched, prepared, slot_count
    )
    anchor_kl = anchor_kl.reshape(-1)
    returned = lax.all_to_all(remote_grad, "group", split_axis=0, concat_axis=0, tiled=True)
    local_grad = local_grads(
        per_step, anchor_ids, local_tiles, remote_refs, table, fetched, prepared[0], prepared[1],
        inverse, delta,
    )
    merged = merge(asked, local_grad, returned)
    node_grad, in_grad, bias_grad, out_grad = finish(
        merged, embedding, features, w_in, b_in, w_out, groups, doms
    )
    return anchor_kl, node_grad, in_grad, bias_grad, out_grad


def solution(mesh):
    return jax.shard_map(
        shards,
        mesh=mesh,
        in_specs=(
            P(("group", "dom"), None),
            P(),
            P(),
            P(),
            P(("group", "dom")),
            P(("group", "dom"), None),
            P("group", "dom", None, None),
            P("group", "dom", None),
            P(("group", "dom"), None),
            P(("group", "dom"), None),
        ),
        out_specs=(P(("group", "dom")), P(("group", "dom"), None), P(), P(), P()),
        check_vma=False,
    )
```

```python
import functools
import math

import jax
import jax.numpy as jnp
from jax import lax
from jax.experimental import pallas as pl
from jax.experimental.pallas import tpu as pltpu
from jax.sharding import PartitionSpec as P

TILE = 128
ABLK = 128

SCORE_SCALE = 8.0
EPSILON = 1e-06
VMEM_LIMIT = 60 * 1024 * 1024
CHUNK = 256
LAY_STEPS = 2

ONE_COPY = pl.Buffered(1)


def whole(shape):
    return pl.BlockSpec(shape, lambda *_: (0,) * len(shape), pipeline_mode=ONE_COPY)


def node_rows(feature_rows, w_in, b_in, w_out):
    pre_act = jnp.dot(feature_rows, w_in, preferred_element_type=jnp.float32) + b_in
    hidden = (pre_act * jax.nn.sigmoid(pre_act)).astype(jnp.bfloat16)
    embedding = jnp.dot(hidden, w_out, preferred_element_type=jnp.float32)
    spread = jnp.sqrt(jnp.mean(embedding * embedding, axis=1, keepdims=True) + EPSILON)
    return embedding, (embedding / spread).astype(jnp.bfloat16)


def rows_of(index, count=TILE):
    return pl.ds(pl.multiple_of(index * count, count), count)


def cost(flops, moved, powers):
    return pl.CostEstimate(flops=flops, bytes_accessed=moved, transcendentals=powers)


def clear_rows(ref):
    zero_chunk = jnp.zeros((CHUNK, ref.shape[1]), ref.dtype)

    def clear(index, carry):
        ref[rows_of(index, CHUNK), :] = zero_chunk
        return carry

    lax.fori_loop(0, ref.shape[0] // CHUNK, clear, 0)


def tile_scores(anchors, context):
    return lax.dot_general(
        anchors, context, (((1,), (1,)), ((), ())), preferred_element_type=jnp.float32
    )


def prepare_block(
    scale, shapes, block, rows, teacher_rows, ids_ref, tiles_ref, refs_ref, counts_ref,
    table, table_f, anchor_rows, context, near_rows, far_rows,
):
    local_count, remote_count, slot_count = shapes

    def gather(index, carry):
        for lane in range(16):
            row = index * 16 + lane
            anchor_rows[row, :] = table_f[ids_ref[block * ABLK + row], :]
        return carry

    lax.fori_loop(0, ABLK // 16, gather, 0)
    anchors = (anchor_rows[...] * scale).astype(jnp.bfloat16)
    for i in range(local_count):
        context[i * TILE : (i + 1) * TILE, :] = table[tiles_ref[block, i]]
    all_scores = tile_scores(anchors, context[...])
    target_sum = gap_sum = student_sum = None
    exps = []
    for i in range(local_count + remote_count):
        teacher = teacher_rows[rows, i * TILE : (i + 1) * TILE].astype(jnp.float32)
        target_exp = jnp.exp(teacher)
        if i >= local_count:
            ref = refs_ref[block, i - local_count]
            live = lax.rem(ref, slot_count) < counts_ref[lax.div(ref, slot_count)]
            target_exp = target_exp * jnp.where(live, 1.0, 0.0).astype(jnp.float32)
            gap = target_exp * teacher
        else:
            scores = all_scores[:, i * TILE : (i + 1) * TILE]
            gap = target_exp * (teacher - scores)
            student_exp = jnp.exp(scores)
            student_sum = student_exp if i == 0 else student_sum + student_exp
        target_sum = target_exp if i == 0 else target_sum + target_exp
        gap_sum = gap if i == 0 else gap_sum + gap
        exps.append(target_exp)
    total = jnp.sum(target_sum.T, axis=0, keepdims=True)
    inverse = 1.0 / total
    base = jnp.sum(gap_sum.T, axis=0, keepdims=True) * inverse - jnp.log(total)
    spread_inverse = jnp.broadcast_to(inverse, (TILE, ABLK)).T
    for i, target_exp in enumerate(exps):
        out, at = (near_rows, i) if i < local_count else (far_rows, i - local_count)
        out[rows, at * TILE : (at + 1) * TILE] = (target_exp * spread_inverse).astype(
            jnp.bfloat16
        )
    return anchors, base, jnp.sum(student_sum.T, axis=0, keepdims=True)


def take_context(block, sub, context, tiles_ref, refs_ref, table_ref, fetched_ref, counts):
    local_count, remote_count = counts
    places = []
    for i in range(local_count):
        place = rows_of(tiles_ref[block, i])
        context[sub, i * TILE : (i + 1) * TILE, :] = table_ref[place, :]
        places.append(place)
    for i in range(remote_count):
        place = rows_of(refs_ref[block, i])
        at = local_count + i
        context[sub, at * TILE : (at + 1) * TILE, :] = fetched_ref[place, :]
        places.append(place)
    return places


def tile_grad(delta, anchors):
    return lax.dot_general(
        delta, anchors, (((0,), (0,)), ((), ())), preferred_element_type=jnp.float32
    )


def score_kernel(
    per_step, remote_count, slot_count, refs_ref, counts_ref,
    fetched_ref, anchors_ref, far_ref, base_ref, partial_ref,
    kl_ref, inverse_ref, delta_ref, remote_grad_ref, remote_acc, context,
):
    @pl.when(pl.program_id(0) == 0)
    def _():
        clear_rows(remote_acc)

    for sub in range(per_step):
        block = pl.program_id(0) * per_step + sub
        rows = slice(sub * ABLK, (sub + 1) * ABLK)
        anchors = anchors_ref[rows, :]
        places = []
        lives = []
        for i in range(remote_count):
            ref = refs_ref[block, i]
            places.append(rows_of(ref))
            live = lax.rem(ref, slot_count) < counts_ref[lax.div(ref, slot_count)]
            lives.append(jnp.where(live, 1.0, 0.0).astype(jnp.float32))
            context[sub, i * TILE : (i + 1) * TILE, :] = fetched_ref[places[i], :]
        all_scores = tile_scores(anchors, context[sub])
        student = []
        student_sum = gap_sum = None
        for i in range(remote_count):
            span = slice(i * TILE, (i + 1) * TILE)
            scores = all_scores[:, span]
            student_exp = jnp.exp(scores) * lives[i]
            gap = far_ref[rows, span].astype(jnp.float32) * scores
            student_sum = student_exp if i == 0 else student_sum + student_exp
            gap_sum = gap if i == 0 else gap_sum + gap
            student.append(student_exp)
        total = partial_ref[sub] + jnp.sum(student_sum.T, axis=0, keepdims=True)
        inverse = 1.0 / total
        kl_ref[sub] = base_ref[sub] + jnp.log(total) - jnp.sum(gap_sum.T, axis=0, keepdims=True)
        inverse_ref[sub] = inverse
        spread_inverse = jnp.broadcast_to(inverse, (TILE, ABLK)).T
        for i in range(remote_count):
            span = slice(i * TILE, (i + 1) * TILE)
            delta = (student[i] * spread_inverse - far_ref[rows, span].astype(jnp.float32)).astype(
                jnp.bfloat16
            )
            delta_ref[rows, span] = delta
        grads = tile_grad(delta_ref[rows, :], anchors)
        for i in range(remote_count):
            remote_acc[places[i], :] += grads[i * TILE : (i + 1) * TILE]

    @pl.when(pl.program_id(0) == pl.num_programs(0) - 1)
    def _():
        def finish(index, carry):
            here = rows_of(index, CHUNK)
            remote_grad_ref[here, :] = remote_acc[here, :].astype(jnp.bfloat16)
            return carry

        lax.fori_loop(0, remote_acc.shape[0] // CHUNK, finish, 0)


def score(per_step, remote_refs, own_counts, fetched, prepared, slots):
    anchors, near, far, base, partial = prepared
    blocks, remote_count = remote_refs.shape
    width = anchors.shape[1]
    rows = per_step * ABLK
    pairs = far.shape[0] * far.shape[1]
    row_spec = pl.BlockSpec((per_step, 1, ABLK), lambda b, *_: (b, 0, 0))
    far_spec = pl.BlockSpec((rows, far.shape[1]), lambda b, *_: (b, 0))
    return pl.pallas_call(
        functools.partial(score_kernel, per_step, remote_count, slots),
        out_shape=(
            jax.ShapeDtypeStruct((blocks, 1, ABLK), jnp.float32),
            jax.ShapeDtypeStruct((blocks, 1, ABLK), jnp.float32),
            jax.ShapeDtypeStruct(far.shape, jnp.bfloat16),
            jax.ShapeDtypeStruct(fetched.shape, jnp.bfloat16),
        ),
        grid_spec=pltpu.PrefetchScalarGridSpec(
            num_scalar_prefetch=2,
            grid=(blocks // per_step,),
            in_specs=[
                whole(fetched.shape),
                pl.BlockSpec((rows, width), lambda b, *_: (b, 0)),
                far_spec,
                row_spec,
                row_spec,
            ],
            out_specs=(row_spec, row_spec, far_spec, whole(fetched.shape)),
            scratch_shapes=[
                pltpu.VMEM(fetched.shape, jnp.float32),
                pltpu.VMEM((per_step, far.shape[1], width), jnp.bfloat16),
            ],
        ),
        compiler_params=pltpu.CompilerParams(vmem_limit_bytes=VMEM_LIMIT),
        cost_estimate=cost(3 * pairs * width, 4 * pairs, pairs),
    )(remote_refs, own_counts, fetched, anchors, far, base, partial)


def local_kernel(
    per_step, local_count, remote_count, lanes, ids_ref, tiles_ref, refs_ref,
    table_ref, fetched_ref, anchors_ref, near_ref, inverse_ref, delta_ref, local_grad_ref,
    context, near_delta, anchor_grad, *row_accs,
):
    scale = SCORE_SCALE / table_ref.shape[1]

    @pl.when(pl.program_id(0) == 0)
    def _():
        clear_rows(local_grad_ref)
        for acc in row_accs:
            clear_rows(acc)

    for sub in range(per_step):
        block = pl.program_id(0) * per_step + sub
        rows = slice(sub * ABLK, (sub + 1) * ABLK)
        places = take_context(
            block, sub, context, tiles_ref, refs_ref, table_ref, fetched_ref,
            (local_count, remote_count),
        )
        anchors = anchors_ref[rows, :]
        spread_inverse = jnp.broadcast_to(inverse_ref[sub], (TILE, ABLK)).T
        near = local_count * TILE
        scores = tile_scores(anchors, context[sub, :near, :])
        for i in range(local_count):
            span = slice(i * TILE, (i + 1) * TILE)
            student = jnp.exp(scores[:, span]) * spread_inverse
            delta = (student - near_ref[rows, span].astype(jnp.float32)).astype(jnp.bfloat16)
            near_delta[rows, span] = delta
        grads = tile_grad(near_delta[rows, :], anchors)
        for i in range(local_count):
            local_grad_ref[places[i], :] += grads[i * TILE : (i + 1) * TILE]
        near_part = jnp.dot(
            near_delta[rows, :], context[sub, :near, :], preferred_element_type=jnp.float32
        )
        far_part = jnp.dot(
            delta_ref[rows, :], context[sub, near:, :], preferred_element_type=jnp.float32
        )
        anchor_grad[rows, :] = (near_part + far_part) * scale
        for row in range(ABLK):
            acc = row_accs[row % lanes]
            at = sub * ABLK + row
            acc[pl.ds(ids_ref[block * ABLK + row], 1), :] += anchor_grad[at : at + 1, :]

    @pl.when(pl.program_id(0) == pl.num_programs(0) - 1)
    def _():
        def finish(index, carry):
            here = rows_of(index, CHUNK)
            total = local_grad_ref[here, :]
            for acc in row_accs:
                total = total + acc[here, :]
            local_grad_ref[here, :] = total
            return carry

        lax.fori_loop(0, local_grad_ref.shape[0] // CHUNK, finish, 0)


def local_grads(
    per_step, anchor_ids, local_tiles, remote_refs, table, fetched, anchors, near, inverse, delta
):
    blocks, local_count = local_tiles.shape
    remote_count = remote_refs.shape[1]
    context_width = near.shape[1] + delta.shape[1]
    width = table.shape[1]
    rows = per_step * ABLK
    lanes = 4 if table.shape[0] <= 8192 else 1
    pairs = delta.shape[0] * context_width
    return pl.pallas_call(
        functools.partial(local_kernel, per_step, local_count, remote_count, lanes),
        out_shape=jax.ShapeDtypeStruct(table.shape, jnp.float32),
        grid_spec=pltpu.PrefetchScalarGridSpec(
            num_scalar_prefetch=3,
            grid=(blocks // per_step,),
            in_specs=[
                whole(table.shape),
                whole(fetched.shape),
                pl.BlockSpec((rows, width), lambda b, *_: (b, 0)),
                pl.BlockSpec((rows, near.shape[1]), lambda b, *_: (b, 0)),
                pl.BlockSpec((per_step, 1, ABLK), lambda b, *_: (b, 0, 0)),
                pl.BlockSpec((rows, delta.shape[1]), lambda b, *_: (b, 0)),
            ],
            out_specs=whole(table.shape),
            scratch_shapes=[
                pltpu.VMEM((per_step, context_width, width), jnp.bfloat16),
                pltpu.VMEM((rows, near.shape[1]), jnp.bfloat16),
                pltpu.VMEM((rows, width), jnp.float32),
            ]
            + [pltpu.VMEM(table.shape, jnp.float32)] * lanes,
        ),
        compiler_params=pltpu.CompilerParams(vmem_limit_bytes=VMEM_LIMIT),
        cost_estimate=cost(3 * pairs * width, 2 * pairs, 0),
    )(
        anchor_ids, local_tiles, remote_refs,
        table, fetched, anchors, near, inverse, delta,
    )


def merge_kernel(
    pieces, asked_ref, local_ref, returned_ref, out_ref,
    acc, returned, merged, local_sems, returned_sems, out_sems,
):
    def copies(src, dst, sems):
        count = src.shape[0] // pieces
        return [
            pltpu.make_async_copy(
                src.at[pl.ds(c * count, count)], dst.at[pl.ds(c * count, count)], sems.at[c]
            )
            for c in range(pieces)
        ]

    local_in = copies(local_ref, acc, local_sems)
    returned_in = copies(returned_ref, returned, returned_sems)
    merged_out = copies(merged, out_ref, out_sems)
    for copy in returned_in + local_in:
        copy.start()
    for copy in local_in:
        copy.wait()
    slots = returned.shape[0] // pieces
    for c in range(pieces):
        returned_in[c].wait()

        def add(index, carry):
            slot = c * slots + index
            acc[asked_ref[slot]] += returned[slot].astype(jnp.float32)
            return carry

        lax.fori_loop(0, slots, add, 0, unroll=4)
    tiles = acc.shape[0] // pieces
    for c in range(pieces):
        def narrow(index, carry):
            here = pl.ds(c * tiles + index * 4, 4)
            merged[here] = acc[here].astype(jnp.bfloat16)
            return carry

        lax.fori_loop(0, tiles // 4, narrow, 0)
        merged_out[c].start()
    for copy in merged_out:
        copy.wait()


def merge(asked, local_grad, returned):
    pieces = 4
    rows, width = local_grad.shape
    local_grad = local_grad.reshape(-1, TILE, width)
    returned = returned.reshape(-1, TILE, width)
    dma = pltpu.SemaphoreType.DMA
    return pl.pallas_call(
        functools.partial(merge_kernel, pieces),
        out_shape=jax.ShapeDtypeStruct(local_grad.shape, jnp.bfloat16),
        in_specs=[pl.BlockSpec(memory_space=pltpu.SMEM), ANYWHERE, ANYWHERE],
        out_specs=ANYWHERE,
        scratch_shapes=[
            pltpu.VMEM(local_grad.shape, jnp.float32),
            pltpu.VMEM(returned.shape, jnp.bfloat16),
            pltpu.VMEM(local_grad.shape, jnp.bfloat16),
            dma((pieces,)),
            dma((pieces,)),
            dma((pieces,)),
        ],
        compiler_params=pltpu.CompilerParams(vmem_limit_bytes=VMEM_LIMIT + 3 * 1024 * 1024),
    )(asked, local_grad, returned).reshape(rows, width)


MESH = pl.DeviceIdType.MESH
ANYWHERE = pl.BlockSpec(memory_space=pl.ANY)
IN_VMEM = pl.BlockSpec(memory_space=pltpu.VMEM)


def greet(partners):
    barrier = pltpu.get_barrier_semaphore()
    for partner in partners:
        pl.semaphore_signal(barrier, inc=1, device_id=partner, device_id_type=MESH)
    pl.semaphore_wait(barrier, len(partners))


def dom_partners(doms):
    group, dom = lax.axis_index("group"), lax.axis_index("dom")
    chips = doms // 2
    chip, core = dom // 2, dom % 2
    other = chip * 2 + (1 - core)
    ahead = [lax.rem(chip + k, chips) * 2 + core for k in range(1, chips)]
    behind = [lax.rem(chip + chips - k, chips) for k in range(1, chips)]
    return group, dom, core, other, ahead, behind


def fetch_kernel(
    groups, doms, chunks, per_step, shapes,
    features_in, w_in_in, b_in_ref, w_out_in, requests_ref, own_asks,
    ids_ref, tiles_ref, refs_ref, counts_ref, teacher_ref,
    table_ref, fetched_ref, embedding_out, asked_ref,
    anchors_ref, near_ref, far_ref, base_ref, partial_ref,
    table, relay, served, blank, ask_out, ask_in, asked,
    features_ref, w_in_ref, w_out_ref, read_sems,
    table_f, anchor_rows, context, embedding_ref, teacher_buf, near_buf, far_buf, anchor_buf,
    in_sems, near_out_sems, far_out_sems, anchor_out_sems,
    near_sems, far_sems, on_sems, swap_sems, relay_near, relay_far, relay_on,
    ask_sems, serve_sems, relay_serve, own_sems,
):
    group, dom, core, other, ahead, behind = dom_partners(doms)
    half = groups // 2
    slots = requests_ref.shape[1]
    count = features_in.shape[0]
    part = count // chunks
    step = min(CHUNK, part)
    first = group // half * half
    place = lax.rem(group, half)
    mates = [first + lax.rem(place + k, half) for k in range(1, half)]
    partner = lax.rem(group + half, groups)
    peers = [lax.rem(group + k, groups) for k in range(1, groups)]
    steps = teacher_ref.shape[0] // (per_step * ABLK)
    step_rows = per_step * ABLK

    def teacher_in(index):
        return pltpu.make_async_copy(
            teacher_ref.at[rows_of(index, step_rows), :],
            teacher_buf.at[lax.rem(index, 2)],
            in_sems.at[lax.rem(index, 2)],
        )

    def targets_out(index):
        at = lax.rem(index, 2)
        rows = rows_of(index, step_rows)
        return (
            pltpu.make_async_copy(near_buf.at[at], near_ref.at[rows, :], near_out_sems.at[at]),
            pltpu.make_async_copy(far_buf.at[at], far_ref.at[rows, :], far_out_sems.at[at]),
            pltpu.make_async_copy(
                anchor_buf.at[at], anchors_ref.at[rows, :], anchor_out_sems.at[at]
            ),
        )

    def prepare_step(index, carry):
        at = lax.rem(index, 2)
        teacher_in(index).wait()

        @pl.when(index + 1 < steps)
        def _():
            teacher_in(index + 1).start()

        @pl.when(index >= 2)
        def _():
            for copy in targets_out(index - 2):
                copy.wait()

        for sub in range(per_step):
            block = index * per_step + sub
            anchors, base, partial = prepare_block(
                SCORE_SCALE / table.shape[2], shapes, block, pl.ds(sub * ABLK, ABLK),
                teacher_buf.at[at], ids_ref, tiles_ref, refs_ref, counts_ref,
                table, table_f, anchor_rows.at[sub], context.at[sub], near_buf.at[at],
                far_buf.at[at],
            )
            anchor_buf[at, sub * ABLK : (sub + 1) * ABLK, :] = anchors
            base_ref[block] = base
            partial_ref[block] = partial
        for copy in targets_out(index):
            copy.start()
        return carry

    reads = [
        pltpu.make_async_copy(src, dst, read_sems.at[k])
        for k, (src, dst) in enumerate(
            [(features_in, features_ref), (w_in_in, w_in_ref), (w_out_in, w_out_ref)]
        )
    ]
    for copy in reads:
        copy.start()
    teacher_in(0).start()
    greet(
        [(group, other)] + [(group, far) for far in ahead]
        + [(peer, dom) for peer in peers]
    )

    tiles = part // TILE

    def span(owner, chunk):
        return pl.ds(owner * (count // TILE) + chunk * tiles, tiles)

    def both(sems, *index):
        return sems[0].at[index], sems[1].at[index]

    def send(src, dst, sems, partner_at):
        copy = pltpu.make_async_remote_copy(
            src_ref=src, dst_ref=dst, send_sem=sems[0], recv_sem=sems[1],
            device_id=partner_at, device_id_type=MESH,
        )
        copy.start()
        return copy

    def spread_chunk(here, owner, chunk, near, far):
        rows = here.at[span(owner, chunk)]
        far_copies = [
            send(rows, rows, both(far, k, chunk), (group, there)) for k, there in enumerate(ahead)
        ]
        return far_copies, send(rows, rows, both(near, chunk), (group, other))

    def pass_on(here, far_copies, chunk, on):
        copies = []
        for k, copy in enumerate(far_copies):
            copy.wait_recv()
            rows = here.at[span(behind[k] * 2 + core, chunk)]
            copies.append(send(rows, rows, both(on, k, chunk), (group, other)))
        return copies

    ask_out[...] = jnp.zeros_like(ask_out)
    ask_out[:, 0:slots] = requests_ref[...]
    asks = [
        send(ask_out, ask_in.at[group], both(ask_sems, k), (peer, dom))
        for k, peer in enumerate(peers)
    ]
    ask_in[group] = ask_out[...]
    blank[...] = jnp.zeros_like(blank)
    sent = []
    far_copies, near_copies, swaps = [], [], []
    for copy in reads:
        copy.wait()
    for chunk in range(chunks):
        def forward(index, carry):
            at = pl.ds(pl.multiple_of(chunk * part + index * step, step), step)
            embedding, unit_rows = node_rows(
                features_ref[at, :], w_in_ref[...], b_in_ref[...], w_out_ref[...]
            )
            embedding_ref[at, :] = embedding
            to = pl.ds((dom * count + chunk * part) // TILE + index * (step // TILE), step // TILE)
            table[to] = unit_rows.reshape(step // TILE, TILE, unit_rows.shape[1])
            return carry

        lax.fori_loop(0, part // step, forward, 0)
        rows = span(dom, chunk)
        swaps.append(
            send(table.at[rows], relay.at[rows], both(swap_sems, chunk), (partner, dom))
        )
        far, near = spread_chunk(table, dom, chunk, near_sems, far_sems)
        far_copies.append(far)
        near_copies.append(near)
    clear = pltpu.make_async_copy(blank, fetched_ref.at[pl.ds(group * slots, slots)], own_sems.at[0])
    clear.start()
    on_copies, relay_fars, relay_nears, relay_ons = [], [], [], []

    def relay_chunk(chunk):
        swaps[chunk].wait_recv()
        far, near = spread_chunk(relay, dom, chunk, relay_near, relay_far)
        relay_fars.append(far)
        relay_nears.append(near)

    for chunk in range(chunks):
        on_copies += pass_on(table, far_copies[chunk], chunk, on_sems)
    keep_embedding = pltpu.make_async_copy(embedding_ref, embedding_out, own_sems.at[4])
    keep_embedding.start()
    relay_chunk(0)
    relay_chunk(1)
    for copy in asks:
        copy.wait_recv()
    read_asks = pltpu.make_async_copy(ask_in, asked, own_sems.at[1])
    read_asks.start()
    asked_ref[...] = ask_in[...]
    for copy in on_copies + near_copies:
        copy.wait_recv()
    keep = pltpu.make_async_copy(table, table_ref, own_sems.at[2])
    keep.start()
    read_asks.wait()

    def serve(here, base, asked_of):
        for k in range(half - 1):
            source = mates[k]

            def pick(slot, carry):
                wanted = asked[source, asked_of, slot]
                served[base + k, slot] = here[wanted]
                return carry

            lax.fori_loop(0, slots, pick, 0)

    def push_served(base, asked_of, sems):
        return [
            send(
                served.at[base + k], fetched_ref.at[pl.ds(asked_of * slots, slots)], both(sems, k),
                (mate, dom),
            )
            for k, mate in enumerate(mates)
        ]

    serve(table, 0, group)
    sent += push_served(0, group, serve_sems)

    def widen(index, carry):
        table_f[rows_of(index), :] = table[index].astype(jnp.float32)
        return carry

    lax.fori_loop(0, table.shape[0], widen, 0)
    bounds = [steps * part // 8 for part in (0, 1, 3, 4, 8)]

    def prepare(segment):
        lax.fori_loop(bounds[segment], bounds[segment + 1], prepare_step, 0)

    def relay_pass(chunk):
        return pass_on(relay, relay_fars[chunk], chunk, relay_on)

    prepare(0)
    relay_chunk(2)
    relay_ons += relay_pass(0) + relay_pass(1)
    prepare(1)
    relay_chunk(3)
    relay_ons += relay_pass(2)
    prepare(2)
    relay_ons += relay_pass(3)
    for copy in relay_ons + relay_nears:
        copy.wait_recv()
    serve(relay, half - 1, partner)
    sent += push_served(half - 1, partner, relay_serve)

    def pick_own(slot, carry):
        wanted = own_asks[partner, slot]
        served[2 * half - 2, slot] = relay[wanted]
        return carry

    lax.fori_loop(0, slots, pick_own, 0)
    mine = pltpu.make_async_copy(
        served.at[2 * half - 2], fetched_ref.at[pl.ds(partner * slots, slots)], own_sems.at[3]
    )
    mine.start()
    prepare(3)
    for index in range(max(steps - 2, 0), steps):
        for copy in targets_out(index):
            copy.wait()
    for copy in sent:
        copy.wait_recv()
    clear.wait()
    keep.wait()
    keep_embedding.wait()
    mine.wait()
    for copy in asks + swaps + near_copies + on_copies + relay_nears + relay_ons + sent:
        copy.wait_send()
    for copies in far_copies + relay_fars:
        for copy in copies:
            copy.wait_send()


def fetch_tiles(
    per_step, features, w_in, b_in, w_out, own_requests, anchor_ids, local_tiles, remote_refs,
    own_counts, teacher, groups, doms,
):
    slots = own_requests.shape[1]
    count = features.shape[0]
    width = w_out.shape[1]
    chunks = 4
    half = groups // 2
    far, mates = max(doms // 2 - 1, 1), max(half - 1, 1)
    dma = pltpu.SemaphoreType.DMA
    nodes = doms * count
    blocks, remote_count = remote_refs.shape
    local_count = local_tiles.shape[1]
    near, far_width = local_count * TILE, remote_count * TILE
    anchors, context_width = teacher.shape
    rows = per_step * ABLK
    peers = max(groups - 1, 1)
    in_smem = pl.BlockSpec(memory_space=pltpu.SMEM)
    table, fetched, embedding, asked, *prepared = pl.pallas_call(
        functools.partial(
            fetch_kernel, groups, doms, chunks, per_step, (local_count, remote_count, slots)
        ),
        out_shape=(
            jax.ShapeDtypeStruct((nodes // TILE, TILE, width), jnp.bfloat16),
            jax.ShapeDtypeStruct((groups * slots, TILE, width), jnp.bfloat16),
            jax.ShapeDtypeStruct((count, width), jnp.float32),
            jax.ShapeDtypeStruct((groups, groups, 128), jnp.int32),
            jax.ShapeDtypeStruct((anchors, width), jnp.bfloat16),
            jax.ShapeDtypeStruct((anchors, near), jnp.bfloat16),
            jax.ShapeDtypeStruct((anchors, far_width), jnp.bfloat16),
            jax.ShapeDtypeStruct((blocks, 1, ABLK), jnp.float32),
            jax.ShapeDtypeStruct((blocks, 1, ABLK), jnp.float32),
        ),
        in_specs=[ANYWHERE, ANYWHERE, IN_VMEM, ANYWHERE, IN_VMEM] + [in_smem] * 5 + [ANYWHERE],
        out_specs=(
            ANYWHERE, ANYWHERE, ANYWHERE, IN_VMEM, ANYWHERE, ANYWHERE, ANYWHERE, IN_VMEM, IN_VMEM
        ),
        scratch_shapes=[
            pltpu.VMEM((nodes // TILE, TILE, width), jnp.bfloat16),
            pltpu.VMEM((nodes // TILE, TILE, width), jnp.bfloat16),
            pltpu.VMEM((2 * half - 1, slots, TILE, width), jnp.bfloat16),
            pltpu.VMEM((slots, TILE, width), jnp.bfloat16),
            pltpu.VMEM((groups, 128), jnp.int32),
            pltpu.VMEM((groups, groups, 128), jnp.int32),
            pltpu.SMEM((groups, groups, 128), jnp.int32),
            pltpu.VMEM(features.shape, jnp.bfloat16),
            pltpu.VMEM(w_in.shape, jnp.bfloat16),
            pltpu.VMEM(w_out.shape, jnp.bfloat16),
            dma((3,)),
            pltpu.VMEM((nodes, width), jnp.float32),
            pltpu.VMEM((per_step, ABLK, width), jnp.float32),
            pltpu.VMEM((per_step, near, width), jnp.bfloat16),
            pltpu.VMEM((count, width), jnp.float32),
            pltpu.VMEM((2, rows, context_width), jnp.bfloat16),
            pltpu.VMEM((2, rows, near), jnp.bfloat16),
            pltpu.VMEM((2, rows, far_width), jnp.bfloat16),
            pltpu.VMEM((2, rows, width), jnp.bfloat16),
            dma((2,)),
            dma((2,)),
            dma((2,)),
            dma((2,)),
            [dma((chunks,)), dma((chunks,))],
            [dma((far, chunks)), dma((far, chunks))],
            [dma((far, chunks)), dma((far, chunks))],
            [dma((chunks,)), dma((chunks,))],
            [dma((chunks,)), dma((chunks,))],
            [dma((far, chunks)), dma((far, chunks))],
            [dma((far, chunks)), dma((far, chunks))],
            [dma((peers,)), dma((peers,))],
            [dma((mates,)), dma((mates,))],
            [dma((mates,)), dma((mates,))],
            dma((5,)),
        ],
        compiler_params=pltpu.CompilerParams(
            collective_id=0, has_side_effects=True, vmem_limit_bytes=VMEM_LIMIT
        ),
    )(
        features, w_in, b_in.reshape(1, -1), w_out, own_requests, own_requests,
        anchor_ids, local_tiles, remote_refs, own_counts, teacher,
    )
    asked = lax.dynamic_index_in_dim(asked, lax.axis_index("group"), 1, keepdims=False)
    return (
        table.reshape(-1, width), fetched.reshape(-1, width), embedding,
        asked[:, :slots].reshape(-1), prepared,
    )


def finish_kernel(
    groups, doms, chunks, merged_ref, embedding_in, features_in, w_in_in, b_in_ref, w_out_in,
    node_out, bias_ref, gathered,
    mine, embedding_ref, features_ref, w_in_ref, w_out_ref, node_ref,
    mine_sems, read_sems, node_sems, near_got, far_out, far_got, grad_rows, acc, bias_acc, bias_other, bias_all,
    half_out, half_got, shard_out, shard_got,
    near_sems, far_sems, half_sems, bias_sems, shard_sems, bias_all_sems, gather_sems, pass_sems,
):
    group, dom, core, other, ahead, behind = dom_partners(doms)
    count, width = node_ref.shape
    chips = doms // 2
    chip = dom // 2
    units = groups * chips
    unit = group * chips + chip
    blocks = acc.shape[0] // 2
    shard = shard_got.shape[1]
    part = count // chunks
    step = min(CHUNK, part)
    per_block = acc.shape[1] // shard
    barrier = pltpu.get_barrier_semaphore()

    def at_unit(index):
        return (index // chips, lax.rem(index, chips) * 2 + core)

    def unit_after(k):
        return lax.rem(unit + k + 1, units)

    def unit_before(k):
        return lax.rem(unit + units - k - 1, units)

    def each(start, stop, work):
        def body(k, carry):
            work(k)
            return carry

        lax.fori_loop(start, stop, body, 0)

    def greet_unit(k):
        pl.semaphore_signal(
            barrier, inc=1, device_id=at_unit(unit_after(k)), device_id_type=MESH
        )

    order = [lax.rem(chip + k, chips) for k in range(1, chips)] + [chip]
    mine_copies = [
        pltpu.make_async_copy(
            merged_ref.at[rows_of(to * 2 + core, count), :], mine.at[k], mine_sems.at[k]
        )
        for k, to in enumerate(order)
    ]
    reads = [
        pltpu.make_async_copy(src, dst, read_sems.at[k])
        for k, (src, dst) in enumerate(
            [
                (embedding_in, embedding_ref), (features_in, features_ref),
                (w_in_in, w_in_ref), (w_out_in, w_out_ref),
            ]
        )
    ]
    pl.semaphore_signal(barrier, inc=1, device_id=(group, other), device_id_type=MESH)
    each(0, units - 1, greet_unit)
    for copy in mine_copies + reads:
        copy.start()
    acc[...] = jnp.zeros_like(acc)
    bias_acc[...] = jnp.zeros_like(bias_acc)
    pl.semaphore_wait(barrier, units)

    def remote(src, dst, sems, index, device):
        return pltpu.make_async_remote_copy(
            src_ref=src, dst_ref=dst, send_sem=sems[0].at[index], recv_sem=sems[1].at[index],
            device_id=device, device_id_type=MESH,
        )


    def rows_in(owner, chunk):
        return pl.ds(pl.multiple_of(owner * count + chunk * part, part), part)

    near_copies = {}
    for chunk in range(chunks):
        rows = pl.ds(chunk * part, part)
        for k, to in enumerate(order):
            theirs = merged_ref.at[rows_in(to * 2 + (1 - core), chunk), :]
            copy = remote(
                theirs, near_got.at[k, rows, :], near_sems, (k, chunk), (group, other)
            )
            copy.start()
            near_copies[k, chunk] = copy
    far_copies = {}
    for copy in mine_copies:
        copy.wait()
    for chunk in range(chunks):
        rows = pl.ds(chunk * part, part)
        for k in range(chips - 1):
            near_copies[k, chunk].wait_recv()
            total = mine[k, rows, :].astype(jnp.float32)
            total = total + near_got[k, rows, :].astype(jnp.float32)
            far_out[k, rows, :] = total.astype(jnp.bfloat16)
            copy = remote(
                far_out.at[k, rows, :], far_got.at[k, rows, :], far_sems, (k, chunk),
                (group, ahead[k]),
            )
            copy.start()
            far_copies[k, chunk] = copy

    def backward(base, hidden_half):
        here = pl.ds(base, step)
        span = blocks * 128
        lanes = pl.ds(pl.multiple_of(hidden_half * span, span), span)
        features = features_ref[here, :]
        grads = grad_rows[here, :]
        pre_act = (
            jnp.dot(features, w_in_ref[:, lanes], preferred_element_type=jnp.float32)
            + b_in_ref[:, lanes]
        )
        sigmoid_pre = jax.nn.sigmoid(pre_act)
        hidden = (pre_act * sigmoid_pre).astype(jnp.bfloat16)
        out_grad = tile_grad(grads, hidden)
        hidden_grad = tile_scores(grads, w_out_ref[lanes, :])
        pre_grad = hidden_grad * sigmoid_pre * (1.0 + pre_act * (1.0 - sigmoid_pre))
        bias = jnp.sum(pre_grad, axis=0, keepdims=True)
        in_grad = tile_grad(features, pre_grad.astype(jnp.bfloat16))
        for b in range(blocks):
            cols = slice(b * 128, (b + 1) * 128)
            at = hidden_half * blocks + b
            acc[at, 0:width, :] += in_grad[:, cols]
            acc[at, width : 2 * width, :] += out_grad[:, cols]
            bias_acc[pl.ds(at, 1), :] += bias[:, cols]

    half_copy = remote(half_out, half_got, half_sems, 0, (group, other))
    bias_copy = remote(bias_acc, bias_other, bias_sems, 0, (group, other))
    node_copies = []
    for copy in reads:
        copy.wait()
    for chunk in range(chunks):
        rows = pl.ds(chunk * part, part)
        near_copies[chips - 1, chunk].wait_recv()
        total = mine[chips - 1, rows, :].astype(jnp.float32)
        total = total + near_got[chips - 1, rows, :].astype(jnp.float32)
        for k in range(chips - 1):
            far_copies[k, chunk].wait_recv()
            total = total + far_got[k, rows, :].astype(jnp.float32)
        node_ref[rows, :] = total
        copy = pltpu.make_async_copy(
            node_ref.at[rows, :], node_out.at[rows, :], node_sems.at[chunk]
        )
        copy.start()
        node_copies.append(copy)
        embedding = embedding_ref[rows, :]
        spread = jnp.sqrt(jnp.mean(embedding * embedding, axis=1, keepdims=True) + EPSILON)
        normed = embedding / spread
        grads = (total - normed * jnp.mean(total * normed, axis=1, keepdims=True)) / spread
        grad_rows[rows, :] = grads.astype(jnp.bfloat16)
        for side in (1 - core, core):
            each(0, part // step, lambda k: backward(chunk * part + k * step, side))
            if chunk == chunks - 1 and side is not core:
                for b in range(blocks):
                    half_out[b] = acc[side * blocks + b].astype(jnp.bfloat16)
                half_copy.start()
    bias_copy.start()
    half_copy.wait_recv()

    def shard_at(index):
        block = index // per_block
        row = pl.ds(pl.multiple_of(lax.rem(index, per_block) * shard, shard), shard)
        mine = acc[core * blocks + block, row, :]
        return mine + half_got[block, row, :].astype(jnp.float32)

    def shard_copy(k):
        return remote(
            shard_out.at[k], shard_got.at[k], shard_sems, k, at_unit(unit_after(k))
        )

    def bias_all_copy(k):
        rows = bias_all.at[unit]
        return remote(rows, rows, bias_all_sems, k, at_unit(unit_after(k)))

    def gather_copy(k):
        rows = gathered.at[core, unit]
        return remote(rows, rows, gather_sems, k, at_unit(unit_after(k)))

    def pass_copy(k):
        rows = gathered.at[core, unit_before(k)]
        return remote(rows, rows, pass_sems, k, (group, other))

    def send_shard(k):
        shard_out[k] = shard_at(unit_after(k)).astype(jnp.bfloat16)
        shard_copy(k).start()

    each(0, units - 1, send_shard)
    bias_copy.wait_recv()
    bias_all[unit] = bias_acc[...] + bias_other[...]
    each(0, units - 1, lambda k: bias_all_copy(k).start())

    def add_shard(k, total):
        shard_copy(k).wait_recv()
        return total + shard_got[k].astype(jnp.float32)

    total = lax.fori_loop(0, units - 1, add_shard, shard_at(unit))
    scale = 1.0 / (groups * doms)
    gathered[core, unit] = (total * scale).astype(jnp.bfloat16)
    each(0, units - 1, lambda k: gather_copy(k).start())
    pass_copy(units - 1).start()

    def pass_on(k):
        gather_copy(k).wait_recv()
        pass_copy(k).start()

    each(0, units - 1, lambda k: bias_all_copy(k).wait_recv())
    bias_ref[...] = lax.fori_loop(
        1, units, lambda k, total: total + bias_all[k], bias_all[0]
    ) * scale
    each(0, units - 1, pass_on)

    each(0, units, lambda k: pass_copy(k).wait_recv())
    for copy in node_copies:
        copy.wait()
    for copy in list(near_copies.values()) + list(far_copies.values()) + [half_copy, bias_copy]:
        copy.wait_send()

    def drain(k):
        shard_copy(k).wait_send()
        bias_all_copy(k).wait_send()
        gather_copy(k).wait_send()
        pass_copy(k).wait_send()

    each(0, units - 1, drain)
    pass_copy(units - 1).wait_send()


def lay_out_kernel(node_ref, bias_ref, gathered_ref, node_out, in_out, bias_out, out_out):
    width = out_out.shape[1]
    node_out[...] = node_ref[...]
    for b in range(gathered_ref.shape[0]):
        rows = gathered_ref[b].astype(jnp.float32)
        in_out[:, b * 128 : (b + 1) * 128] = rows[0:width]
        out_out[b * 128 : (b + 1) * 128, :] = rows[width : 2 * width].T

    @pl.when(pl.program_id(0) == 0)
    def _():
        for b in range(bias_ref.shape[0]):
            bias_out[b * 128 : (b + 1) * 128] = bias_ref[b, :]


def lay_out(node_grad, bias, gathered):
    count, width = node_grad.shape
    blocks = bias.shape[0]
    return pl.pallas_call(
        lay_out_kernel,
        out_shape=(
            jax.ShapeDtypeStruct((count, width), jnp.float32),
            jax.ShapeDtypeStruct((width, blocks * 128), jnp.float32),
            jax.ShapeDtypeStruct((blocks * 128,), jnp.float32),
            jax.ShapeDtypeStruct((blocks * 128, width), jnp.float32),
        ),
        grid=(LAY_STEPS,),
        in_specs=[
            pl.BlockSpec((count // LAY_STEPS, width), lambda b: (b, 0)),
            whole(bias.shape),
            pl.BlockSpec((blocks // LAY_STEPS, 2 * width, 128), lambda b: (b, 0, 0)),
        ],
        out_specs=(
            pl.BlockSpec((count // LAY_STEPS, width), lambda b: (b, 0)),
            pl.BlockSpec((width, 128 * blocks // LAY_STEPS), lambda b: (0, b)),
            whole((blocks * 128,)),
            pl.BlockSpec((128 * blocks // LAY_STEPS, width), lambda b: (b, 0)),
        ),
    )(node_grad, bias, gathered)


def finish(merged, embedding, features, w_in, b_in, w_out, groups, doms):
    count, width = embedding.shape
    hid = w_out.shape[0]
    chips = doms // 2
    units = groups * chips
    chunks = 8
    blocks = hid // 128
    shard = hid * 2 * width // (2 * 128) // units
    far = max(chips - 1, 1)
    half = jnp.bfloat16
    dma = pltpu.SemaphoreType.DMA

    def pair(*shape):
        return [dma(shape), dma(shape)]

    node_grad, bias, gathered = pl.pallas_call(
        functools.partial(finish_kernel, groups, doms, chunks),
        out_shape=(
            jax.ShapeDtypeStruct((count, width), jnp.float32),
            jax.ShapeDtypeStruct((blocks, 128), jnp.float32),
            jax.ShapeDtypeStruct((2, units, shard, 128), half),
        ),
        in_specs=[ANYWHERE] * 4 + [IN_VMEM, ANYWHERE],
        out_specs=(ANYWHERE, IN_VMEM, IN_VMEM),
        scratch_shapes=[
            pltpu.VMEM((chips, count, width), half),
            pltpu.VMEM((count, width), jnp.float32),
            pltpu.VMEM(features.shape, half),
            pltpu.VMEM(w_in.shape, half),
            pltpu.VMEM(w_out.shape, half),
            pltpu.VMEM((count, width), jnp.float32),
            dma((chips,)),
            dma((4,)),
            dma((chunks,)),
            pltpu.VMEM((chips, count, width), half),
            pltpu.VMEM((far, count, width), half),
            pltpu.VMEM((far, count, width), half),
            pltpu.VMEM((count, width), half),
            pltpu.VMEM((blocks, 2 * width, 128), jnp.float32),
            pltpu.VMEM((blocks, 128), jnp.float32),
            pltpu.VMEM((blocks, 128), jnp.float32),
            pltpu.VMEM((units, blocks, 128), jnp.float32),
            pltpu.VMEM((blocks // 2, 2 * width, 128), half),
            pltpu.VMEM((blocks // 2, 2 * width, 128), half),
            pltpu.VMEM((units - 1, shard, 128), half),
            pltpu.VMEM((units - 1, shard, 128), half),
            pair(chips, chunks),
            pair(far, chunks),
            pair(1),
            pair(1),
            pair(units - 1),
            pair(units - 1),
            pair(units - 1),
            pair(units),
        ],
        compiler_params=pltpu.CompilerParams(
            collective_id=1, has_side_effects=True, vmem_limit_bytes=VMEM_LIMIT
        ),
    )(merged, embedding, features, w_in, b_in.reshape(1, -1), w_out)
    return lay_out(node_grad, bias, gathered.reshape(blocks, 2 * width, 128))


def shards(
    features, w_in, b_in, w_out, anchor_ids, local_tiles, requests, counts, remote_refs, teacher
):
    groups = lax.axis_size("group")
    doms = lax.axis_size("dom")
    devices = groups * doms
    own_requests = requests[0, 0]
    own_counts = counts[0, 0]
    slot_count = own_requests.shape[1]
    per_step = math.gcd(local_tiles.shape[0], 4)
    table, fetched, embedding, asked, prepared = fetch_tiles(
        per_step, features, w_in, b_in, w_out, own_requests, anchor_ids, local_tiles,
        remote_refs, own_counts, teacher, groups, doms,
    )
    anchor_kl, inverse, delta, remote_grad = score(
        math.gcd(local_tiles.shape[0], 8), remote_refs, own_counts, fetched, prepared, slot_count
    )
    anchor_kl = anchor_kl.reshape(-1)
    returned = lax.all_to_all(remote_grad, "group", split_axis=0, concat_axis=0, tiled=True)
    local_grad = local_grads(
        per_step, anchor_ids, local_tiles, remote_refs, table, fetched, prepared[0], prepared[1],
        inverse, delta,
    )
    merged = merge(asked, local_grad, returned)
    node_grad, in_grad, bias_grad, out_grad = finish(
        merged, embedding, features, w_in, b_in, w_out, groups, doms
    )
    return anchor_kl, node_grad, in_grad, bias_grad, out_grad


def solution(mesh):
    return jax.shard_map(
        shards,
        mesh=mesh,
        in_specs=(
            P(("group", "dom"), None),
            P(),
            P(),
            P(),
            P(("group", "dom")),
            P(("group", "dom"), None),
            P("group", "dom", None, None),
            P("group", "dom", None),
            P(("group", "dom"), None),
            P(("group", "dom"), None),
        ),
        out_specs=(P(("group", "dom")), P(("group", "dom"), None), P(), P(), P()),
        check_vma=False,
    )
```

```python
import functools
import math

import jax
import jax.numpy as jnp
from jax import lax
from jax.experimental import pallas as pl
from jax.experimental.pallas import tpu as pltpu
from jax.sharding import PartitionSpec as P

TILE = 128
ABLK = 128

SCORE_SCALE = 8.0
EPSILON = 1e-06
VMEM_LIMIT = 60 * 1024 * 1024
CHUNK = 256

ONE_COPY = pl.Buffered(1)


def whole(shape):
    return pl.BlockSpec(shape, lambda *_: (0,) * len(shape), pipeline_mode=ONE_COPY)


def node_rows(feature_rows, w_in, b_in, w_out):
    pre_act = jnp.dot(feature_rows, w_in, preferred_element_type=jnp.float32) + b_in
    hidden = (pre_act * jax.nn.sigmoid(pre_act)).astype(jnp.bfloat16)
    embedding = jnp.dot(hidden, w_out, preferred_element_type=jnp.float32)
    spread = jnp.sqrt(jnp.mean(embedding * embedding, axis=1, keepdims=True) + EPSILON)
    return embedding, (embedding / spread).astype(jnp.bfloat16)


def rows_of(index, count=TILE):
    return pl.ds(pl.multiple_of(index * count, count), count)


def cost(flops, moved, powers):
    return pl.CostEstimate(flops=flops, bytes_accessed=moved, transcendentals=powers)


def clear_rows(ref):
    zero_chunk = jnp.zeros((CHUNK, ref.shape[1]), ref.dtype)

    def clear(index, carry):
        ref[rows_of(index, CHUNK), :] = zero_chunk
        return carry

    lax.fori_loop(0, ref.shape[0] // CHUNK, clear, 0)


def tile_scores(anchors, context):
    return lax.dot_general(
        anchors, context, (((1,), (1,)), ((), ())), preferred_element_type=jnp.float32
    )


def prepare_block(
    scale, shapes, block, rows, teacher_rows, ids_ref, tiles_ref, refs_ref, counts_ref,
    table, table_f, anchor_rows, context, near_rows, far_rows,
):
    local_count, remote_count, slot_count = shapes

    def gather(index, carry):
        for lane in range(16):
            row = index * 16 + lane
            anchor_rows[row, :] = table_f[ids_ref[block * ABLK + row], :]
        return carry

    lax.fori_loop(0, ABLK // 16, gather, 0)
    anchors = (anchor_rows[...] * scale).astype(jnp.bfloat16)
    for i in range(local_count):
        context[i * TILE : (i + 1) * TILE, :] = table[tiles_ref[i, block]]
    all_scores = tile_scores(anchors, context[...])
    target_sum = gap_sum = student_sum = None
    exps = []
    for i in range(local_count + remote_count):
        teacher = teacher_rows[rows, i * TILE : (i + 1) * TILE].astype(jnp.float32)
        target_exp = jnp.exp(teacher)
        if i >= local_count:
            ref = refs_ref[i - local_count, block]
            live = lax.rem(ref, slot_count) < counts_ref[lax.div(ref, slot_count)]
            target_exp = target_exp * jnp.where(live, 1.0, 0.0).astype(jnp.float32)
            gap = target_exp * teacher
        else:
            scores = all_scores[:, i * TILE : (i + 1) * TILE]
            gap = target_exp * (teacher - scores)
            student_exp = jnp.exp(scores)
            student_sum = student_exp if i == 0 else student_sum + student_exp
        target_sum = target_exp if i == 0 else target_sum + target_exp
        gap_sum = gap if i == 0 else gap_sum + gap
        exps.append(target_exp)
    total = jnp.sum(target_sum.T, axis=0, keepdims=True)
    inverse = 1.0 / total
    base = jnp.sum(gap_sum.T, axis=0, keepdims=True) * inverse - jnp.log(total)
    spread_inverse = jnp.broadcast_to(inverse, (TILE, ABLK)).T
    for i, target_exp in enumerate(exps):
        out, at = (near_rows, i) if i < local_count else (far_rows, i - local_count)
        out[rows, at * TILE : (at + 1) * TILE] = (target_exp * spread_inverse).astype(
            jnp.bfloat16
        )
    return anchors, base, jnp.sum(student_sum.T, axis=0, keepdims=True)


def take_context(block, sub, context, tiles_ref, refs_ref, table_ref, fetched_ref, counts):
    local_count, remote_count = counts
    places = []
    for i in range(local_count):
        place = rows_of(tiles_ref[i, block])
        context[sub, i * TILE : (i + 1) * TILE, :] = table_ref[place, :]
        places.append(place)
    for i in range(remote_count):
        place = rows_of(refs_ref[i, block])
        at = local_count + i
        context[sub, at * TILE : (at + 1) * TILE, :] = fetched_ref[place, :]
        places.append(place)
    return places


def tile_grad(delta, anchors):
    return lax.dot_general(
        delta, anchors, (((0,), (0,)), ((), ())), preferred_element_type=jnp.float32
    )


def score_kernel(
    per_step, remote_count, slot_count, refs_ref, counts_ref,
    fetched_ref, anchors_ref, far_ref, base_ref, partial_ref,
    kl_ref, inverse_ref, delta_ref, remote_grad_ref, remote_acc, context,
):
    @pl.when(pl.program_id(0) == 0)
    def _():
        clear_rows(remote_acc)

    for sub in range(per_step):
        block = pl.program_id(0) * per_step + sub
        rows = slice(sub * ABLK, (sub + 1) * ABLK)
        anchors = anchors_ref[rows, :]
        places = []
        lives = []
        for i in range(remote_count):
            ref = refs_ref[i, block]
            places.append(rows_of(ref))
            live = lax.rem(ref, slot_count) < counts_ref[lax.div(ref, slot_count)]
            lives.append(jnp.where(live, 1.0, 0.0).astype(jnp.float32))
            context[sub, i * TILE : (i + 1) * TILE, :] = fetched_ref[places[i], :]
        all_scores = tile_scores(anchors, context[sub])
        student = []
        student_sum = gap_sum = None
        for i in range(remote_count):
            span = slice(i * TILE, (i + 1) * TILE)
            scores = all_scores[:, span]
            student_exp = jnp.exp(scores) * lives[i]
            gap = far_ref[rows, span].astype(jnp.float32) * scores
            student_sum = student_exp if i == 0 else student_sum + student_exp
            gap_sum = gap if i == 0 else gap_sum + gap
            student.append(student_exp)
        total = partial_ref[sub] + jnp.sum(student_sum.T, axis=0, keepdims=True)
        inverse = 1.0 / total
        kl_ref[sub] = base_ref[sub] + jnp.log(total) - jnp.sum(gap_sum.T, axis=0, keepdims=True)
        inverse_ref[sub] = inverse
        spread_inverse = jnp.broadcast_to(inverse, (TILE, ABLK)).T
        for i in range(remote_count):
            span = slice(i * TILE, (i + 1) * TILE)
            delta = (student[i] * spread_inverse - far_ref[rows, span].astype(jnp.float32)).astype(
                jnp.bfloat16
            )
            delta_ref[rows, span] = delta
        grads = tile_grad(delta_ref[rows, :], anchors)
        for i in range(remote_count):
            remote_acc[places[i], :] += grads[i * TILE : (i + 1) * TILE]

    @pl.when(pl.program_id(0) == pl.num_programs(0) - 1)
    def _():
        def finish(index, carry):
            here = rows_of(index, CHUNK)
            remote_grad_ref[here, :] = remote_acc[here, :].astype(jnp.bfloat16)
            return carry

        lax.fori_loop(0, remote_acc.shape[0] // CHUNK, finish, 0)


def score(per_step, remote_refs, own_counts, fetched, prepared, slots):
    anchors, near, far, base, partial = prepared
    blocks, remote_count = remote_refs.shape
    width = anchors.shape[1]
    rows = per_step * ABLK
    pairs = far.shape[0] * far.shape[1]
    row_spec = pl.BlockSpec((per_step, 1, ABLK), lambda b, *_: (b, 0, 0))
    far_spec = pl.BlockSpec((rows, far.shape[1]), lambda b, *_: (b, 0))
    return pl.pallas_call(
        functools.partial(score_kernel, per_step, remote_count, slots),
        out_shape=(
            jax.ShapeDtypeStruct((blocks, 1, ABLK), jnp.float32),
            jax.ShapeDtypeStruct((blocks, 1, ABLK), jnp.float32),
            jax.ShapeDtypeStruct(far.shape, jnp.bfloat16),
            jax.ShapeDtypeStruct(fetched.shape, jnp.bfloat16),
        ),
        grid_spec=pltpu.PrefetchScalarGridSpec(
            num_scalar_prefetch=2,
            grid=(blocks // per_step,),
            in_specs=[
                whole(fetched.shape),
                pl.BlockSpec((rows, width), lambda b, *_: (b, 0)),
                far_spec,
                row_spec,
                row_spec,
            ],
            out_specs=(row_spec, row_spec, far_spec, whole(fetched.shape)),
            scratch_shapes=[
                pltpu.VMEM(fetched.shape, jnp.float32),
                pltpu.VMEM((per_step, far.shape[1], width), jnp.bfloat16),
            ],
        ),
        compiler_params=pltpu.CompilerParams(vmem_limit_bytes=VMEM_LIMIT),
        cost_estimate=cost(3 * pairs * width, 4 * pairs, pairs),
    )(remote_refs.T, own_counts, fetched, anchors, far, base, partial)


def local_kernel(
    per_step, local_count, remote_count, lanes, ids_ref, tiles_ref, refs_ref,
    table_ref, fetched_ref, anchors_ref, near_ref, inverse_ref, delta_ref, local_grad_ref,
    context, near_delta, anchor_grad, *row_accs,
):
    scale = SCORE_SCALE / table_ref.shape[1]

    @pl.when(pl.program_id(0) == 0)
    def _():
        clear_rows(local_grad_ref)
        for acc in row_accs:
            clear_rows(acc)

    for sub in range(per_step):
        block = pl.program_id(0) * per_step + sub
        rows = slice(sub * ABLK, (sub + 1) * ABLK)
        places = take_context(
            block, sub, context, tiles_ref, refs_ref, table_ref, fetched_ref,
            (local_count, remote_count),
        )
        anchors = anchors_ref[rows, :]
        spread_inverse = jnp.broadcast_to(inverse_ref[sub], (TILE, ABLK)).T
        near = local_count * TILE
        scores = tile_scores(anchors, context[sub, :near, :])
        for i in range(local_count):
            span = slice(i * TILE, (i + 1) * TILE)
            student = jnp.exp(scores[:, span]) * spread_inverse
            delta = (student - near_ref[rows, span].astype(jnp.float32)).astype(jnp.bfloat16)
            near_delta[rows, span] = delta
        grads = tile_grad(near_delta[rows, :], anchors)
        for i in range(local_count):
            local_grad_ref[places[i], :] += grads[i * TILE : (i + 1) * TILE]
        near_part = jnp.dot(
            near_delta[rows, :], context[sub, :near, :], preferred_element_type=jnp.float32
        )
        far_part = jnp.dot(
            delta_ref[rows, :], context[sub, near:, :], preferred_element_type=jnp.float32
        )
        anchor_grad[rows, :] = (near_part + far_part) * scale
        for row in range(ABLK):
            acc = row_accs[row % lanes]
            at = sub * ABLK + row
            acc[pl.ds(ids_ref[block * ABLK + row], 1), :] += anchor_grad[at : at + 1, :]

    @pl.when(pl.program_id(0) == pl.num_programs(0) - 1)
    def _():
        def finish(index, carry):
            here = rows_of(index, CHUNK)
            total = local_grad_ref[here, :]
            for acc in row_accs:
                total = total + acc[here, :]
            local_grad_ref[here, :] = total
            return carry

        lax.fori_loop(0, local_grad_ref.shape[0] // CHUNK, finish, 0)


def local_grads(
    per_step, anchor_ids, local_tiles, remote_refs, table, fetched, anchors, near, inverse, delta
):
    blocks, local_count = local_tiles.shape
    remote_count = remote_refs.shape[1]
    context_width = near.shape[1] + delta.shape[1]
    width = table.shape[1]
    rows = per_step * ABLK
    lanes = 4 if table.shape[0] <= 8192 else 1
    pairs = delta.shape[0] * context_width
    return pl.pallas_call(
        functools.partial(local_kernel, per_step, local_count, remote_count, lanes),
        out_shape=jax.ShapeDtypeStruct(table.shape, jnp.float32),
        grid_spec=pltpu.PrefetchScalarGridSpec(
            num_scalar_prefetch=3,
            grid=(blocks // per_step,),
            in_specs=[
                whole(table.shape),
                whole(fetched.shape),
                pl.BlockSpec((rows, width), lambda b, *_: (b, 0)),
                pl.BlockSpec((rows, near.shape[1]), lambda b, *_: (b, 0)),
                pl.BlockSpec((per_step, 1, ABLK), lambda b, *_: (b, 0, 0)),
                pl.BlockSpec((rows, delta.shape[1]), lambda b, *_: (b, 0)),
            ],
            out_specs=whole(table.shape),
            scratch_shapes=[
                pltpu.VMEM((per_step, context_width, width), jnp.bfloat16),
                pltpu.VMEM((rows, near.shape[1]), jnp.bfloat16),
                pltpu.VMEM((rows, width), jnp.float32),
            ]
            + [pltpu.VMEM(table.shape, jnp.float32)] * lanes,
        ),
        compiler_params=pltpu.CompilerParams(vmem_limit_bytes=VMEM_LIMIT),
        cost_estimate=cost(3 * pairs * width, 2 * pairs, 0),
    )(
        anchor_ids, local_tiles.T, remote_refs.T,
        table, fetched, anchors, near, inverse, delta,
    )


def merge_kernel(
    pieces, asked_ref, local_ref, returned_ref, out_ref,
    acc, returned, merged, local_sems, returned_sems, out_sems,
):
    def copies(src, dst, sems):
        count = src.shape[0] // pieces
        return [
            pltpu.make_async_copy(
                src.at[pl.ds(c * count, count)], dst.at[pl.ds(c * count, count)], sems.at[c]
            )
            for c in range(pieces)
        ]

    local_in = copies(local_ref, acc, local_sems)
    returned_in = copies(returned_ref, returned, returned_sems)
    merged_out = copies(merged, out_ref, out_sems)
    for copy in returned_in + local_in:
        copy.start()
    for copy in local_in:
        copy.wait()
    slots = returned.shape[0] // pieces
    for c in range(pieces):
        returned_in[c].wait()

        def add(index, carry):
            slot = c * slots + index
            acc[asked_ref[slot]] += returned[slot].astype(jnp.float32)
            return carry

        lax.fori_loop(0, slots, add, 0, unroll=4)
    tiles = acc.shape[0] // pieces
    for c in range(pieces):
        def narrow(index, carry):
            here = pl.ds(c * tiles + index * 4, 4)
            merged[here] = acc[here].astype(jnp.bfloat16)
            return carry

        lax.fori_loop(0, tiles // 4, narrow, 0)
        merged_out[c].start()
    for copy in merged_out:
        copy.wait()


def merge(asked, local_grad, returned):
    pieces = 4
    rows, width = local_grad.shape
    local_grad = local_grad.reshape(-1, TILE, width)
    returned = returned.reshape(-1, TILE, width)
    dma = pltpu.SemaphoreType.DMA
    return pl.pallas_call(
        functools.partial(merge_kernel, pieces),
        out_shape=jax.ShapeDtypeStruct(local_grad.shape, jnp.bfloat16),
        in_specs=[pl.BlockSpec(memory_space=pltpu.SMEM), ANYWHERE, ANYWHERE],
        out_specs=ANYWHERE,
        scratch_shapes=[
            pltpu.VMEM(local_grad.shape, jnp.float32),
            pltpu.VMEM(returned.shape, jnp.bfloat16),
            pltpu.VMEM(local_grad.shape, jnp.bfloat16),
            dma((pieces,)),
            dma((pieces,)),
            dma((pieces,)),
        ],
        compiler_params=pltpu.CompilerParams(vmem_limit_bytes=12 * local_grad.size),
    )(asked, local_grad, returned).reshape(rows, width)


MESH = pl.DeviceIdType.MESH
ANYWHERE = pl.BlockSpec(memory_space=pl.ANY)
IN_VMEM = pl.BlockSpec(memory_space=pltpu.VMEM)


def greet(partners):
    barrier = pltpu.get_barrier_semaphore()
    for partner in partners:
        pl.semaphore_signal(barrier, inc=1, device_id=partner, device_id_type=MESH)
    pl.semaphore_wait(barrier, len(partners))


def dom_partners(doms):
    group, dom = lax.axis_index("group"), lax.axis_index("dom")
    chips = doms // 2
    chip, core = dom // 2, dom % 2
    other = chip * 2 + (1 - core)
    ahead = [lax.rem(chip + k, chips) * 2 + core for k in range(1, chips)]
    behind = [lax.rem(chip + chips - k, chips) for k in range(1, chips)]
    return group, dom, core, other, ahead, behind


def fetch_kernel(
    groups, doms, chunks, per_step, shapes,
    features_in, w_in_in, b_in_ref, w_out_in, requests_ref, own_asks,
    ids_ref, tiles_ref, refs_ref, counts_ref, teacher_ref,
    table_ref, fetched_ref, embedding_out, asked_ref,
    anchors_ref, near_ref, far_ref, base_ref, partial_ref,
    table, relay, served, blank, ask_out, ask_in, asked,
    features_ref, w_in_ref, w_out_ref, read_sems,
    table_f, anchor_rows, context, embedding_ref, teacher_buf, near_buf, far_buf, anchor_buf,
    in_sems, near_out_sems, far_out_sems, anchor_out_sems,
    near_sems, far_sems, on_sems, swap_sems, relay_near, relay_far, relay_on,
    ask_sems, serve_sems, relay_serve, own_sems,
):
    group, dom, core, other, ahead, behind = dom_partners(doms)
    half = groups // 2
    slots = requests_ref.shape[1]
    count = features_in.shape[0]
    part = count // chunks
    step = min(CHUNK, part)
    first = group // half * half
    place = lax.rem(group, half)
    mates = [first + lax.rem(place + k, half) for k in range(1, half)]
    partner = lax.rem(group + half, groups)
    peers = [lax.rem(group + k, groups) for k in range(1, groups)]
    steps = teacher_ref.shape[0] // (per_step * ABLK)
    step_rows = per_step * ABLK

    def teacher_in(index):
        return pltpu.make_async_copy(
            teacher_ref.at[rows_of(index, step_rows), :],
            teacher_buf.at[lax.rem(index, 2)],
            in_sems.at[lax.rem(index, 2)],
        )

    def targets_out(index):
        at = lax.rem(index, 2)
        rows = rows_of(index, step_rows)
        return (
            pltpu.make_async_copy(near_buf.at[at], near_ref.at[rows, :], near_out_sems.at[at]),
            pltpu.make_async_copy(far_buf.at[at], far_ref.at[rows, :], far_out_sems.at[at]),
            pltpu.make_async_copy(
                anchor_buf.at[at], anchors_ref.at[rows, :], anchor_out_sems.at[at]
            ),
        )

    def prepare_step(index, carry):
        at = lax.rem(index, 2)
        teacher_in(index).wait()

        @pl.when(index + 1 < steps)
        def _():
            teacher_in(index + 1).start()

        @pl.when(index >= 2)
        def _():
            for copy in targets_out(index - 2):
                copy.wait()

        for sub in range(per_step):
            block = index * per_step + sub
            anchors, base, partial = prepare_block(
                SCORE_SCALE / table.shape[2], shapes, block, pl.ds(sub * ABLK, ABLK),
                teacher_buf.at[at], ids_ref, tiles_ref, refs_ref, counts_ref,
                table, table_f, anchor_rows.at[sub], context.at[sub], near_buf.at[at],
                far_buf.at[at],
            )
            anchor_buf[at, sub * ABLK : (sub + 1) * ABLK, :] = anchors
            base_ref[block] = base
            partial_ref[block] = partial
        for copy in targets_out(index):
            copy.start()
        return carry

    reads = [
        pltpu.make_async_copy(src, dst, read_sems.at[k])
        for k, (src, dst) in enumerate(
            [(features_in, features_ref), (w_in_in, w_in_ref), (w_out_in, w_out_ref)]
        )
    ]
    for copy in reads:
        copy.start()
    teacher_in(0).start()
    greet(
        [(group, other)] + [(group, far) for far in ahead]
        + [(peer, dom) for peer in peers]
    )

    tiles = part // TILE

    def span(owner, chunk):
        return pl.ds(owner * (count // TILE) + chunk * tiles, tiles)

    def both(sems, *index):
        return sems[0].at[index], sems[1].at[index]

    def send(src, dst, sems, partner_at):
        copy = pltpu.make_async_remote_copy(
            src_ref=src, dst_ref=dst, send_sem=sems[0], recv_sem=sems[1],
            device_id=partner_at, device_id_type=MESH,
        )
        copy.start()
        return copy

    def spread_chunk(here, owner, chunk, near, far):
        rows = here.at[span(owner, chunk)]
        far_copies = [
            send(rows, rows, both(far, k, chunk), (group, there)) for k, there in enumerate(ahead)
        ]
        return far_copies, send(rows, rows, both(near, chunk), (group, other))

    def pass_on(here, far_copies, chunk, on):
        copies = []
        for k, copy in enumerate(far_copies):
            copy.wait_recv()
            rows = here.at[span(behind[k] * 2 + core, chunk)]
            copies.append(send(rows, rows, both(on, k, chunk), (group, other)))
        return copies

    ask_out[...] = jnp.zeros_like(ask_out)
    ask_out[:, 0:slots] = requests_ref[...]
    asks = [
        send(ask_out, ask_in.at[group], both(ask_sems, k), (peer, dom))
        for k, peer in enumerate(peers)
    ]
    ask_in[group] = ask_out[...]
    blank[...] = jnp.zeros_like(blank)
    sent = []
    far_copies, near_copies, swaps = [], [], []
    for copy in reads:
        copy.wait()
    for chunk in range(chunks):
        def forward(index, carry):
            at = pl.ds(pl.multiple_of(chunk * part + index * step, step), step)
            embedding, unit_rows = node_rows(
                features_ref[at, :], w_in_ref[...], b_in_ref[...], w_out_ref[...]
            )
            embedding_ref[at, :] = embedding
            to = pl.ds((dom * count + chunk * part) // TILE + index * (step // TILE), step // TILE)
            table[to] = unit_rows.reshape(step // TILE, TILE, unit_rows.shape[1])
            return carry

        lax.fori_loop(0, part // step, forward, 0)
        rows = span(dom, chunk)
        swaps.append(
            send(table.at[rows], relay.at[rows], both(swap_sems, chunk), (partner, dom))
        )
        far, near = spread_chunk(table, dom, chunk, near_sems, far_sems)
        far_copies.append(far)
        near_copies.append(near)
    clear = pltpu.make_async_copy(blank, fetched_ref.at[pl.ds(group * slots, slots)], own_sems.at[0])
    clear.start()
    on_copies, relay_fars, relay_nears, relay_ons = [], [], [], []

    def relay_chunk(chunk):
        swaps[chunk].wait_recv()
        far, near = spread_chunk(relay, dom, chunk, relay_near, relay_far)
        relay_fars.append(far)
        relay_nears.append(near)

    for chunk in range(chunks):
        on_copies += pass_on(table, far_copies[chunk], chunk, on_sems)
    keep_embedding = pltpu.make_async_copy(embedding_ref, embedding_out, own_sems.at[4])
    keep_embedding.start()
    relay_chunk(0)
    relay_chunk(1)
    for copy in asks:
        copy.wait_recv()
    read_asks = pltpu.make_async_copy(ask_in, asked, own_sems.at[1])
    read_asks.start()
    asked_ref[...] = ask_in[...]
    for copy in on_copies + near_copies:
        copy.wait_recv()
    keep = pltpu.make_async_copy(table, table_ref, own_sems.at[2])
    keep.start()
    read_asks.wait()

    def serve(here, base, asked_of):
        for k in range(half - 1):
            source = mates[k]

            def pick(slot, carry):
                wanted = asked[source, asked_of, slot]
                served[base + k, slot] = here[wanted]
                return carry

            lax.fori_loop(0, slots, pick, 0)

    def push_served(base, asked_of, sems):
        return [
            send(
                served.at[base + k], fetched_ref.at[pl.ds(asked_of * slots, slots)], both(sems, k),
                (mate, dom),
            )
            for k, mate in enumerate(mates)
        ]

    serve(table, 0, group)
    sent += push_served(0, group, serve_sems)

    def widen(index, carry):
        table_f[rows_of(index), :] = table[index].astype(jnp.float32)
        return carry

    lax.fori_loop(0, table.shape[0], widen, 0)
    bounds = [steps * part // 8 for part in (0, 1, 3, 4, 8)]

    def prepare(segment):
        lax.fori_loop(bounds[segment], bounds[segment + 1], prepare_step, 0)

    def relay_pass(chunk):
        return pass_on(relay, relay_fars[chunk], chunk, relay_on)

    prepare(0)
    relay_chunk(2)
    relay_ons += relay_pass(0) + relay_pass(1)
    prepare(1)
    relay_chunk(3)
    relay_ons += relay_pass(2)
    prepare(2)
    relay_ons += relay_pass(3)
    for copy in relay_ons + relay_nears:
        copy.wait_recv()
    serve(relay, half - 1, partner)
    sent += push_served(half - 1, partner, relay_serve)

    def pick_own(slot, carry):
        wanted = own_asks[partner, slot]
        served[2 * half - 2, slot] = relay[wanted]
        return carry

    lax.fori_loop(0, slots, pick_own, 0)
    mine = pltpu.make_async_copy(
        served.at[2 * half - 2], fetched_ref.at[pl.ds(partner * slots, slots)], own_sems.at[3]
    )
    mine.start()
    prepare(3)
    for index in range(max(steps - 2, 0), steps):
        for copy in targets_out(index):
            copy.wait()
    for copy in sent:
        copy.wait_recv()
    clear.wait()
    keep.wait()
    keep_embedding.wait()
    mine.wait()
    for copy in asks + swaps + near_copies + on_copies + relay_nears + relay_ons + sent:
        copy.wait_send()
    for copies in far_copies + relay_fars:
        for copy in copies:
            copy.wait_send()


def fetch_tiles(
    per_step, features, w_in, b_in, w_out, own_requests, anchor_ids, local_tiles, remote_refs,
    own_counts, teacher, groups, doms,
):
    slots = own_requests.shape[1]
    count = features.shape[0]
    width = w_out.shape[1]
    chunks = 4
    half = groups // 2
    far, mates = max(doms // 2 - 1, 1), max(half - 1, 1)
    dma = pltpu.SemaphoreType.DMA
    nodes = doms * count
    blocks, remote_count = remote_refs.shape
    local_count = local_tiles.shape[1]
    near, far_width = local_count * TILE, remote_count * TILE
    anchors, context_width = teacher.shape
    rows = per_step * ABLK
    peers = max(groups - 1, 1)
    in_smem = pl.BlockSpec(memory_space=pltpu.SMEM)
    table, fetched, embedding, asked, *prepared = pl.pallas_call(
        functools.partial(
            fetch_kernel, groups, doms, chunks, per_step, (local_count, remote_count, slots)
        ),
        out_shape=(
            jax.ShapeDtypeStruct((nodes // TILE, TILE, width), jnp.bfloat16),
            jax.ShapeDtypeStruct((groups * slots, TILE, width), jnp.bfloat16),
            jax.ShapeDtypeStruct((count, width), jnp.float32),
            jax.ShapeDtypeStruct((groups, groups, 128), jnp.int32),
            jax.ShapeDtypeStruct((anchors, width), jnp.bfloat16),
            jax.ShapeDtypeStruct((anchors, near), jnp.bfloat16),
            jax.ShapeDtypeStruct((anchors, far_width), jnp.bfloat16),
            jax.ShapeDtypeStruct((blocks, 1, ABLK), jnp.float32),
            jax.ShapeDtypeStruct((blocks, 1, ABLK), jnp.float32),
        ),
        in_specs=[ANYWHERE, ANYWHERE, IN_VMEM, ANYWHERE, IN_VMEM] + [in_smem] * 5 + [ANYWHERE],
        out_specs=(
            ANYWHERE, ANYWHERE, ANYWHERE, IN_VMEM, ANYWHERE, ANYWHERE, ANYWHERE, IN_VMEM, IN_VMEM
        ),
        scratch_shapes=[
            pltpu.VMEM((nodes // TILE, TILE, width), jnp.bfloat16),
            pltpu.VMEM((nodes // TILE, TILE, width), jnp.bfloat16),
            pltpu.VMEM((2 * half - 1, slots, TILE, width), jnp.bfloat16),
            pltpu.VMEM((slots, TILE, width), jnp.bfloat16),
            pltpu.VMEM((groups, 128), jnp.int32),
            pltpu.VMEM((groups, groups, 128), jnp.int32),
            pltpu.SMEM((groups, groups, 128), jnp.int32),
            pltpu.VMEM(features.shape, jnp.bfloat16),
            pltpu.VMEM(w_in.shape, jnp.bfloat16),
            pltpu.VMEM(w_out.shape, jnp.bfloat16),
            dma((3,)),
            pltpu.VMEM((nodes, width), jnp.float32),
            pltpu.VMEM((per_step, ABLK, width), jnp.float32),
            pltpu.VMEM((per_step, near, width), jnp.bfloat16),
            pltpu.VMEM((count, width), jnp.float32),
            pltpu.VMEM((2, rows, context_width), jnp.bfloat16),
            pltpu.VMEM((2, rows, near), jnp.bfloat16),
            pltpu.VMEM((2, rows, far_width), jnp.bfloat16),
            pltpu.VMEM((2, rows, width), jnp.bfloat16),
            dma((2,)),
            dma((2,)),
            dma((2,)),
            dma((2,)),
            [dma((chunks,)), dma((chunks,))],
            [dma((far, chunks)), dma((far, chunks))],
            [dma((far, chunks)), dma((far, chunks))],
            [dma((chunks,)), dma((chunks,))],
            [dma((chunks,)), dma((chunks,))],
            [dma((far, chunks)), dma((far, chunks))],
            [dma((far, chunks)), dma((far, chunks))],
            [dma((peers,)), dma((peers,))],
            [dma((mates,)), dma((mates,))],
            [dma((mates,)), dma((mates,))],
            dma((5,)),
        ],
        compiler_params=pltpu.CompilerParams(
            collective_id=0, has_side_effects=True, vmem_limit_bytes=VMEM_LIMIT
        ),
    )(
        features, w_in, b_in.reshape(1, -1), w_out, own_requests, own_requests,
        anchor_ids, local_tiles.T, remote_refs.T, own_counts, teacher,
    )
    asked = lax.dynamic_index_in_dim(asked, lax.axis_index("group"), 1, keepdims=False)
    return (
        table.reshape(-1, width), fetched.reshape(-1, width), embedding,
        asked[:, :slots].reshape(-1), prepared,
    )


def finish_kernel(
    groups, doms, chunks, merged_ref, embedding_in, features_in, w_in_in, b_in_ref, w_out_in,
    node_out, bias_ref, gathered,
    mine, embedding_ref, features_ref, w_in_ref, w_out_ref, node_ref,
    mine_sems, read_sems, node_sems, near_got, far_out, far_got, grad_rows, acc, bias_acc, bias_other, bias_all,
    half_out, half_got, shard_out, shard_got,
    near_sems, far_sems, half_sems, bias_sems, shard_sems, bias_all_sems, gather_sems, pass_sems,
):
    group, dom, core, other, ahead, behind = dom_partners(doms)
    count, width = node_ref.shape
    chips = doms // 2
    chip = dom // 2
    units = groups * chips
    unit = group * chips + chip
    blocks = acc.shape[0] // 2
    shard = shard_got.shape[1]
    part = count // chunks
    step = min(CHUNK, part)
    per_block = acc.shape[1] // shard
    barrier = pltpu.get_barrier_semaphore()

    def at_unit(index):
        return (index // chips, lax.rem(index, chips) * 2 + core)

    def unit_after(k):
        return lax.rem(unit + k + 1, units)

    def unit_before(k):
        return lax.rem(unit + units - k - 1, units)

    def each(start, stop, work):
        def body(k, carry):
            work(k)
            return carry

        lax.fori_loop(start, stop, body, 0)

    def greet_unit(k):
        pl.semaphore_signal(
            barrier, inc=1, device_id=at_unit(unit_after(k)), device_id_type=MESH
        )

    order = [lax.rem(chip + k, chips) for k in range(1, chips)] + [chip]
    mine_copies = [
        pltpu.make_async_copy(
            merged_ref.at[rows_of(to * 2 + core, count), :], mine.at[k], mine_sems.at[k]
        )
        for k, to in enumerate(order)
    ]
    reads = [
        pltpu.make_async_copy(src, dst, read_sems.at[k])
        for k, (src, dst) in enumerate(
            [
                (embedding_in, embedding_ref), (features_in, features_ref),
                (w_in_in, w_in_ref), (w_out_in, w_out_ref),
            ]
        )
    ]
    pl.semaphore_signal(barrier, inc=1, device_id=(group, other), device_id_type=MESH)
    each(0, units - 1, greet_unit)
    for copy in mine_copies + reads:
        copy.start()
    acc[...] = jnp.zeros_like(acc)
    bias_acc[...] = jnp.zeros_like(bias_acc)
    pl.semaphore_wait(barrier, units)

    def remote(src, dst, sems, index, device):
        return pltpu.make_async_remote_copy(
            src_ref=src, dst_ref=dst, send_sem=sems[0].at[index], recv_sem=sems[1].at[index],
            device_id=device, device_id_type=MESH,
        )


    def rows_in(owner, chunk):
        return pl.ds(pl.multiple_of(owner * count + chunk * part, part), part)

    near_copies = {}
    for chunk in range(chunks):
        rows = pl.ds(chunk * part, part)
        for k, to in enumerate(order):
            theirs = merged_ref.at[rows_in(to * 2 + (1 - core), chunk), :]
            copy = remote(
                theirs, near_got.at[k, rows, :], near_sems, (k, chunk), (group, other)
            )
            copy.start()
            near_copies[k, chunk] = copy
    far_copies = {}
    for copy in mine_copies:
        copy.wait()
    for chunk in range(chunks):
        rows = pl.ds(chunk * part, part)
        for k in range(chips - 1):
            near_copies[k, chunk].wait_recv()
            total = mine[k, rows, :].astype(jnp.float32)
            total = total + near_got[k, rows, :].astype(jnp.float32)
            far_out[k, rows, :] = total.astype(jnp.bfloat16)
            copy = remote(
                far_out.at[k, rows, :], far_got.at[k, rows, :], far_sems, (k, chunk),
                (group, ahead[k]),
            )
            copy.start()
            far_copies[k, chunk] = copy

    def backward(base, hidden_half):
        here = pl.ds(base, step)
        span = blocks * 128
        lanes = pl.ds(pl.multiple_of(hidden_half * span, span), span)
        features = features_ref[here, :]
        grads = grad_rows[here, :]
        pre_act = (
            jnp.dot(features, w_in_ref[:, lanes], preferred_element_type=jnp.float32)
            + b_in_ref[:, lanes]
        )
        sigmoid_pre = jax.nn.sigmoid(pre_act)
        hidden = (pre_act * sigmoid_pre).astype(jnp.bfloat16)
        out_grad = tile_grad(grads, hidden)
        hidden_grad = tile_scores(grads, w_out_ref[lanes, :])
        pre_grad = hidden_grad * sigmoid_pre * (1.0 + pre_act * (1.0 - sigmoid_pre))
        bias = jnp.sum(pre_grad, axis=0, keepdims=True)
        in_grad = tile_grad(features, pre_grad.astype(jnp.bfloat16))
        for b in range(blocks):
            cols = slice(b * 128, (b + 1) * 128)
            at = hidden_half * blocks + b
            acc[at, 0:width, :] += in_grad[:, cols]
            acc[at, width : 2 * width, :] += out_grad[:, cols]
            bias_acc[pl.ds(at, 1), :] += bias[:, cols]

    half_copy = remote(half_out, half_got, half_sems, 0, (group, other))
    bias_copy = remote(bias_acc, bias_other, bias_sems, 0, (group, other))
    node_copies = []
    for copy in reads:
        copy.wait()
    for chunk in range(chunks):
        rows = pl.ds(chunk * part, part)
        near_copies[chips - 1, chunk].wait_recv()
        total = mine[chips - 1, rows, :].astype(jnp.float32)
        total = total + near_got[chips - 1, rows, :].astype(jnp.float32)
        for k in range(chips - 1):
            far_copies[k, chunk].wait_recv()
            total = total + far_got[k, rows, :].astype(jnp.float32)
        node_ref[rows, :] = total
        copy = pltpu.make_async_copy(
            node_ref.at[rows, :], node_out.at[rows, :], node_sems.at[chunk]
        )
        copy.start()
        node_copies.append(copy)
        embedding = embedding_ref[rows, :]
        spread = jnp.sqrt(jnp.mean(embedding * embedding, axis=1, keepdims=True) + EPSILON)
        normed = embedding / spread
        grads = (total - normed * jnp.mean(total * normed, axis=1, keepdims=True)) / spread
        grad_rows[rows, :] = grads.astype(jnp.bfloat16)
        for side in (1 - core, core):
            each(0, part // step, lambda k: backward(chunk * part + k * step, side))
            if chunk == chunks - 1 and side is not core:
                for b in range(blocks):
                    half_out[b] = acc[side * blocks + b].astype(jnp.bfloat16)
                half_copy.start()
    bias_copy.start()
    half_copy.wait_recv()

    def shard_at(index):
        block = index // per_block
        row = pl.ds(pl.multiple_of(lax.rem(index, per_block) * shard, shard), shard)
        mine = acc[core * blocks + block, row, :]
        return mine + half_got[block, row, :].astype(jnp.float32)

    def shard_copy(k):
        return remote(
            shard_out.at[k], shard_got.at[k], shard_sems, k, at_unit(unit_after(k))
        )

    def bias_all_copy(k):
        rows = bias_all.at[unit]
        return remote(rows, rows, bias_all_sems, k, at_unit(unit_after(k)))

    def gather_copy(k):
        rows = gathered.at[core, unit]
        return remote(rows, rows, gather_sems, k, at_unit(unit_after(k)))

    def pass_copy(k):
        rows = gathered.at[core, unit_before(k)]
        return remote(rows, rows, pass_sems, k, (group, other))

    def send_shard(k):
        shard_out[k] = shard_at(unit_after(k)).astype(jnp.bfloat16)
        shard_copy(k).start()

    each(0, units - 1, send_shard)
    bias_copy.wait_recv()
    bias_all[unit] = bias_acc[...] + bias_other[...]
    each(0, units - 1, lambda k: bias_all_copy(k).start())

    def add_shard(k, total):
        shard_copy(k).wait_recv()
        return total + shard_got[k].astype(jnp.float32)

    total = lax.fori_loop(0, units - 1, add_shard, shard_at(unit))
    scale = 1.0 / (groups * doms)
    gathered[core, unit] = (total * scale).astype(jnp.bfloat16)
    each(0, units - 1, lambda k: gather_copy(k).start())
    pass_copy(units - 1).start()

    def pass_on(k):
        gather_copy(k).wait_recv()
        pass_copy(k).start()

    each(0, units - 1, lambda k: bias_all_copy(k).wait_recv())
    bias_ref[...] = lax.fori_loop(
        1, units, lambda k, total: total + bias_all[k], bias_all[0]
    ) * scale
    each(0, units - 1, pass_on)

    each(0, units, lambda k: pass_copy(k).wait_recv())
    for copy in node_copies:
        copy.wait()
    for copy in list(near_copies.values()) + list(far_copies.values()) + [half_copy, bias_copy]:
        copy.wait_send()

    def drain(k):
        shard_copy(k).wait_send()
        bias_all_copy(k).wait_send()
        gather_copy(k).wait_send()
        pass_copy(k).wait_send()

    each(0, units - 1, drain)
    pass_copy(units - 1).wait_send()


def lay_out_kernel(
    node_ref, bias_ref, gathered_ref, node_out, in_out, bias_out, out_out,
    in_rows, out_rows, node_sem, in_sems, out_sems,
):
    width = out_out.shape[1]
    blocks = bias_ref.shape[0]
    copies = [pltpu.make_async_copy(node_ref, node_out, node_sem.at[0])]
    copies[0].start()
    for b in range(blocks):
        rows = gathered_ref[b].astype(jnp.float32)
        in_rows[b] = rows[0:width]
        out_rows[b] = rows[width : 2 * width].T
        span = pl.ds(b * 128, 128)
        copies.append(pltpu.make_async_copy(in_rows.at[b], in_out.at[:, span], in_sems.at[b]))
        copies.append(pltpu.make_async_copy(out_rows.at[b], out_out.at[span, :], out_sems.at[b]))
        copies[-2].start()
        copies[-1].start()
        bias_out[span] = bias_ref[b, :]
    for copy in copies:
        copy.wait()


def lay_out(node_grad, bias, gathered):
    count, width = node_grad.shape
    blocks = bias.shape[0]
    dma = pltpu.SemaphoreType.DMA
    return pl.pallas_call(
        lay_out_kernel,
        out_shape=(
            jax.ShapeDtypeStruct((count, width), jnp.float32),
            jax.ShapeDtypeStruct((width, blocks * 128), jnp.float32),
            jax.ShapeDtypeStruct((blocks * 128,), jnp.float32),
            jax.ShapeDtypeStruct((blocks * 128, width), jnp.float32),
        ),
        in_specs=[IN_VMEM] * 3,
        out_specs=(ANYWHERE, ANYWHERE, IN_VMEM, ANYWHERE),
        scratch_shapes=[
            pltpu.VMEM((blocks, width, 128), jnp.float32),
            pltpu.VMEM((blocks, 128, width), jnp.float32),
            dma((1,)),
            dma((blocks,)),
            dma((blocks,)),
        ],
        compiler_params=pltpu.CompilerParams(vmem_limit_bytes=VMEM_LIMIT // 4),
    )(node_grad, bias, gathered)


def finish(merged, embedding, features, w_in, b_in, w_out, groups, doms):
    count, width = embedding.shape
    hid = w_out.shape[0]
    chips = doms // 2
    units = groups * chips
    chunks = 8
    blocks = hid // 128
    shard = hid * 2 * width // (2 * 128) // units
    far = max(chips - 1, 1)
    half = jnp.bfloat16
    dma = pltpu.SemaphoreType.DMA

    def pair(*shape):
        return [dma(shape), dma(shape)]

    node_grad, bias, gathered = pl.pallas_call(
        functools.partial(finish_kernel, groups, doms, chunks),
        out_shape=(
            jax.ShapeDtypeStruct((count, width), jnp.float32),
            jax.ShapeDtypeStruct((blocks, 128), jnp.float32),
            jax.ShapeDtypeStruct((2, units, shard, 128), half),
        ),
        in_specs=[ANYWHERE] * 4 + [IN_VMEM, ANYWHERE],
        out_specs=(ANYWHERE, IN_VMEM, IN_VMEM),
        scratch_shapes=[
            pltpu.VMEM((chips, count, width), half),
            pltpu.VMEM((count, width), jnp.float32),
            pltpu.VMEM(features.shape, half),
            pltpu.VMEM(w_in.shape, half),
            pltpu.VMEM(w_out.shape, half),
            pltpu.VMEM((count, width), jnp.float32),
            dma((chips,)),
            dma((4,)),
            dma((chunks,)),
            pltpu.VMEM((chips, count, width), half),
            pltpu.VMEM((far, count, width), half),
            pltpu.VMEM((far, count, width), half),
            pltpu.VMEM((count, width), half),
            pltpu.VMEM((blocks, 2 * width, 128), jnp.float32),
            pltpu.VMEM((blocks, 128), jnp.float32),
            pltpu.VMEM((blocks, 128), jnp.float32),
            pltpu.VMEM((units, blocks, 128), jnp.float32),
            pltpu.VMEM((blocks // 2, 2 * width, 128), half),
            pltpu.VMEM((blocks // 2, 2 * width, 128), half),
            pltpu.VMEM((units - 1, shard, 128), half),
            pltpu.VMEM((units - 1, shard, 128), half),
            pair(chips, chunks),
            pair(far, chunks),
            pair(1),
            pair(1),
            pair(units - 1),
            pair(units - 1),
            pair(units - 1),
            pair(units),
        ],
        compiler_params=pltpu.CompilerParams(
            collective_id=1, has_side_effects=True, vmem_limit_bytes=VMEM_LIMIT // 2
        ),
    )(merged, embedding, features, w_in, b_in.reshape(1, -1), w_out)
    return lay_out(node_grad, bias, gathered.reshape(blocks, 2 * width, 128))


def shards(
    features, w_in, b_in, w_out, anchor_ids, local_tiles, requests, counts, remote_refs, teacher
):
    groups = lax.axis_size("group")
    doms = lax.axis_size("dom")
    devices = groups * doms
    own_requests = requests[0, 0]
    own_counts = counts[0, 0]
    slot_count = own_requests.shape[1]
    per_step = math.gcd(local_tiles.shape[0], 4)
    table, fetched, embedding, asked, prepared = fetch_tiles(
        per_step, features, w_in, b_in, w_out, own_requests, anchor_ids, local_tiles,
        remote_refs, own_counts, teacher, groups, doms,
    )
    anchor_kl, inverse, delta, remote_grad = score(
        math.gcd(local_tiles.shape[0], 8), remote_refs, own_counts, fetched, prepared, slot_count
    )
    anchor_kl = anchor_kl.reshape(-1)
    returned = lax.all_to_all(remote_grad, "group", split_axis=0, concat_axis=0, tiled=True)
    local_grad = local_grads(
        per_step, anchor_ids, local_tiles, remote_refs, table, fetched, prepared[0], prepared[1],
        inverse, delta,
    )
    merged = merge(asked, local_grad, returned)
    node_grad, in_grad, bias_grad, out_grad = finish(
        merged, embedding, features, w_in, b_in, w_out, groups, doms
    )
    return anchor_kl, node_grad, in_grad, bias_grad, out_grad


def solution(mesh):
    return jax.shard_map(
        shards,
        mesh=mesh,
        in_specs=(
            P(("group", "dom"), None),
            P(),
            P(),
            P(),
            P(("group", "dom")),
            P(("group", "dom"), None),
            P("group", "dom", None, None),
            P("group", "dom", None),
            P(("group", "dom"), None),
            P(("group", "dom"), None),
        ),
        out_specs=(P(("group", "dom")), P(("group", "dom"), None), P(), P(), P()),
        check_vma=False,
    )
```

```python
import functools
import math

import jax
import jax.numpy as jnp
from jax import lax
from jax.experimental import pallas as pl
from jax.experimental.pallas import tpu as pltpu
from jax.sharding import PartitionSpec as P

TILE = 128
ABLK = 128

SCORE_SCALE = 8.0
EPSILON = 1e-06
VMEM_LIMIT = 60 * 1024 * 1024
CHUNK = 256

ONE_COPY = pl.Buffered(1)


def whole(shape):
    return pl.BlockSpec(shape, lambda *_: (0,) * len(shape), pipeline_mode=ONE_COPY)


def node_rows(feature_rows, w_in, b_in, w_out):
    pre_act = jnp.dot(feature_rows, w_in, preferred_element_type=jnp.float32) + b_in
    hidden = (pre_act * jax.nn.sigmoid(pre_act)).astype(jnp.bfloat16)
    embedding = jnp.dot(hidden, w_out, preferred_element_type=jnp.float32)
    spread = jnp.sqrt(jnp.mean(embedding * embedding, axis=1, keepdims=True) + EPSILON)
    return embedding, (embedding / spread).astype(jnp.bfloat16)


def rows_of(index, count=TILE):
    return pl.ds(pl.multiple_of(index * count, count), count)


def cost(flops, moved, powers):
    return pl.CostEstimate(flops=flops, bytes_accessed=moved, transcendentals=powers)


def clear_rows(ref):
    zero_chunk = jnp.zeros((CHUNK, ref.shape[1]), ref.dtype)

    def clear(index, carry):
        ref[rows_of(index, CHUNK), :] = zero_chunk
        return carry

    lax.fori_loop(0, ref.shape[0] // CHUNK, clear, 0)


def tile_scores(anchors, context):
    return lax.dot_general(
        anchors, context, (((1,), (1,)), ((), ())), preferred_element_type=jnp.float32
    )


def prepare_block(
    scale, shapes, block, rows, teacher_rows, ids_ref, tiles_ref, refs_ref, counts_ref,
    table, table_f, anchor_rows, context, near_rows, far_rows,
):
    local_count, remote_count, slot_count = shapes

    def gather(index, carry):
        for lane in range(16):
            row = index * 16 + lane
            anchor_rows[row, :] = table_f[ids_ref[block * ABLK + row], :]
        return carry

    lax.fori_loop(0, ABLK // 16, gather, 0)
    anchors = (anchor_rows[...] * scale).astype(jnp.bfloat16)
    for i in range(local_count):
        context[i * TILE : (i + 1) * TILE, :] = table[tiles_ref[i, block]]
    all_scores = tile_scores(anchors, context[...])
    target_sum = gap_sum = student_sum = None
    exps = []
    for i in range(local_count + remote_count):
        teacher = teacher_rows[rows, i * TILE : (i + 1) * TILE].astype(jnp.float32)
        target_exp = jnp.exp(teacher)
        if i >= local_count:
            ref = refs_ref[i - local_count, block]
            live = lax.rem(ref, slot_count) < counts_ref[lax.div(ref, slot_count)]
            target_exp = target_exp * jnp.where(live, 1.0, 0.0).astype(jnp.float32)
            gap = target_exp * teacher
        else:
            scores = all_scores[:, i * TILE : (i + 1) * TILE]
            gap = target_exp * (teacher - scores)
            student_exp = jnp.exp(scores)
            student_sum = student_exp if i == 0 else student_sum + student_exp
        target_sum = target_exp if i == 0 else target_sum + target_exp
        gap_sum = gap if i == 0 else gap_sum + gap
        exps.append(target_exp)
    total = jnp.sum(target_sum.T, axis=0, keepdims=True)
    inverse = 1.0 / total
    base = jnp.sum(gap_sum.T, axis=0, keepdims=True) * inverse - jnp.log(total)
    spread_inverse = jnp.broadcast_to(inverse, (TILE, ABLK)).T
    for i, target_exp in enumerate(exps):
        out, at = (near_rows, i) if i < local_count else (far_rows, i - local_count)
        out[rows, at * TILE : (at + 1) * TILE] = (target_exp * spread_inverse).astype(
            jnp.bfloat16
        )
    return anchors, base, jnp.sum(student_sum.T, axis=0, keepdims=True)


def take_context(block, sub, context, tiles_ref, refs_ref, table_ref, fetched_ref, counts):
    local_count, remote_count = counts
    places = []
    for i in range(local_count):
        place = rows_of(tiles_ref[i, block])
        context[sub, i * TILE : (i + 1) * TILE, :] = table_ref[place, :]
        places.append(place)
    for i in range(remote_count):
        place = rows_of(refs_ref[i, block])
        at = local_count + i
        context[sub, at * TILE : (at + 1) * TILE, :] = fetched_ref[place, :]
        places.append(place)
    return places


def tile_grad(delta, anchors):
    return lax.dot_general(
        delta, anchors, (((0,), (0,)), ((), ())), preferred_element_type=jnp.float32
    )


def score_kernel(
    per_step, remote_count, slot_count, refs_ref, counts_ref,
    fetched_ref, anchors_ref, far_ref, base_ref, partial_ref,
    kl_ref, inverse_ref, delta_ref, remote_grad_ref, remote_acc, context,
):
    @pl.when(pl.program_id(0) == 0)
    def _():
        clear_rows(remote_acc)

    for sub in range(per_step):
        block = pl.program_id(0) * per_step + sub
        rows = slice(sub * ABLK, (sub + 1) * ABLK)
        anchors = anchors_ref[rows, :]
        places = []
        lives = []
        for i in range(remote_count):
            ref = refs_ref[i, block]
            places.append(rows_of(ref))
            live = lax.rem(ref, slot_count) < counts_ref[lax.div(ref, slot_count)]
            lives.append(jnp.where(live, 1.0, 0.0).astype(jnp.float32))
            context[sub, i * TILE : (i + 1) * TILE, :] = fetched_ref[places[i], :]
        all_scores = tile_scores(anchors, context[sub])
        student = []
        student_sum = gap_sum = None
        for i in range(remote_count):
            span = slice(i * TILE, (i + 1) * TILE)
            scores = all_scores[:, span]
            student_exp = jnp.exp(scores) * lives[i]
            gap = far_ref[rows, span].astype(jnp.float32) * scores
            student_sum = student_exp if i == 0 else student_sum + student_exp
            gap_sum = gap if i == 0 else gap_sum + gap
            student.append(student_exp)
        total = partial_ref[sub] + jnp.sum(student_sum.T, axis=0, keepdims=True)
        inverse = 1.0 / total
        kl_ref[sub] = base_ref[sub] + jnp.log(total) - jnp.sum(gap_sum.T, axis=0, keepdims=True)
        inverse_ref[sub] = inverse
        spread_inverse = jnp.broadcast_to(inverse, (TILE, ABLK)).T
        for i in range(remote_count):
            span = slice(i * TILE, (i + 1) * TILE)
            delta = (student[i] * spread_inverse - far_ref[rows, span].astype(jnp.float32)).astype(
                jnp.bfloat16
            )
            delta_ref[rows, span] = delta
        grads = tile_grad(delta_ref[rows, :], anchors)
        for i in range(remote_count):
            remote_acc[places[i], :] += grads[i * TILE : (i + 1) * TILE]

    @pl.when(pl.program_id(0) == pl.num_programs(0) - 1)
    def _():
        def finish(index, carry):
            here = rows_of(index, CHUNK)
            remote_grad_ref[here, :] = remote_acc[here, :].astype(jnp.bfloat16)
            return carry

        lax.fori_loop(0, remote_acc.shape[0] // CHUNK, finish, 0)


def score(per_step, remote_refs, own_counts, fetched, prepared, slots):
    anchors, near, far, base, partial = prepared
    blocks, remote_count = remote_refs.shape
    width = anchors.shape[1]
    rows = per_step * ABLK
    pairs = far.shape[0] * far.shape[1]
    row_spec = pl.BlockSpec((per_step, 1, ABLK), lambda b, *_: (b, 0, 0))
    far_spec = pl.BlockSpec((rows, far.shape[1]), lambda b, *_: (b, 0))
    return pl.pallas_call(
        functools.partial(score_kernel, per_step, remote_count, slots),
        out_shape=(
            jax.ShapeDtypeStruct((blocks, 1, ABLK), jnp.float32),
            jax.ShapeDtypeStruct((blocks, 1, ABLK), jnp.float32),
            jax.ShapeDtypeStruct(far.shape, jnp.bfloat16),
            jax.ShapeDtypeStruct(fetched.shape, jnp.bfloat16),
        ),
        grid_spec=pltpu.PrefetchScalarGridSpec(
            num_scalar_prefetch=2,
            grid=(blocks // per_step,),
            in_specs=[
                whole(fetched.shape),
                pl.BlockSpec((rows, width), lambda b, *_: (b, 0)),
                far_spec,
                row_spec,
                row_spec,
            ],
            out_specs=(row_spec, row_spec, far_spec, whole(fetched.shape)),
            scratch_shapes=[
                pltpu.VMEM(fetched.shape, jnp.float32),
                pltpu.VMEM((per_step, far.shape[1], width), jnp.bfloat16),
            ],
        ),
        compiler_params=pltpu.CompilerParams(vmem_limit_bytes=VMEM_LIMIT),
        cost_estimate=cost(3 * pairs * width, 4 * pairs, pairs),
    )(remote_refs.T, own_counts, fetched, anchors, far, base, partial)


def local_kernel(
    per_step, local_count, remote_count, lanes, ids_ref, tiles_ref, refs_ref,
    table_ref, fetched_ref, anchors_ref, near_ref, inverse_ref, delta_ref, local_out_ref,
    local_grad_ref, context, near_delta, anchor_grad, *row_accs,
):
    scale = SCORE_SCALE / table_ref.shape[1]

    @pl.when(pl.program_id(0) == 0)
    def _():
        clear_rows(local_grad_ref)
        for acc in row_accs:
            clear_rows(acc)

    for sub in range(per_step):
        block = pl.program_id(0) * per_step + sub
        rows = slice(sub * ABLK, (sub + 1) * ABLK)
        places = take_context(
            block, sub, context, tiles_ref, refs_ref, table_ref, fetched_ref,
            (local_count, remote_count),
        )
        anchors = anchors_ref[rows, :]
        spread_inverse = jnp.broadcast_to(inverse_ref[sub], (TILE, ABLK)).T
        near = local_count * TILE
        scores = tile_scores(anchors, context[sub, :near, :])
        for i in range(local_count):
            span = slice(i * TILE, (i + 1) * TILE)
            student = jnp.exp(scores[:, span]) * spread_inverse
            delta = (student - near_ref[rows, span].astype(jnp.float32)).astype(jnp.bfloat16)
            near_delta[rows, span] = delta
        grads = tile_grad(near_delta[rows, :], anchors)
        for i in range(local_count):
            local_grad_ref[places[i], :] += grads[i * TILE : (i + 1) * TILE]
        near_part = jnp.dot(
            near_delta[rows, :], context[sub, :near, :], preferred_element_type=jnp.float32
        )
        far_part = jnp.dot(
            delta_ref[rows, :], context[sub, near:, :], preferred_element_type=jnp.float32
        )
        anchor_grad[rows, :] = (near_part + far_part) * scale
        for row in range(ABLK):
            acc = row_accs[row % lanes]
            at = sub * ABLK + row
            acc[pl.ds(ids_ref[block * ABLK + row], 1), :] += anchor_grad[at : at + 1, :]

    @pl.when(pl.program_id(0) == pl.num_programs(0) - 1)
    def _():
        def finish(index, carry):
            here = rows_of(index, CHUNK)
            total = local_grad_ref[here, :]
            for acc in row_accs:
                total = total + acc[here, :]
            local_out_ref[here, :] = total.astype(jnp.bfloat16)
            return carry

        lax.fori_loop(0, local_grad_ref.shape[0] // CHUNK, finish, 0)


def local_grads(
    per_step, anchor_ids, local_tiles, remote_refs, table, fetched, anchors, near, inverse, delta
):
    blocks, local_count = local_tiles.shape
    remote_count = remote_refs.shape[1]
    context_width = near.shape[1] + delta.shape[1]
    width = table.shape[1]
    rows = per_step * ABLK
    lanes = 4 if table.shape[0] <= 8192 else 1
    pairs = delta.shape[0] * context_width
    return pl.pallas_call(
        functools.partial(local_kernel, per_step, local_count, remote_count, lanes),
        out_shape=jax.ShapeDtypeStruct(table.shape, jnp.bfloat16),
        grid_spec=pltpu.PrefetchScalarGridSpec(
            num_scalar_prefetch=3,
            grid=(blocks // per_step,),
            in_specs=[
                whole(table.shape),
                whole(fetched.shape),
                pl.BlockSpec((rows, width), lambda b, *_: (b, 0)),
                pl.BlockSpec((rows, near.shape[1]), lambda b, *_: (b, 0)),
                pl.BlockSpec((per_step, 1, ABLK), lambda b, *_: (b, 0, 0)),
                pl.BlockSpec((rows, delta.shape[1]), lambda b, *_: (b, 0)),
            ],
            out_specs=whole(table.shape),
            scratch_shapes=[
                pltpu.VMEM(table.shape, jnp.float32),
                pltpu.VMEM((per_step, context_width, width), jnp.bfloat16),
                pltpu.VMEM((rows, near.shape[1]), jnp.bfloat16),
                pltpu.VMEM((rows, width), jnp.float32),
            ]
            + [pltpu.VMEM(table.shape, jnp.float32)] * lanes,
        ),
        compiler_params=pltpu.CompilerParams(vmem_limit_bytes=VMEM_LIMIT),
        cost_estimate=cost(3 * pairs * width, 2 * pairs, 0),
    )(
        anchor_ids, local_tiles.T, remote_refs.T,
        table, fetched, anchors, near, inverse, delta,
    )


def merge_kernel(
    pieces, asked_ref, local_ref, returned_ref, out_ref,
    acc, local, returned, merged, local_sems, returned_sems, out_sems,
):
    def copies(src, dst, sems):
        count = src.shape[0] // pieces
        return [
            pltpu.make_async_copy(
                src.at[pl.ds(c * count, count)], dst.at[pl.ds(c * count, count)], sems.at[c]
            )
            for c in range(pieces)
        ]

    local_in = copies(local_ref, local, local_sems)
    returned_in = copies(returned_ref, returned, returned_sems)
    merged_out = copies(merged, out_ref, out_sems)
    for copy in returned_in + local_in:
        copy.start()
    tiles = acc.shape[0] // pieces
    for c in range(pieces):
        local_in[c].wait()

        def widen(index, carry):
            here = pl.ds(c * tiles + index * 4, 4)
            acc[here] = local[here].astype(jnp.float32)
            return carry

        lax.fori_loop(0, tiles // 4, widen, 0)
    slots = returned.shape[0] // pieces
    for c in range(pieces):
        returned_in[c].wait()

        def add(index, carry):
            slot = c * slots + index
            acc[asked_ref[slot]] += returned[slot].astype(jnp.float32)
            return carry

        lax.fori_loop(0, slots, add, 0, unroll=4)
    for c in range(pieces):
        def narrow(index, carry):
            here = pl.ds(c * tiles + index * 4, 4)
            merged[here] = acc[here].astype(jnp.bfloat16)
            return carry

        lax.fori_loop(0, tiles // 4, narrow, 0)
        merged_out[c].start()
    for copy in merged_out:
        copy.wait()


def merge(asked, local_grad, returned):
    pieces = 4
    rows, width = local_grad.shape
    local_grad = local_grad.reshape(-1, TILE, width)
    returned = returned.reshape(-1, TILE, width)
    dma = pltpu.SemaphoreType.DMA
    return pl.pallas_call(
        functools.partial(merge_kernel, pieces),
        out_shape=jax.ShapeDtypeStruct(local_grad.shape, jnp.bfloat16),
        in_specs=[pl.BlockSpec(memory_space=pltpu.SMEM), ANYWHERE, ANYWHERE],
        out_specs=ANYWHERE,
        scratch_shapes=[
            pltpu.VMEM(local_grad.shape, jnp.float32),
            pltpu.VMEM(local_grad.shape, jnp.bfloat16),
            pltpu.VMEM(returned.shape, jnp.bfloat16),
            pltpu.VMEM(local_grad.shape, jnp.bfloat16),
            dma((pieces,)),
            dma((pieces,)),
            dma((pieces,)),
        ],
        compiler_params=pltpu.CompilerParams(vmem_limit_bytes=12 * local_grad.size),
    )(asked, local_grad, returned).reshape(rows, width)


MESH = pl.DeviceIdType.MESH
ANYWHERE = pl.BlockSpec(memory_space=pl.ANY)
IN_VMEM = pl.BlockSpec(memory_space=pltpu.VMEM)


def greet(partners):
    barrier = pltpu.get_barrier_semaphore()
    for partner in partners:
        pl.semaphore_signal(barrier, inc=1, device_id=partner, device_id_type=MESH)
    pl.semaphore_wait(barrier, len(partners))


def dom_partners(doms):
    group, dom = lax.axis_index("group"), lax.axis_index("dom")
    chips = doms // 2
    chip, core = dom // 2, dom % 2
    other = chip * 2 + (1 - core)
    ahead = [lax.rem(chip + k, chips) * 2 + core for k in range(1, chips)]
    behind = [lax.rem(chip + chips - k, chips) for k in range(1, chips)]
    return group, dom, core, other, ahead, behind


def fetch_kernel(
    groups, doms, chunks, per_step, shapes,
    features_in, w_in_in, b_in_ref, w_out_in, requests_ref, own_asks,
    ids_ref, tiles_ref, refs_ref, counts_ref, teacher_ref,
    table_ref, fetched_ref, embedding_out, asked_ref,
    anchors_ref, near_ref, far_ref, base_ref, partial_ref,
    table, relay, served, blank, ask_out, ask_in, asked,
    features_ref, w_in_ref, w_out_ref, read_sems,
    table_f, anchor_rows, context, embedding_ref, teacher_buf, near_buf, far_buf, anchor_buf,
    in_sems, near_out_sems, far_out_sems, anchor_out_sems,
    near_sems, far_sems, on_sems, swap_sems, relay_near, relay_far, relay_on,
    ask_sems, serve_sems, relay_serve, own_sems,
):
    group, dom, core, other, ahead, behind = dom_partners(doms)
    half = groups // 2
    slots = requests_ref.shape[1]
    count = features_in.shape[0]
    part = count // chunks
    step = min(CHUNK, part)
    first = group // half * half
    place = lax.rem(group, half)
    mates = [first + lax.rem(place + k, half) for k in range(1, half)]
    partner = lax.rem(group + half, groups)
    peers = [lax.rem(group + k, groups) for k in range(1, groups)]
    steps = teacher_ref.shape[0] // (per_step * ABLK)
    step_rows = per_step * ABLK

    def teacher_in(index):
        return pltpu.make_async_copy(
            teacher_ref.at[rows_of(index, step_rows), :],
            teacher_buf.at[lax.rem(index, 2)],
            in_sems.at[lax.rem(index, 2)],
        )

    def targets_out(index):
        at = lax.rem(index, 2)
        rows = rows_of(index, step_rows)
        return (
            pltpu.make_async_copy(near_buf.at[at], near_ref.at[rows, :], near_out_sems.at[at]),
            pltpu.make_async_copy(far_buf.at[at], far_ref.at[rows, :], far_out_sems.at[at]),
            pltpu.make_async_copy(
                anchor_buf.at[at], anchors_ref.at[rows, :], anchor_out_sems.at[at]
            ),
        )

    def prepare_step(index, carry):
        at = lax.rem(index, 2)
        teacher_in(index).wait()

        @pl.when(index + 1 < steps)
        def _():
            teacher_in(index + 1).start()

        @pl.when(index >= 2)
        def _():
            for copy in targets_out(index - 2):
                copy.wait()

        for sub in range(per_step):
            block = index * per_step + sub
            anchors, base, partial = prepare_block(
                SCORE_SCALE / table.shape[2], shapes, block, pl.ds(sub * ABLK, ABLK),
                teacher_buf.at[at], ids_ref, tiles_ref, refs_ref, counts_ref,
                table, table_f, anchor_rows.at[sub], context.at[sub], near_buf.at[at],
                far_buf.at[at],
            )
            anchor_buf[at, sub * ABLK : (sub + 1) * ABLK, :] = anchors
            base_ref[block] = base
            partial_ref[block] = partial
        for copy in targets_out(index):
            copy.start()
        return carry

    reads = [
        pltpu.make_async_copy(src, dst, read_sems.at[k])
        for k, (src, dst) in enumerate(
            [(features_in, features_ref), (w_in_in, w_in_ref), (w_out_in, w_out_ref)]
        )
    ]
    for copy in reads:
        copy.start()
    teacher_in(0).start()
    greet(
        [(group, other)] + [(group, far) for far in ahead]
        + [(peer, dom) for peer in peers]
    )

    tiles = part // TILE

    def span(owner, chunk):
        return pl.ds(owner * (count // TILE) + chunk * tiles, tiles)

    def both(sems, *index):
        return sems[0].at[index], sems[1].at[index]

    def send(src, dst, sems, partner_at):
        copy = pltpu.make_async_remote_copy(
            src_ref=src, dst_ref=dst, send_sem=sems[0], recv_sem=sems[1],
            device_id=partner_at, device_id_type=MESH,
        )
        copy.start()
        return copy

    def spread_chunk(here, owner, chunk, near, far):
        rows = here.at[span(owner, chunk)]
        far_copies = [
            send(rows, rows, both(far, k, chunk), (group, there)) for k, there in enumerate(ahead)
        ]
        return far_copies, send(rows, rows, both(near, chunk), (group, other))

    def pass_on(here, far_copies, chunk, on):
        copies = []
        for k, copy in enumerate(far_copies):
            copy.wait_recv()
            rows = here.at[span(behind[k] * 2 + core, chunk)]
            copies.append(send(rows, rows, both(on, k, chunk), (group, other)))
        return copies

    ask_out[...] = jnp.zeros_like(ask_out)
    ask_out[:, 0:slots] = requests_ref[...]
    asks = [
        send(ask_out, ask_in.at[group], both(ask_sems, k), (peer, dom))
        for k, peer in enumerate(peers)
    ]
    ask_in[group] = ask_out[...]
    blank[...] = jnp.zeros_like(blank)
    sent = []
    far_copies, near_copies, swaps = [], [], []
    for copy in reads:
        copy.wait()
    for chunk in range(chunks):
        def forward(index, carry):
            at = pl.ds(pl.multiple_of(chunk * part + index * step, step), step)
            embedding, unit_rows = node_rows(
                features_ref[at, :], w_in_ref[...], b_in_ref[...], w_out_ref[...]
            )
            embedding_ref[at, :] = embedding
            to = pl.ds((dom * count + chunk * part) // TILE + index * (step // TILE), step // TILE)
            table[to] = unit_rows.reshape(step // TILE, TILE, unit_rows.shape[1])
            return carry

        lax.fori_loop(0, part // step, forward, 0)
        rows = span(dom, chunk)
        swaps.append(
            send(table.at[rows], relay.at[rows], both(swap_sems, chunk), (partner, dom))
        )
        far, near = spread_chunk(table, dom, chunk, near_sems, far_sems)
        far_copies.append(far)
        near_copies.append(near)
    clear = pltpu.make_async_copy(blank, fetched_ref.at[pl.ds(group * slots, slots)], own_sems.at[0])
    clear.start()
    on_copies, relay_fars, relay_nears, relay_ons = [], [], [], []

    def relay_chunk(chunk):
        swaps[chunk].wait_recv()
        far, near = spread_chunk(relay, dom, chunk, relay_near, relay_far)
        relay_fars.append(far)
        relay_nears.append(near)

    for chunk in range(chunks):
        on_copies += pass_on(table, far_copies[chunk], chunk, on_sems)
    keep_embedding = pltpu.make_async_copy(embedding_ref, embedding_out, own_sems.at[4])
    keep_embedding.start()
    relay_chunk(0)
    relay_chunk(1)
    for copy in asks:
        copy.wait_recv()
    read_asks = pltpu.make_async_copy(ask_in, asked, own_sems.at[1])
    read_asks.start()
    asked_ref[...] = ask_in[...]
    for copy in on_copies + near_copies:
        copy.wait_recv()
    keep = pltpu.make_async_copy(table, table_ref, own_sems.at[2])
    keep.start()
    read_asks.wait()

    def serve(here, base, asked_of):
        for k in range(half - 1):
            source = mates[k]

            def pick(slot, carry):
                wanted = asked[source, asked_of, slot]
                served[base + k, slot] = here[wanted]
                return carry

            lax.fori_loop(0, slots, pick, 0)

    def push_served(base, asked_of, sems):
        return [
            send(
                served.at[base + k], fetched_ref.at[pl.ds(asked_of * slots, slots)], both(sems, k),
                (mate, dom),
            )
            for k, mate in enumerate(mates)
        ]

    serve(table, 0, group)
    sent += push_served(0, group, serve_sems)

    def widen(index, carry):
        table_f[rows_of(index), :] = table[index].astype(jnp.float32)
        return carry

    lax.fori_loop(0, table.shape[0], widen, 0)
    bounds = [steps * part // 8 for part in (0, 1, 3, 4, 8)]

    def prepare(segment):
        lax.fori_loop(bounds[segment], bounds[segment + 1], prepare_step, 0)

    def relay_pass(chunk):
        return pass_on(relay, relay_fars[chunk], chunk, relay_on)

    prepare(0)
    relay_chunk(2)
    relay_ons += relay_pass(0) + relay_pass(1)
    prepare(1)
    relay_chunk(3)
    relay_ons += relay_pass(2)
    prepare(2)
    relay_ons += relay_pass(3)
    for copy in relay_ons + relay_nears:
        copy.wait_recv()
    serve(relay, half - 1, partner)
    sent += push_served(half - 1, partner, relay_serve)

    def pick_own(slot, carry):
        wanted = own_asks[partner, slot]
        served[2 * half - 2, slot] = relay[wanted]
        return carry

    lax.fori_loop(0, slots, pick_own, 0)
    mine = pltpu.make_async_copy(
        served.at[2 * half - 2], fetched_ref.at[pl.ds(partner * slots, slots)], own_sems.at[3]
    )
    mine.start()
    prepare(3)
    for index in range(max(steps - 2, 0), steps):
        for copy in targets_out(index):
            copy.wait()
    for copy in sent:
        copy.wait_recv()
    clear.wait()
    keep.wait()
    keep_embedding.wait()
    mine.wait()
    for copy in asks + swaps + near_copies + on_copies + relay_nears + relay_ons + sent:
        copy.wait_send()
    for copies in far_copies + relay_fars:
        for copy in copies:
            copy.wait_send()


def fetch_tiles(
    per_step, features, w_in, b_in, w_out, own_requests, anchor_ids, local_tiles, remote_refs,
    own_counts, teacher, groups, doms,
):
    slots = own_requests.shape[1]
    count = features.shape[0]
    width = w_out.shape[1]
    chunks = 4
    half = groups // 2
    far, mates = max(doms // 2 - 1, 1), max(half - 1, 1)
    dma = pltpu.SemaphoreType.DMA
    nodes = doms * count
    blocks, remote_count = remote_refs.shape
    local_count = local_tiles.shape[1]
    near, far_width = local_count * TILE, remote_count * TILE
    anchors, context_width = teacher.shape
    rows = per_step * ABLK
    peers = max(groups - 1, 1)
    in_smem = pl.BlockSpec(memory_space=pltpu.SMEM)
    table, fetched, embedding, asked, *prepared = pl.pallas_call(
        functools.partial(
            fetch_kernel, groups, doms, chunks, per_step, (local_count, remote_count, slots)
        ),
        out_shape=(
            jax.ShapeDtypeStruct((nodes // TILE, TILE, width), jnp.bfloat16),
            jax.ShapeDtypeStruct((groups * slots, TILE, width), jnp.bfloat16),
            jax.ShapeDtypeStruct((count, width), jnp.float32),
            jax.ShapeDtypeStruct((groups, groups, 128), jnp.int32),
            jax.ShapeDtypeStruct((anchors, width), jnp.bfloat16),
            jax.ShapeDtypeStruct((anchors, near), jnp.bfloat16),
            jax.ShapeDtypeStruct((anchors, far_width), jnp.bfloat16),
            jax.ShapeDtypeStruct((blocks, 1, ABLK), jnp.float32),
            jax.ShapeDtypeStruct((blocks, 1, ABLK), jnp.float32),
        ),
        in_specs=[ANYWHERE, ANYWHERE, IN_VMEM, ANYWHERE, IN_VMEM] + [in_smem] * 5 + [ANYWHERE],
        out_specs=(
            ANYWHERE, ANYWHERE, ANYWHERE, IN_VMEM, ANYWHERE, ANYWHERE, ANYWHERE, IN_VMEM, IN_VMEM
        ),
        scratch_shapes=[
            pltpu.VMEM((nodes // TILE, TILE, width), jnp.bfloat16),
            pltpu.VMEM((nodes // TILE, TILE, width), jnp.bfloat16),
            pltpu.VMEM((2 * half - 1, slots, TILE, width), jnp.bfloat16),
            pltpu.VMEM((slots, TILE, width), jnp.bfloat16),
            pltpu.VMEM((groups, 128), jnp.int32),
            pltpu.VMEM((groups, groups, 128), jnp.int32),
            pltpu.SMEM((groups, groups, 128), jnp.int32),
            pltpu.VMEM(features.shape, jnp.bfloat16),
            pltpu.VMEM(w_in.shape, jnp.bfloat16),
            pltpu.VMEM(w_out.shape, jnp.bfloat16),
            dma((3,)),
            pltpu.VMEM((nodes, width), jnp.float32),
            pltpu.VMEM((per_step, ABLK, width), jnp.float32),
            pltpu.VMEM((per_step, near, width), jnp.bfloat16),
            pltpu.VMEM((count, width), jnp.float32),
            pltpu.VMEM((2, rows, context_width), jnp.bfloat16),
            pltpu.VMEM((2, rows, near), jnp.bfloat16),
            pltpu.VMEM((2, rows, far_width), jnp.bfloat16),
            pltpu.VMEM((2, rows, width), jnp.bfloat16),
            dma((2,)),
            dma((2,)),
            dma((2,)),
            dma((2,)),
            [dma((chunks,)), dma((chunks,))],
            [dma((far, chunks)), dma((far, chunks))],
            [dma((far, chunks)), dma((far, chunks))],
            [dma((chunks,)), dma((chunks,))],
            [dma((chunks,)), dma((chunks,))],
            [dma((far, chunks)), dma((far, chunks))],
            [dma((far, chunks)), dma((far, chunks))],
            [dma((peers,)), dma((peers,))],
            [dma((mates,)), dma((mates,))],
            [dma((mates,)), dma((mates,))],
            dma((5,)),
        ],
        compiler_params=pltpu.CompilerParams(
            collective_id=0, has_side_effects=True, vmem_limit_bytes=VMEM_LIMIT
        ),
    )(
        features, w_in, b_in.reshape(1, -1), w_out, own_requests, own_requests,
        anchor_ids, local_tiles.T, remote_refs.T, own_counts, teacher,
    )
    asked = lax.dynamic_index_in_dim(asked, lax.axis_index("group"), 1, keepdims=False)
    return (
        table.reshape(-1, width), fetched.reshape(-1, width), embedding,
        asked[:, :slots].reshape(-1), prepared,
    )


def finish_kernel(
    groups, doms, chunks, merged_ref, embedding_in, features_in, w_in_in, b_in_ref, w_out_in,
    node_out, bias_ref, gathered,
    mine, embedding_ref, features_ref, w_in_ref, w_out_ref, node_ref,
    mine_sems, read_sems, node_sems, near_got, far_out, far_got, grad_rows, acc, bias_acc, bias_other, bias_all,
    half_out, half_got, shard_out, shard_got,
    near_sems, far_sems, half_sems, bias_sems, shard_sems, bias_all_sems, gather_sems, pass_sems,
):
    group, dom, core, other, ahead, behind = dom_partners(doms)
    count, width = node_ref.shape
    chips = doms // 2
    chip = dom // 2
    units = groups * chips
    unit = group * chips + chip
    blocks = acc.shape[0] // 2
    shard = shard_got.shape[1]
    part = count // chunks
    step = min(CHUNK, part)
    per_block = acc.shape[1] // shard
    barrier = pltpu.get_barrier_semaphore()

    def at_unit(index):
        return (index // chips, lax.rem(index, chips) * 2 + core)

    def unit_after(k):
        return lax.rem(unit + k + 1, units)

    def unit_before(k):
        return lax.rem(unit + units - k - 1, units)

    def each(start, stop, work):
        def body(k, carry):
            work(k)
            return carry

        lax.fori_loop(start, stop, body, 0)

    def greet_unit(k):
        pl.semaphore_signal(
            barrier, inc=1, device_id=at_unit(unit_after(k)), device_id_type=MESH
        )

    order = [lax.rem(chip + k, chips) for k in range(1, chips)] + [chip]
    mine_copies = [
        pltpu.make_async_copy(
            merged_ref.at[rows_of(to * 2 + core, count), :], mine.at[k], mine_sems.at[k]
        )
        for k, to in enumerate(order)
    ]
    reads = [
        pltpu.make_async_copy(src, dst, read_sems.at[k])
        for k, (src, dst) in enumerate(
            [
                (embedding_in, embedding_ref), (features_in, features_ref),
                (w_in_in, w_in_ref), (w_out_in, w_out_ref),
            ]
        )
    ]
    pl.semaphore_signal(barrier, inc=1, device_id=(group, other), device_id_type=MESH)
    each(0, units - 1, greet_unit)
    for copy in mine_copies + reads:
        copy.start()
    acc[...] = jnp.zeros_like(acc)
    bias_acc[...] = jnp.zeros_like(bias_acc)
    pl.semaphore_wait(barrier, units)

    def remote(src, dst, sems, index, device):
        return pltpu.make_async_remote_copy(
            src_ref=src, dst_ref=dst, send_sem=sems[0].at[index], recv_sem=sems[1].at[index],
            device_id=device, device_id_type=MESH,
        )


    def rows_in(owner, chunk):
        return pl.ds(pl.multiple_of(owner * count + chunk * part, part), part)

    near_copies = {}
    for chunk in range(chunks):
        rows = pl.ds(chunk * part, part)
        for k, to in enumerate(order):
            theirs = merged_ref.at[rows_in(to * 2 + (1 - core), chunk), :]
            copy = remote(
                theirs, near_got.at[k, rows, :], near_sems, (k, chunk), (group, other)
            )
            copy.start()
            near_copies[k, chunk] = copy
    far_copies = {}
    for copy in mine_copies:
        copy.wait()
    for chunk in range(chunks):
        rows = pl.ds(chunk * part, part)
        for k in range(chips - 1):
            near_copies[k, chunk].wait_recv()
            total = mine[k, rows, :].astype(jnp.float32)
            total = total + near_got[k, rows, :].astype(jnp.float32)
            far_out[k, rows, :] = total.astype(jnp.bfloat16)
            copy = remote(
                far_out.at[k, rows, :], far_got.at[k, rows, :], far_sems, (k, chunk),
                (group, ahead[k]),
            )
            copy.start()
            far_copies[k, chunk] = copy

    def backward(base, hidden_half):
        here = pl.ds(base, step)
        span = blocks * 128
        lanes = pl.ds(pl.multiple_of(hidden_half * span, span), span)
        features = features_ref[here, :]
        grads = grad_rows[here, :]
        pre_act = (
            jnp.dot(features, w_in_ref[:, lanes], preferred_element_type=jnp.float32)
            + b_in_ref[:, lanes]
        )
        sigmoid_pre = jax.nn.sigmoid(pre_act)
        hidden = (pre_act * sigmoid_pre).astype(jnp.bfloat16)
        out_grad = tile_grad(grads, hidden)
        hidden_grad = tile_scores(grads, w_out_ref[lanes, :])
        pre_grad = hidden_grad * sigmoid_pre * (1.0 + pre_act * (1.0 - sigmoid_pre))
        bias = jnp.sum(pre_grad, axis=0, keepdims=True)
        in_grad = tile_grad(features, pre_grad.astype(jnp.bfloat16))
        for b in range(blocks):
            cols = slice(b * 128, (b + 1) * 128)
            at = hidden_half * blocks + b
            acc[at, 0:width, :] += in_grad[:, cols]
            acc[at, width : 2 * width, :] += out_grad[:, cols]
            bias_acc[pl.ds(at, 1), :] += bias[:, cols]

    half_copy = remote(half_out, half_got, half_sems, 0, (group, other))
    bias_copy = remote(bias_acc, bias_other, bias_sems, 0, (group, other))
    node_copies = []
    for copy in reads:
        copy.wait()
    for chunk in range(chunks):
        rows = pl.ds(chunk * part, part)
        near_copies[chips - 1, chunk].wait_recv()
        total = mine[chips - 1, rows, :].astype(jnp.float32)
        total = total + near_got[chips - 1, rows, :].astype(jnp.float32)
        for k in range(chips - 1):
            far_copies[k, chunk].wait_recv()
            total = total + far_got[k, rows, :].astype(jnp.float32)
        node_ref[rows, :] = total
        copy = pltpu.make_async_copy(
            node_ref.at[rows, :], node_out.at[rows, :], node_sems.at[chunk]
        )
        copy.start()
        node_copies.append(copy)
        embedding = embedding_ref[rows, :]
        spread = jnp.sqrt(jnp.mean(embedding * embedding, axis=1, keepdims=True) + EPSILON)
        normed = embedding / spread
        grads = (total - normed * jnp.mean(total * normed, axis=1, keepdims=True)) / spread
        grad_rows[rows, :] = grads.astype(jnp.bfloat16)
        for side in (1 - core, core):
            each(0, part // step, lambda k: backward(chunk * part + k * step, side))
            if chunk == chunks - 1 and side is not core:
                for b in range(blocks):
                    half_out[b] = acc[side * blocks + b].astype(jnp.bfloat16)
                half_copy.start()
    bias_copy.start()
    half_copy.wait_recv()

    def shard_at(index):
        block = index // per_block
        row = pl.ds(pl.multiple_of(lax.rem(index, per_block) * shard, shard), shard)
        mine = acc[core * blocks + block, row, :]
        return mine + half_got[block, row, :].astype(jnp.float32)

    def shard_copy(k):
        return remote(
            shard_out.at[k], shard_got.at[k], shard_sems, k, at_unit(unit_after(k))
        )

    def bias_all_copy(k):
        rows = bias_all.at[unit]
        return remote(rows, rows, bias_all_sems, k, at_unit(unit_after(k)))

    def gather_copy(k):
        rows = gathered.at[core, unit]
        return remote(rows, rows, gather_sems, k, at_unit(unit_after(k)))

    def pass_copy(k):
        rows = gathered.at[core, unit_before(k)]
        return remote(rows, rows, pass_sems, k, (group, other))

    def send_shard(k):
        shard_out[k] = shard_at(unit_after(k)).astype(jnp.bfloat16)
        shard_copy(k).start()

    each(0, units - 1, send_shard)
    bias_copy.wait_recv()
    bias_all[unit] = bias_acc[...] + bias_other[...]
    each(0, units - 1, lambda k: bias_all_copy(k).start())

    def add_shard(k, total):
        shard_copy(k).wait_recv()
        return total + shard_got[k].astype(jnp.float32)

    total = lax.fori_loop(0, units - 1, add_shard, shard_at(unit))
    scale = 1.0 / (groups * doms)
    gathered[core, unit] = (total * scale).astype(jnp.bfloat16)
    each(0, units - 1, lambda k: gather_copy(k).start())
    pass_copy(units - 1).start()

    def pass_on(k):
        gather_copy(k).wait_recv()
        pass_copy(k).start()

    each(0, units - 1, lambda k: bias_all_copy(k).wait_recv())
    bias_ref[...] = lax.fori_loop(
        1, units, lambda k, total: total + bias_all[k], bias_all[0]
    ) * scale
    each(0, units - 1, pass_on)

    each(0, units, lambda k: pass_copy(k).wait_recv())
    for copy in node_copies:
        copy.wait()
    for copy in list(near_copies.values()) + list(far_copies.values()) + [half_copy, bias_copy]:
        copy.wait_send()

    def drain(k):
        shard_copy(k).wait_send()
        bias_all_copy(k).wait_send()
        gather_copy(k).wait_send()
        pass_copy(k).wait_send()

    each(0, units - 1, drain)
    pass_copy(units - 1).wait_send()


def lay_out_kernel(
    node_ref, bias_ref, gathered_ref, node_out, in_out, bias_out, out_out,
    in_rows, out_rows, node_sem, in_sems, out_sems,
):
    width = out_out.shape[1]
    blocks = bias_ref.shape[0]
    copies = [pltpu.make_async_copy(node_ref, node_out, node_sem.at[0])]
    copies[0].start()
    for b in range(blocks):
        rows = gathered_ref[b].astype(jnp.float32)
        in_rows[b] = rows[0:width]
        out_rows[b] = rows[width : 2 * width].T
        span = pl.ds(b * 128, 128)
        copies.append(pltpu.make_async_copy(in_rows.at[b], in_out.at[:, span], in_sems.at[b]))
        copies.append(pltpu.make_async_copy(out_rows.at[b], out_out.at[span, :], out_sems.at[b]))
        copies[-2].start()
        copies[-1].start()
        bias_out[span] = bias_ref[b, :]
    for copy in copies:
        copy.wait()


def lay_out(node_grad, bias, gathered):
    count, width = node_grad.shape
    blocks = bias.shape[0]
    dma = pltpu.SemaphoreType.DMA
    return pl.pallas_call(
        lay_out_kernel,
        out_shape=(
            jax.ShapeDtypeStruct((count, width), jnp.float32),
            jax.ShapeDtypeStruct((width, blocks * 128), jnp.float32),
            jax.ShapeDtypeStruct((blocks * 128,), jnp.float32),
            jax.ShapeDtypeStruct((blocks * 128, width), jnp.float32),
        ),
        in_specs=[IN_VMEM] * 3,
        out_specs=(ANYWHERE, ANYWHERE, IN_VMEM, ANYWHERE),
        scratch_shapes=[
            pltpu.VMEM((blocks, width, 128), jnp.float32),
            pltpu.VMEM((blocks, 128, width), jnp.float32),
            dma((1,)),
            dma((blocks,)),
            dma((blocks,)),
        ],
        compiler_params=pltpu.CompilerParams(vmem_limit_bytes=VMEM_LIMIT // 4),
    )(node_grad, bias, gathered)


def finish(merged, embedding, features, w_in, b_in, w_out, groups, doms):
    count, width = embedding.shape
    hid = w_out.shape[0]
    chips = doms // 2
    units = groups * chips
    chunks = 8
    blocks = hid // 128
    shard = hid * 2 * width // (2 * 128) // units
    far = max(chips - 1, 1)
    half = jnp.bfloat16
    dma = pltpu.SemaphoreType.DMA

    def pair(*shape):
        return [dma(shape), dma(shape)]

    node_grad, bias, gathered = pl.pallas_call(
        functools.partial(finish_kernel, groups, doms, chunks),
        out_shape=(
            jax.ShapeDtypeStruct((count, width), jnp.float32),
            jax.ShapeDtypeStruct((blocks, 128), jnp.float32),
            jax.ShapeDtypeStruct((2, units, shard, 128), half),
        ),
        in_specs=[ANYWHERE] * 4 + [IN_VMEM, ANYWHERE],
        out_specs=(ANYWHERE, IN_VMEM, IN_VMEM),
        scratch_shapes=[
            pltpu.VMEM((chips, count, width), half),
            pltpu.VMEM((count, width), jnp.float32),
            pltpu.VMEM(features.shape, half),
            pltpu.VMEM(w_in.shape, half),
            pltpu.VMEM(w_out.shape, half),
            pltpu.VMEM((count, width), jnp.float32),
            dma((chips,)),
            dma((4,)),
            dma((chunks,)),
            pltpu.VMEM((chips, count, width), half),
            pltpu.VMEM((far, count, width), half),
            pltpu.VMEM((far, count, width), half),
            pltpu.VMEM((count, width), half),
            pltpu.VMEM((blocks, 2 * width, 128), jnp.float32),
            pltpu.VMEM((blocks, 128), jnp.float32),
            pltpu.VMEM((blocks, 128), jnp.float32),
            pltpu.VMEM((units, blocks, 128), jnp.float32),
            pltpu.VMEM((blocks // 2, 2 * width, 128), half),
            pltpu.VMEM((blocks // 2, 2 * width, 128), half),
            pltpu.VMEM((units - 1, shard, 128), half),
            pltpu.VMEM((units - 1, shard, 128), half),
            pair(chips, chunks),
            pair(far, chunks),
            pair(1),
            pair(1),
            pair(units - 1),
            pair(units - 1),
            pair(units - 1),
            pair(units),
        ],
        compiler_params=pltpu.CompilerParams(
            collective_id=1, has_side_effects=True, vmem_limit_bytes=VMEM_LIMIT // 2
        ),
    )(merged, embedding, features, w_in, b_in.reshape(1, -1), w_out)
    return lay_out(node_grad, bias, gathered.reshape(blocks, 2 * width, 128))


def shards(
    features, w_in, b_in, w_out, anchor_ids, local_tiles, requests, counts, remote_refs, teacher
):
    groups = lax.axis_size("group")
    doms = lax.axis_size("dom")
    devices = groups * doms
    own_requests = requests[0, 0]
    own_counts = counts[0, 0]
    slot_count = own_requests.shape[1]
    per_step = math.gcd(local_tiles.shape[0], 4)
    table, fetched, embedding, asked, prepared = fetch_tiles(
        per_step, features, w_in, b_in, w_out, own_requests, anchor_ids, local_tiles,
        remote_refs, own_counts, teacher, groups, doms,
    )
    anchor_kl, inverse, delta, remote_grad = score(
        math.gcd(local_tiles.shape[0], 8), remote_refs, own_counts, fetched, prepared, slot_count
    )
    anchor_kl = anchor_kl.reshape(-1)
    returned = lax.all_to_all(remote_grad, "group", split_axis=0, concat_axis=0, tiled=True)
    local_grad = local_grads(
        per_step, anchor_ids, local_tiles, remote_refs, table, fetched, prepared[0], prepared[1],
        inverse, delta,
    )
    merged = merge(asked, local_grad, returned)
    node_grad, in_grad, bias_grad, out_grad = finish(
        merged, embedding, features, w_in, b_in, w_out, groups, doms
    )
    return anchor_kl, node_grad, in_grad, bias_grad, out_grad


def solution(mesh):
    return jax.shard_map(
        shards,
        mesh=mesh,
        in_specs=(
            P(("group", "dom"), None),
            P(),
            P(),
            P(),
            P(("group", "dom")),
            P(("group", "dom"), None),
            P("group", "dom", None, None),
            P("group", "dom", None),
            P(("group", "dom"), None),
            P(("group", "dom"), None),
        ),
        out_specs=(P(("group", "dom")), P(("group", "dom"), None), P(), P(), P()),
        check_vma=False,
    )
```
